32 devices in a mesh: pp: 2 (over x), ep: 16 (over z, y, core).
Axes of the slice: x: 2, y: 2, z: 4, core: 2. Of those that a mesh axis runs over, the one named last changes fastest.
Arguments:
- upstream: bfloat16 [2, 2048, 4096], P('pp', 'ep'), may hold values from -6 to 6
- saved: bfloat16 [2, 2048, 4096], P('pp', 'ep'), may hold values from -6 to 6
- routes: int32 [2, 2048, 8], P('pp', 'ep'), may hold values from 0 to 127, all different within a row
- route_weight: float32 [2, 2048, 8], P('pp', 'ep'), may hold values from 0.05 to 0.5
- w_gate: bfloat16 [2, 1024, 4096], P('pp', 'ep'), may hold values from -0.09375 to 0.09375
- w_up: bfloat16 [2, 1024, 4096], P('pp', 'ep'), may hold values from -0.09375 to 0.09375
- w_down: bfloat16 [2, 1024, 4096], P('pp', 'ep'), may hold values from -0.09375 to 0.09375
Outputs:
- grad_prev: bfloat16 [2, 2048, 4096], P('pp', 'ep')
- weight_grad: float32 [2, 2048, 8], P('pp', 'ep')
The draws below stay inside these ranges and needn't reach their ends.
Inputs may be any that keep to these rules, and one draw needn't show every extreme that they name: `routes`: each token names 8 different experts.
All inputs are finite; a program needn't handle non-finite values.
Results may differ from the reference program's by a relative error of at most 0.0011.
Values may be sent and summed in bfloat16 or wider, within the bound.
No kernel may reach another device: no remote copies, remote signals or barrier semaphores. Data moves between devices by JAX's collectives and lax.ppermute only.
A program may use at most 64 MiB of HBM per device.

```python
import math
import jax
import jax.numpy as jnp
from jax import lax

D = 4096
EXPERTS = 128
TOP = 8
HIDDEN_SIZE = 1024
SHARDS = 16
CAP = 10
TOK_DEV = 128
EXP_WIN = 1
TOKENS = 2048
N_PP = 2
N_EP = 16


def steps_of(key, dims, shards, smallest, high):
    def one(position, parts):
        draws = jax.random.uniform(jax.random.fold_in(jax.random.fold_in(key, 6), position), (parts,), jnp.float32, smallest / len(shards), high / len(shards))
        return jnp.repeat(jnp.exp(draws), dims[position] // parts).reshape((-1,) + (1,) * (len(dims) - position - 1))

    level = one(*shards[0])
    for cut in shards[1:]:
        level = level * one(*cut)
    return level


def choose_distinct(own_key, rows, amount, top, lift):
    order = jax.random.permutation(jax.random.fold_in(own_key, 1), amount)
    favour = order
    for power in range(3):
        favour = favour * favour // amount
    favour = favour * lift // amount
    chance = jax.random.randint(jax.random.fold_in(own_key, 2), (rows, amount), 0, 4096) + favour
    sure = jax.random.permutation(jax.random.fold_in(own_key, 3), rows)[jnp.arange(amount) % rows]
    chance = jnp.where(jnp.arange(rows)[:, None] == sure[None, :], 1 << 14, chance)
    merit = chance * amount + jnp.arange(amount)
    return lax.top_k(merit.astype(jnp.int32), top)[1].astype(jnp.int32)


def scatter_about(rng, shape, deviation, reach, split=(), kind=jnp.bfloat16):
    result = jax.random.normal(rng, shape, jnp.float32) * deviation
    if len(split) > 0:
        result = steps_of(rng, shape, split, -0.22, 0.18) * result
    return jnp.clip(result, min=-reach, max=reach).astype(kind)


def setup_inputs(seed: int = 0) -> dict:
    seeds = jax.random.split(jax.random.key(seed), 8)
    return {
        "upstream": scatter_about(seeds[0], (N_PP, TOKENS, D), 1.0, 6.0, ((0, 2), (1, 16))),
        "saved": scatter_about(seeds[1], (N_PP, TOKENS, D), 1.0, 6.0, ((0, 2), (1, 16))),
        "routes": choose_distinct(seeds[2], N_PP * TOKENS, EXPERTS, TOP, 512).reshape((N_PP, TOKENS, TOP)),
        "route_weight": jnp.clip(jnp.exp(math.log(0.5) - 2.3025851 * jax.random.uniform(seeds[3], (N_PP, TOKENS, TOP), jnp.float32) ** steps_of(seeds[3], (N_PP, TOKENS, TOP), ((0, 2), (1, 16)), -0.2, 0.2)), 0.05, 0.5),
        "w_gate": scatter_about(seeds[4], (N_PP, EXP_WIN * HIDDEN_SIZE, D), D ** -0.5, 0.09375, ((0, 2), (1, 16))),
        "w_up": scatter_about(seeds[5], (N_PP, EXP_WIN * HIDDEN_SIZE, D), D ** -0.5, 0.09375, ((0, 2), (1, 16))),
        "w_down": scatter_about(seeds[6], (N_PP, EXP_WIN * HIDDEN_SIZE, D), D ** -0.5, 0.09375, ((0, 2), (1, 16))),
    }


def route_match(block_routes, experts_win):
    flat_routes = block_routes.reshape(-1)
    onehot = (flat_routes[:, None] == jnp.arange(experts_win, dtype=jnp.int32)[None, :]).astype(jnp.int32)
    earlier = jnp.cumsum(onehot, axis=0) - onehot
    ranking = lax.optimization_barrier(jnp.sum(earlier * onehot, axis=1))
    kept = (flat_routes < experts_win) & (ranking < CAP)
    slot_index = flat_routes * CAP + ranking
    match = (slot_index[:, None] == jnp.arange(experts_win * CAP, dtype=jnp.int32)[None, :]) & kept[:, None]
    return match.astype(jnp.float32)

def expert_grad(grad_rows, input_rows, gate_rows, up_rows, down_rows):
    contract = (((1,), (1,)), ((), ()))
    gate = lax.dot_general(input_rows, gate_rows, contract, preferred_element_type=jnp.float32)
    up_proj = lax.dot_general(input_rows, up_rows, contract, preferred_element_type=jnp.float32)
    grad_hidden = lax.dot_general(grad_rows, down_rows, contract, preferred_element_type=jnp.float32)
    sigmoid = jax.nn.sigmoid(gate)
    swish = gate * sigmoid
    hidden = swish * up_proj
    slot_weight = lax.optimization_barrier(jnp.sum(grad_hidden * hidden, axis=1))
    grad_up = (grad_hidden * swish).astype(jnp.bfloat16)
    grad_gate = (grad_hidden * up_proj * sigmoid * (1.0 + gate * (1.0 - sigmoid))).astype(jnp.bfloat16)
    partial_value = jnp.dot(grad_gate, gate_rows, preferred_element_type=jnp.float32)
    partial_value = partial_value + jnp.dot(grad_up, up_rows, preferred_element_type=jnp.float32)
    return (partial_value, slot_weight)

def finish_block(block):
    match_block, grad_block, weight_block, grad_y, route_w = block
    slot_count = match_block.shape[1]
    weighted = lax.optimization_barrier(jnp.sum(match_block.reshape(TOK_DEV, TOP, slot_count) * route_w[:, :, None], axis=1))
    mixed = jnp.dot(weighted, grad_block, precision=lax.Precision.HIGHEST, preferred_element_type=jnp.float32)
    grad_x = (grad_y.astype(jnp.float32) + mixed).astype(jnp.bfloat16)
    weights = jnp.dot(match_block, weight_block, precision=lax.Precision.HIGHEST, preferred_element_type=jnp.float32)
    return (grad_x, weights.reshape(TOK_DEV, TOP))

def reference(upstream, saved, routes, route_weight, w_gate, w_up, w_down):
    experts_win = N_EP // SHARDS
    slot_count = experts_win * CAP
    grad_all = jnp.roll(upstream, -1, axis=0)
    grad_list = []
    weight_list = []
    for section in range(N_PP):
        grad_y = grad_all[section].reshape(N_EP, TOK_DEV, D)
        inputs = saved[section].reshape(N_EP, TOK_DEV, D)
        match = jax.vmap(lambda block_routes: route_match(block_routes, experts_win))(routes[section].reshape(N_EP, TOK_DEV, TOP))
        tok_match = match.reshape(N_EP, TOK_DEV, TOP, slot_count).sum(axis=2)
        grad_slots = jnp.einsum('rts,rtd->rsd', tok_match, grad_y.astype(jnp.float32)).astype(jnp.bfloat16)
        input_slots = jnp.einsum('rts,rtd->rsd', tok_match, inputs.astype(jnp.float32)).astype(jnp.bfloat16)
        grad_slots = grad_slots.reshape(N_EP, experts_win, CAP, D).transpose(1, 0, 2, 3).reshape(experts_win, N_EP * CAP, D)
        input_slots = input_slots.reshape(N_EP, experts_win, CAP, D).transpose(1, 0, 2, 3).reshape(experts_win, N_EP * CAP, D)
        gate_all = w_gate[section].reshape(experts_win, HIDDEN_SIZE, D)
        up_all = w_up[section].reshape(experts_win, HIDDEN_SIZE, D)
        down_all = w_down[section].reshape(experts_win, HIDDEN_SIZE, D)
        partial_value, slot_weight = lax.map(lambda group: expert_grad(*group), (grad_slots, input_slots, gate_all, up_all, down_all))
        partial_value = partial_value.reshape(experts_win, N_EP, CAP, D).transpose(1, 0, 2, 3).reshape(N_EP, slot_count, D)
        slot_weight = slot_weight.reshape(experts_win, N_EP, CAP).transpose(1, 0, 2).reshape(N_EP, slot_count)
        grad_x, weights = lax.map(finish_block, (match, partial_value, slot_weight, grad_y, route_weight[section].reshape(N_EP, TOK_DEV, TOP)))
        grad_list.append(grad_x.reshape(TOKENS, D))
        weight_list.append(weights.reshape(TOKENS, TOP))
    grad_prev = jnp.roll(jnp.stack(grad_list), -1, axis=0)
    return (grad_prev, jnp.stack(weight_list))
```

```python
import functools

import jax
import jax.numpy as jnp
from jax import lax
from jax.experimental import pallas as pl
from jax.experimental.pallas import tpu as pltpu
from jax.sharding import PartitionSpec as P

TOP = 8
SHARDS = 16
CAP = 10
MAIN = 8
TAIL = CAP - MAIN
FOLDS = MAIN // TAIL
F32 = jnp.float32
BF16 = jnp.bfloat16


def from_partner(block, axis, apart):
    count = lax.axis_size(axis)
    route = []
    for low in range(count):
        high = low | 1 << apart
        if high != low and high < count:
            route += [(low, high), (high, low)]
    return lax.ppermute(block, axis, route)


def passed_along(value, axis, by):
    size = lax.axis_size(axis)
    return lax.ppermute(value, axis, [(i, (i + by) % size) for i in range(size)])


def route_match(block_routes, experts_win):
    flat_routes = block_routes.reshape(-1)
    onehot = (flat_routes[:, None] == jnp.arange(experts_win, dtype=jnp.int32)[None, :]).astype(
        jnp.int32
    )
    earlier = jnp.cumsum(onehot, axis=0) - onehot
    ranking = jnp.sum(earlier * onehot, axis=1)
    kept = (flat_routes < experts_win) & (ranking < CAP)
    slot_index = flat_routes * CAP + ranking
    match = (slot_index[:, None] == jnp.arange(experts_win * CAP, dtype=jnp.int32)[None, :]) & kept[
        :, None
    ]
    return match.astype(jnp.float32)


def expert_grad(grad_rows, input_rows, gate_rows, up_rows, down_rows):
    contract = (((1,), (1,)), ((), ()))
    gate = lax.dot_general(input_rows, gate_rows, contract, preferred_element_type=jnp.float32)
    up_proj = lax.dot_general(input_rows, up_rows, contract, preferred_element_type=jnp.float32)
    grad_hidden = lax.dot_general(
        grad_rows, down_rows, contract, preferred_element_type=jnp.float32
    )
    sigmoid = jax.nn.sigmoid(gate)
    swish = gate * sigmoid
    hidden = swish * up_proj
    slot_weight = jnp.sum(grad_hidden * hidden, axis=1)
    grad_up = (grad_hidden * swish).astype(jnp.bfloat16)
    grad_gate = (grad_hidden * up_proj * sigmoid * (1.0 + gate * (1.0 - sigmoid))).astype(
        jnp.bfloat16
    )
    partial_value = jnp.dot(grad_gate, gate_rows, preferred_element_type=jnp.float32)
    partial_value = partial_value + jnp.dot(grad_up, up_rows, preferred_element_type=jnp.float32)
    return (partial_value, slot_weight)


def pair_rows(mine, other, pair_low):
    return jnp.where(
        pair_low, jnp.concatenate([mine, other], axis=0), jnp.concatenate([other, mine], axis=0)
    )


def general_device(upstream, saved, routes, route_weight, w_gate, w_up, w_down):
    shards = SHARDS
    groups = shards // 2
    experts_win = lax.axis_size("ep") // shards
    dev_count = experts_win * shards
    my_index = lax.axis_index("ep")
    half_cap = CAP // 2
    pair_low = my_index % 2 == 0
    other_gate, other_up, other_down = from_partner((w_gate[0], w_up[0], w_down[0]), "ep", 0)
    gate_rows = pair_rows(w_gate[0], other_gate, pair_low)
    up_rows = pair_rows(w_up[0], other_up, pair_low)
    down_rows = pair_rows(w_down[0], other_down, pair_low)
    grad_in = passed_along(upstream, "pp", -1)[0]
    inputs = saved[0]
    token_count, width = inputs.shape
    slot_total = experts_win * CAP
    match = route_match(routes[0], experts_win)
    match_three = match.reshape(token_count, TOP, slot_total)
    tok_match = match_three.sum(axis=1).astype(jnp.bfloat16)
    grad_slots = jnp.einsum(
        "ts,td->sd", tok_match, grad_in, preferred_element_type=jnp.float32
    ).astype(jnp.bfloat16)
    input_slots = jnp.einsum(
        "ts,td->sd", tok_match, inputs, preferred_element_type=jnp.float32
    ).astype(jnp.bfloat16)
    grad_halves = grad_slots.reshape(experts_win, 2, half_cap, width)
    input_halves = input_slots.reshape(experts_win, 2, half_cap, width)

    def copies_of(halves):
        return jnp.broadcast_to(halves[:, None], (experts_win, groups, 2, half_cap, width)).reshape(
            dev_count, half_cap, width
        )

    recv_grad, recv_input = (
        lax.all_to_all(copies_of(grad_halves), "ep", split_axis=0, concat_axis=0, tiled=True),
        lax.all_to_all(copies_of(input_halves), "ep", split_axis=0, concat_axis=0, tiled=True),
    )
    grad_rows = recv_grad.reshape(dev_count * half_cap, width)
    input_rows = recv_input.reshape(dev_count * half_cap, width)
    partial_value, slot_weight = expert_grad(grad_rows, input_rows, gate_rows, up_rows, down_rows)
    back_part, back_weight = (
        lax.all_to_all(
            partial_value.reshape(dev_count, half_cap, width),
            "ep",
            split_axis=0,
            concat_axis=0,
            tiled=True,
        ),
        lax.all_to_all(
            slot_weight.reshape(dev_count, half_cap), "ep", split_axis=0, concat_axis=0, tiled=True
        ),
    )
    slot_grads = (
        back_part.reshape(experts_win, groups, 2, half_cap, width)
        .sum(axis=1)
        .reshape(slot_total, width)
    )
    slot_weights = (
        back_weight.reshape(experts_win, groups, 2, half_cap).sum(axis=1).reshape(slot_total)
    )
    weighted = jnp.sum(match_three * route_weight[0][:, :, None], axis=1)
    mixed = jnp.dot(
        weighted, slot_grads, precision=lax.Precision.HIGHEST, preferred_element_type=jnp.float32
    )
    grad_out = (grad_in.astype(jnp.float32) + mixed).astype(jnp.bfloat16)
    weight_out = jnp.dot(
        match, slot_weights, precision=lax.Precision.HIGHEST, preferred_element_type=jnp.float32
    )
    weight_out = weight_out.reshape(token_count, TOP)
    sent_back = passed_along(grad_out[None], "pp", -1)
    return (sent_back, weight_out[None])


def slot_of_token(routes_t):
    count = routes_t.shape[1]
    hit = routes_t == 0
    found = jnp.max(hit.astype(F32), axis=0, keepdims=True)
    found = jnp.broadcast_to(found, (MAIN, count))
    before = lax.broadcasted_iota(jnp.int32, (count, count), 0) < lax.broadcasted_iota(
        jnp.int32, (count, count), 1
    )
    rank = jnp.dot(
        found.astype(BF16), before.astype(F32).astype(BF16), preferred_element_type=F32
    )
    slot = jnp.where((found > 0.5) & (rank < CAP - 0.5), rank, -1.0)
    return hit, slot


def main_pick(slot):
    row = lax.broadcasted_iota(jnp.int32, slot.shape, 0).astype(F32)
    return slot == row


def tail_pick(slot, fold):
    row = lax.broadcasted_iota(jnp.int32, slot.shape, 0)
    want = (row + (MAIN - TAIL * fold)).astype(F32)
    inside = (row >= TAIL * fold) & (row < TAIL * fold + TAIL)
    return (slot == want) & inside


def as_bf16(mask):
    return mask.astype(F32).astype(BF16)


def pick_kernel(routes_ref, rows_ref, out_ref):
    width = rows_ref.shape[1]
    part = width // FOLDS
    _, slot = slot_of_token(routes_ref[...])
    main = as_bf16(main_pick(slot))
    out_ref[:, :width] = jnp.dot(main, rows_ref[...], preferred_element_type=F32).astype(BF16)
    tail = jnp.zeros((MAIN, part), F32)
    for fold in range(FOLDS):
        tail = tail + jnp.dot(
            as_bf16(tail_pick(slot, fold)),
            rows_ref[:, fold * part : (fold + 1) * part],
            preferred_element_type=F32,
        )
    out_ref[:, width:] = tail.astype(BF16)


def pick_rows(routes_t, rows, name):
    width = rows.shape[1]
    return pl.pallas_call(
        pick_kernel,
        out_shape=jax.ShapeDtypeStruct((MAIN, width + width // FOLDS), BF16),
        name=name,
    )(routes_t, rows)


def unfold(blocks, width, rows_ref):
    part = width // FOLDS
    count = len(blocks)
    for k, block in enumerate(blocks):
        rows_ref[MAIN * k : MAIN * (k + 1), :] = block[:, :width]
    tails = jnp.concatenate([block[:, width:] for block in blocks], axis=0)
    row = lax.broadcasted_iota(jnp.int32, (TAIL * count, MAIN * count), 0)
    col = lax.broadcasted_iota(jnp.int32, (TAIL * count, MAIN * count), 1)
    for fold in range(FOLDS):
        place = as_bf16(col == (row // TAIL) * MAIN + TAIL * fold + row % TAIL)
        rows_ref[MAIN * count :, fold * part : (fold + 1) * part] = jnp.dot(
            place, tails, preferred_element_type=F32
        ).astype(BF16)


def read_blocks(refs):
    blocks = []
    for ref in refs:
        if len(ref.shape) == 2:
            blocks.append(ref)
        else:
            blocks += [ref.at[k] for k in range(ref.shape[0])]
    return blocks


NT = (((1,), (1,)), ((), ()))


def forward_kernel(*refs):
    *x_refs, gu_ref, h_ref, rows_ref = refs
    unfold(read_blocks(x_refs), gu_ref.shape[1], rows_ref)
    h_ref[...] = lax.dot_general(rows_ref[...], gu_ref[...], NT, preferred_element_type=F32)


def three_parts(value):
    high = value.astype(BF16)
    rest = value - high.astype(F32)
    mid = rest.astype(BF16)
    low = (rest - mid.astype(F32)).astype(BF16)
    return high, mid, low


def backward_kernel(*refs):
    *g_refs, down_ref, gu_ref, h_ref, near_ref, far_ref, rows_ref = refs
    width = gu_ref.shape[1]
    part = width // FOLDS
    units = down_ref.shape[0]
    slots = rows_ref.shape[0]
    count = slots // CAP
    unfold(read_blocks(g_refs), width, rows_ref)
    grad_hidden = lax.dot_general(rows_ref[...], down_ref[...], NT, preferred_element_type=F32)
    gate = h_ref[:, :units]
    up = h_ref[:, units:]
    sigmoid = 1.0 / (1.0 + jnp.exp(-gate))
    swish = gate * sigmoid
    weight = jnp.sum(grad_hidden * (swish * up), axis=1, keepdims=True)
    grad_up = (grad_hidden * swish).astype(BF16)
    grad_gate = (grad_hidden * up * sigmoid * (1.0 + gate * (1.0 - sigmoid))).astype(BF16)
    both = jnp.concatenate([grad_gate, grad_up], axis=1)
    half = count // 2
    outs = [(near_ref, k) for k in range(half)] + [(far_ref, k) for k in range(half)]
    back = lax.broadcasted_iota(jnp.int32, (MAIN * count, TAIL * count), 0)
    col = lax.broadcasted_iota(jnp.int32, (MAIN * count, TAIL * count), 1)
    tails = jnp.zeros((MAIN * count, part), F32)
    for fold in range(FOLDS):
        span = slice(fold * part, (fold + 1) * part)
        value = jnp.dot(both, gu_ref[:, span], preferred_element_type=F32).astype(BF16)
        for k, (ref, j) in enumerate(outs):
            ref[j, :, span] = value[MAIN * k : MAIN * (k + 1), :]
        place = as_bf16(back == (col // TAIL) * MAIN + TAIL * fold + col % TAIL)
        tails = tails + jnp.dot(place, value[MAIN * count :, :], preferred_element_type=F32)
    lane = lax.broadcasted_iota(jnp.int32, (slots, 128), 1)
    high, mid, low = (p.astype(F32) for p in three_parts(weight))
    spread = jnp.where(lane == 0, high, jnp.where(lane == 1, mid, jnp.where(lane == 2, low, 0.0)))
    shifted = jnp.where(lane == 3, high, jnp.where(lane == 4, mid, jnp.where(lane == 5, low, 0.0)))
    place = as_bf16(back == (col // TAIL) * MAIN + col % TAIL)
    tile = spread[: MAIN * count, :] + jnp.dot(
        place, shifted[MAIN * count :, :].astype(BF16), preferred_element_type=F32
    )
    tails = tails.astype(BF16)
    tile = tile.astype(BF16)
    full = width + part
    for k, (ref, j) in enumerate(outs):
        rows = slice(MAIN * k, MAIN * (k + 1))
        ref[j, :, width:full] = tails[rows, :]
        ref[j, :, full:] = tile[rows, :]


def fold_kernel(near_ref, other_ref, *out_refs):
    full = near_ref.shape[2] - 128
    for k, ref in enumerate(out_refs):
        ref[:, :full] = (
            near_ref[k, :, :full].astype(F32) + other_ref[k, :, :full].astype(F32)
        ).astype(BF16)
        ref[:, full : full + 128] = near_ref[k, :, full:]
        ref[:, full + 128 :] = other_ref[k, :, full:]


def slot_scale(slot, weight_row):
    main = jnp.sum(jnp.where(main_pick(slot), weight_row, 0.0), axis=1, keepdims=True)
    tail = jnp.zeros_like(main)
    for fold in range(FOLDS):
        tail = tail + jnp.sum(
            jnp.where(tail_pick(slot, fold), weight_row, 0.0), axis=1, keepdims=True
        )
    return main, tail


def gather_kernel(routes_ref, weight_ref, *refs):
    *in_refs, out_ref = refs
    full = out_ref.shape[1]
    width = full * FOLDS // (FOLDS + 1)
    hit, slot = slot_of_token(routes_ref[...])
    weight_row = jnp.sum(jnp.where(hit, weight_ref[...], 0.0), axis=0, keepdims=True)
    main, tail = slot_scale(slot, weight_row)
    total = in_refs[0][:, :full].astype(F32)
    for ref in in_refs[1:]:
        total = total + ref[:, :full].astype(F32)
    out_ref[:, :width] = (total[:, :width] * main).astype(BF16)
    out_ref[:, width:] = (total[:, width:] * tail).astype(BF16)


def weight_kernel(routes_ref, *refs):
    *in_refs, out_ref = refs
    hit, slot = slot_of_token(routes_ref[...])
    tile = jnp.zeros((MAIN, 128), F32)
    for ref in in_refs:
        full = ref.shape[1] - 256
        tile = tile + ref[:, full : full + 128].astype(F32) + ref[:, full + 128 :].astype(F32)
    lane = lax.broadcasted_iota(jnp.int32, tile.shape, 1)
    main = jnp.sum(jnp.where(lane < 3, tile, 0.0), axis=1, keepdims=True)
    tail = jnp.sum(jnp.where((lane >= 3) & (lane < 6), tile, 0.0), axis=1, keepdims=True)
    row = lax.broadcasted_iota(jnp.int32, slot.shape, 0).astype(F32)
    value = jnp.sum(
        jnp.where(slot == row, main, 0.0) + jnp.where((slot == row + MAIN) & (row < TAIL), tail, 0.0),
        axis=0,
        keepdims=True,
    )
    out_ref[...] = jnp.where(hit, value, 0.0)


TN = (((0,), (0,)), ((), ()))


def final_kernel(routes_ref, rows_ref, tail_ref, base_ref, out_ref):
    fold = pl.program_id(0)
    _, slot = slot_of_token(routes_ref[...])
    main = main_pick(slot)
    row = lax.broadcasted_iota(jnp.int32, slot.shape, 0)
    want = (row + (MAIN - TAIL * fold)).astype(F32)
    inside = (row >= TAIL * fold) & (row < TAIL * fold + TAIL)
    tail = (slot == want) & inside
    pick = jnp.concatenate([main.astype(F32), tail.astype(F32)], axis=0).astype(BF16)
    rows = jnp.concatenate([rows_ref[...], tail_ref[...]], axis=0)
    mixed = lax.dot_general(pick, rows, TN, preferred_element_type=F32)
    out_ref[...] = (base_ref[...].astype(F32) + mixed).astype(BF16)


def final_rows(routes_t, slot_rows, base):
    count, width = base.shape
    part = width // FOLDS
    return pl.pallas_call(
        final_kernel,
        out_shape=jax.ShapeDtypeStruct((count, width), BF16),
        grid=(FOLDS,),
        in_specs=[
            pl.BlockSpec(routes_t.shape, lambda q: (0, 0)),
            pl.BlockSpec((MAIN, part), lambda q: (0, q)),
            pl.BlockSpec((MAIN, part), lambda q: (0, FOLDS)),
            pl.BlockSpec((count, part), lambda q: (0, q)),
        ],
        out_specs=pl.BlockSpec((count, part), lambda q: (0, q)),
        name="final_rows",
    )(routes_t, slot_rows, slot_rows, base)


def across(value, bits):
    count = lax.axis_size("ep")
    return lax.ppermute(value, "ep", [(i, i ^ bits) for i in range(count)])


def gather_blocks(block):
    z_blocks = [across(block, 4 * k) for k in (2, 3, 1)]
    y_block = across(block, 2)
    stacked = jnp.stack(z_blocks)
    return [block, *z_blocks, y_block, across(stacked, 2)]


def single_device(upstream, saved, routes, route_weight, w_gate, w_up, w_down):
    routes_t = routes[0].T
    weight_t = route_weight[0].T
    next_routes = passed_along(routes_t, "pp", 1)
    width = saved.shape[2]
    full = width + width // FOLDS
    units = 2 * w_gate.shape[1]
    slots = SHARDS // 2 * CAP

    input_block = pick_rows(routes_t, saved[0], "pick_inputs")
    input_blocks = gather_blocks(input_block)
    own = (w_gate[0], w_up[0], w_down[0])
    other = from_partner(own, "ep", 0)
    gate_up = jnp.concatenate([own[0], other[0], own[1], other[1]], axis=0)
    down = jnp.concatenate([own[2], other[2]], axis=0)

    grad_block = pick_rows(next_routes, upstream[0], "pick_grads")
    grad_block = passed_along(grad_block, "pp", -1)
    grad_blocks = gather_blocks(grad_block)

    hidden = pl.pallas_call(
        forward_kernel,
        out_shape=jax.ShapeDtypeStruct((slots, 2 * units), F32),
        scratch_shapes=[pltpu.VMEM((slots, width), BF16)],
        name="expert_forward",
    )(*input_blocks, gate_up)
    quarter = SHARDS // 4
    near, far = pl.pallas_call(
        backward_kernel,
        out_shape=[jax.ShapeDtypeStruct((quarter, MAIN, full + 128), BF16)] * 2,
        scratch_shapes=[pltpu.VMEM((slots, width), BF16)],
        name="expert_backward",
    )(*grad_blocks, down, gate_up, hidden)
    other_part = across(far, 2)
    sums = pl.pallas_call(
        fold_kernel,
        out_shape=[jax.ShapeDtypeStruct((MAIN, full + 256), BF16)] * quarter,
        name="fold_y",
    )(near, other_part)
    arrived = [sums[0]] + [across(sums[i], 4 * k) for i, k in ((1, 2), (2, 3), (3, 1))]
    slot_rows = pl.pallas_call(
        gather_kernel,
        out_shape=jax.ShapeDtypeStruct((MAIN, full), BF16),
        name="sum_z",
    )(routes_t, weight_t, *arrived)
    weight_out = pl.pallas_call(
        weight_kernel,
        out_shape=jax.ShapeDtypeStruct((TOP, routes_t.shape[1]), F32),
        name="weight_out",
    )(routes_t, *arrived)
    slot_rows = passed_along(slot_rows, "pp", -1)
    grad_prev = final_rows(next_routes, slot_rows, upstream[0])
    return (grad_prev[None], weight_out.T[None])


def solution(mesh):
    single = mesh.shape["ep"] == SHARDS and mesh.shape["pp"] == 2
    spec = P("pp", "ep", None)
    return jax.shard_map(
        single_device if single else general_device,
        mesh=mesh,
        in_specs=(spec,) * 7,
        out_specs=(spec, spec),
        check_vma=False,
    )
```

```python
import functools

import jax
import jax.numpy as jnp
from jax import lax
from jax.experimental import pallas as pl
from jax.experimental.pallas import tpu as pltpu
from jax.sharding import PartitionSpec as P

TOP = 8
SHARDS = 16
CAP = 10
MAIN = 8
TAIL = CAP - MAIN
FOLDS = MAIN // TAIL
F32 = jnp.float32
BF16 = jnp.bfloat16


def from_partner(block, axis, apart):
    count = lax.axis_size(axis)
    route = []
    for low in range(count):
        high = low | 1 << apart
        if high != low and high < count:
            route += [(low, high), (high, low)]
    return lax.ppermute(block, axis, route)


def passed_along(value, axis, by):
    size = lax.axis_size(axis)
    return lax.ppermute(value, axis, [(i, (i + by) % size) for i in range(size)])


def route_match(block_routes, experts_win):
    flat_routes = block_routes.reshape(-1)
    onehot = (flat_routes[:, None] == jnp.arange(experts_win, dtype=jnp.int32)[None, :]).astype(
        jnp.int32
    )
    earlier = jnp.cumsum(onehot, axis=0) - onehot
    ranking = jnp.sum(earlier * onehot, axis=1)
    kept = (flat_routes < experts_win) & (ranking < CAP)
    slot_index = flat_routes * CAP + ranking
    match = (slot_index[:, None] == jnp.arange(experts_win * CAP, dtype=jnp.int32)[None, :]) & kept[
        :, None
    ]
    return match.astype(jnp.float32)


def expert_grad(grad_rows, input_rows, gate_rows, up_rows, down_rows):
    contract = (((1,), (1,)), ((), ()))
    gate = lax.dot_general(input_rows, gate_rows, contract, preferred_element_type=jnp.float32)
    up_proj = lax.dot_general(input_rows, up_rows, contract, preferred_element_type=jnp.float32)
    grad_hidden = lax.dot_general(
        grad_rows, down_rows, contract, preferred_element_type=jnp.float32
    )
    sigmoid = jax.nn.sigmoid(gate)
    swish = gate * sigmoid
    hidden = swish * up_proj
    slot_weight = jnp.sum(grad_hidden * hidden, axis=1)
    grad_up = (grad_hidden * swish).astype(jnp.bfloat16)
    grad_gate = (grad_hidden * up_proj * sigmoid * (1.0 + gate * (1.0 - sigmoid))).astype(
        jnp.bfloat16
    )
    partial_value = jnp.dot(grad_gate, gate_rows, preferred_element_type=jnp.float32)
    partial_value = partial_value + jnp.dot(grad_up, up_rows, preferred_element_type=jnp.float32)
    return (partial_value, slot_weight)


def pair_rows(mine, other, pair_low):
    return jnp.where(
        pair_low, jnp.concatenate([mine, other], axis=0), jnp.concatenate([other, mine], axis=0)
    )


def general_device(upstream, saved, routes, route_weight, w_gate, w_up, w_down):
    shards = SHARDS
    groups = shards // 2
    experts_win = lax.axis_size("ep") // shards
    dev_count = experts_win * shards
    my_index = lax.axis_index("ep")
    half_cap = CAP // 2
    pair_low = my_index % 2 == 0
    other_gate, other_up, other_down = from_partner((w_gate[0], w_up[0], w_down[0]), "ep", 0)
    gate_rows = pair_rows(w_gate[0], other_gate, pair_low)
    up_rows = pair_rows(w_up[0], other_up, pair_low)
    down_rows = pair_rows(w_down[0], other_down, pair_low)
    grad_in = passed_along(upstream, "pp", -1)[0]
    inputs = saved[0]
    token_count, width = inputs.shape
    slot_total = experts_win * CAP
    match = route_match(routes[0], experts_win)
    match_three = match.reshape(token_count, TOP, slot_total)
    tok_match = match_three.sum(axis=1).astype(jnp.bfloat16)
    grad_slots = jnp.einsum(
        "ts,td->sd", tok_match, grad_in, preferred_element_type=jnp.float32
    ).astype(jnp.bfloat16)
    input_slots = jnp.einsum(
        "ts,td->sd", tok_match, inputs, preferred_element_type=jnp.float32
    ).astype(jnp.bfloat16)
    grad_halves = grad_slots.reshape(experts_win, 2, half_cap, width)
    input_halves = input_slots.reshape(experts_win, 2, half_cap, width)

    def copies_of(halves):
        return jnp.broadcast_to(halves[:, None], (experts_win, groups, 2, half_cap, width)).reshape(
            dev_count, half_cap, width
        )

    recv_grad, recv_input = (
        lax.all_to_all(copies_of(grad_halves), "ep", split_axis=0, concat_axis=0, tiled=True),
        lax.all_to_all(copies_of(input_halves), "ep", split_axis=0, concat_axis=0, tiled=True),
    )
    grad_rows = recv_grad.reshape(dev_count * half_cap, width)
    input_rows = recv_input.reshape(dev_count * half_cap, width)
    partial_value, slot_weight = expert_grad(grad_rows, input_rows, gate_rows, up_rows, down_rows)
    back_part, back_weight = (
        lax.all_to_all(
            partial_value.reshape(dev_count, half_cap, width),
            "ep",
            split_axis=0,
            concat_axis=0,
            tiled=True,
        ),
        lax.all_to_all(
            slot_weight.reshape(dev_count, half_cap), "ep", split_axis=0, concat_axis=0, tiled=True
        ),
    )
    slot_grads = (
        back_part.reshape(experts_win, groups, 2, half_cap, width)
        .sum(axis=1)
        .reshape(slot_total, width)
    )
    slot_weights = (
        back_weight.reshape(experts_win, groups, 2, half_cap).sum(axis=1).reshape(slot_total)
    )
    weighted = jnp.sum(match_three * route_weight[0][:, :, None], axis=1)
    mixed = jnp.dot(
        weighted, slot_grads, precision=lax.Precision.HIGHEST, preferred_element_type=jnp.float32
    )
    grad_out = (grad_in.astype(jnp.float32) + mixed).astype(jnp.bfloat16)
    weight_out = jnp.dot(
        match, slot_weights, precision=lax.Precision.HIGHEST, preferred_element_type=jnp.float32
    )
    weight_out = weight_out.reshape(token_count, TOP)
    sent_back = passed_along(grad_out[None], "pp", -1)
    return (sent_back, weight_out[None])


def near_call(kernel, out_shape, *args, **kwargs):
    args = [pltpu.with_memory_space_constraint(arg, pltpu.VMEM) for arg in args]
    params = pltpu.CompilerParams(vmem_limit_bytes=16 * 1024 * 1024)
    return pl.pallas_call(kernel, out_shape=out_shape, compiler_params=params, **kwargs)(*args)


def slot_of_token(routes_t):
    count = routes_t.shape[1]
    hit = routes_t == 0
    found = jnp.max(hit.astype(F32), axis=0, keepdims=True)
    found = jnp.broadcast_to(found, (MAIN, count))
    before = lax.broadcasted_iota(jnp.int32, (count, count), 0) < lax.broadcasted_iota(
        jnp.int32, (count, count), 1
    )
    rank = jnp.dot(
        found.astype(BF16), before.astype(F32).astype(BF16), preferred_element_type=F32
    )
    slot = jnp.where((found > 0.5) & (rank < CAP - 0.5), rank, -1.0)
    return hit, slot


def main_pick(slot):
    row = lax.broadcasted_iota(jnp.int32, slot.shape, 0).astype(F32)
    return slot == row


def tail_pick(slot, fold):
    row = lax.broadcasted_iota(jnp.int32, slot.shape, 0)
    want = (row + (MAIN - TAIL * fold)).astype(F32)
    inside = (row >= TAIL * fold) & (row < TAIL * fold + TAIL)
    return (slot == want) & inside


def both_picks(slot, fold):
    picks = [main_pick(slot).astype(F32), tail_pick(slot, fold).astype(F32)]
    return jnp.concatenate(picks, axis=0).astype(BF16)


def as_bf16(mask):
    return mask.astype(F32).astype(BF16)


def pick_into(slot, rows_ref, out_ref):
    width = rows_ref.shape[1]
    part = width // FOLDS
    tail = jnp.zeros((MAIN, part), F32)
    for fold in range(FOLDS):
        span = slice(fold * part, (fold + 1) * part)
        got = jnp.dot(both_picks(slot, fold), rows_ref[:, span], preferred_element_type=F32)
        out_ref[:, span] = got[:MAIN].astype(BF16)
        tail = tail + got[MAIN:]
    out_ref[:, width:] = tail.astype(BF16)


def slot_scale(slot, weight_row):
    main = jnp.sum(jnp.where(main_pick(slot), weight_row, 0.0), axis=1, keepdims=True)
    tail = jnp.zeros_like(main)
    for fold in range(FOLDS):
        tail = tail + jnp.sum(
            jnp.where(tail_pick(slot, fold), weight_row, 0.0), axis=1, keepdims=True
        )
    return main, tail


def pick_inputs_kernel(routes_ref, weight_ref, rows_ref, out_ref, scale_ref):
    hit, slot = slot_of_token(routes_ref[...])
    pick_into(slot, rows_ref, out_ref)
    weight_row = jnp.sum(jnp.where(hit, weight_ref[...], 0.0), axis=0, keepdims=True)
    main, tail = slot_scale(slot, weight_row)
    scale_ref[:, :128] = jnp.broadcast_to(main, (MAIN, 128))
    scale_ref[:, 128:] = jnp.broadcast_to(tail, (MAIN, 128))


TN = (((0,), (0,)), ((), ()))
NT = (((1,), (1,)), ((), ()))


def pick_grads_kernel(routes_ref, rows_ref, out_ref, back_ref):
    _, slot = slot_of_token(routes_ref[...])
    pick_into(slot, rows_ref, out_ref)
    size = 2 * MAIN
    eye = as_bf16(
        lax.broadcasted_iota(jnp.int32, (size, size), 0)
        == lax.broadcasted_iota(jnp.int32, (size, size), 1)
    )
    for fold in range(FOLDS):
        back_ref[fold] = lax.dot_general(
            both_picks(slot, fold), eye, TN, preferred_element_type=F32
        ).astype(BF16)


def unfold(blocks, width, rows_ref):
    part = width // FOLDS
    count = len(blocks)
    for k, block in enumerate(blocks):
        rows_ref[MAIN * k : MAIN * (k + 1), :] = block[:, :width]
    tails = jnp.concatenate([block[:, width:] for block in blocks], axis=0)
    row = lax.broadcasted_iota(jnp.int32, (TAIL * count, MAIN * count), 0)
    col = lax.broadcasted_iota(jnp.int32, (TAIL * count, MAIN * count), 1)
    for fold in range(FOLDS):
        place = as_bf16(col == (row // TAIL) * MAIN + TAIL * fold + row % TAIL)
        rows_ref[MAIN * count :, fold * part : (fold + 1) * part] = jnp.dot(
            place, tails, preferred_element_type=F32
        ).astype(BF16)


def read_blocks(refs):
    blocks = []
    for ref in refs:
        if len(ref.shape) == 2:
            blocks.append(ref)
        else:
            blocks += [ref.at[k] for k in range(ref.shape[0])]
    return blocks


def forward_kernel(*refs):
    *x_refs, gu_ref, h_ref, rows_ref = refs
    unfold(read_blocks(x_refs), gu_ref.shape[1], rows_ref)
    h_ref[...] = lax.dot_general(rows_ref[...], gu_ref[...], NT, preferred_element_type=F32)


def three_parts(value):
    high = value.astype(BF16)
    rest = value - high.astype(F32)
    mid = rest.astype(BF16)
    low = (rest - mid.astype(F32)).astype(BF16)
    return high, mid, low


def backward_kernel(*refs):
    *g_refs, down_ref, gu_ref, h_ref, near_a, near_b, far_a, far_b, rows_ref = refs
    width = gu_ref.shape[1]
    part = width // FOLDS
    units = down_ref.shape[0]
    slots = rows_ref.shape[0]
    count = slots // CAP
    unfold(read_blocks(g_refs), width, rows_ref)
    grad_hidden = lax.dot_general(rows_ref[...], down_ref[...], NT, preferred_element_type=F32)
    gate = h_ref[:, :units]
    up = h_ref[:, units:]
    sigmoid = 1.0 / (1.0 + jnp.exp(-gate))
    swish = gate * sigmoid
    weight = jnp.sum(grad_hidden * (swish * up), axis=1, keepdims=True)
    grad_up = (grad_hidden * swish).astype(BF16)
    grad_gate = (grad_hidden * up * sigmoid * (1.0 + gate * (1.0 - sigmoid))).astype(BF16)
    both = jnp.concatenate([grad_gate, grad_up], axis=1)
    outs = [(ref, k) for ref in (near_a, near_b, far_a, far_b) for k in range(ref.shape[0])]
    back = lax.broadcasted_iota(jnp.int32, (MAIN * count, TAIL * count), 0)
    col = lax.broadcasted_iota(jnp.int32, (MAIN * count, TAIL * count), 1)
    tails = jnp.zeros((MAIN * count, part), F32)
    for fold in range(FOLDS):
        span = slice(fold * part, (fold + 1) * part)
        value = jnp.dot(both, gu_ref[:, span], preferred_element_type=F32).astype(BF16)
        for k, (ref, j) in enumerate(outs):
            ref[j, :, span] = value[MAIN * k : MAIN * (k + 1), :]
        place = as_bf16(back == (col // TAIL) * MAIN + TAIL * fold + col % TAIL)
        tails = tails + jnp.dot(place, value[MAIN * count :, :], preferred_element_type=F32)
    lane = lax.broadcasted_iota(jnp.int32, (slots, 128), 1)
    high, mid, low = (p.astype(F32) for p in three_parts(weight))
    spread = jnp.where(lane == 0, high, jnp.where(lane == 1, mid, jnp.where(lane == 2, low, 0.0)))
    shifted = jnp.where(lane == 3, high, jnp.where(lane == 4, mid, jnp.where(lane == 5, low, 0.0)))
    place = as_bf16(back == (col // TAIL) * MAIN + col % TAIL)
    tile = spread[: MAIN * count, :] + jnp.dot(
        place, shifted[MAIN * count :, :].astype(BF16), preferred_element_type=F32
    )
    tails = tails.astype(BF16)
    tile = tile.astype(BF16)
    full = width + part
    for k, (ref, j) in enumerate(outs):
        rows = slice(MAIN * k, MAIN * (k + 1))
        ref[j, :, width:full] = tails[rows, :]
        ref[j, :, full:] = tile[rows, :]


def fold_kernel(near_ref, other_ref, *out_refs):
    full = near_ref.shape[2] - 128
    for k, ref in enumerate(out_refs):
        ref[:, :full] = (
            near_ref[k, :, :full].astype(F32) + other_ref[k, :, :full].astype(F32)
        ).astype(BF16)
        ref[:, full : full + 128] = near_ref[k, :, full:]
        ref[:, full + 128 :] = other_ref[k, :, full:]


def gather_kernel(scale_ref, *refs):
    *in_refs, out_ref = refs
    full = out_ref.shape[1]
    width = full * FOLDS // (FOLDS + 1)
    total = in_refs[0][:, :full].astype(F32)
    for ref in in_refs[1:]:
        total = total + ref[:, :full].astype(F32)
    out_ref[:, :width] = (total[:, :width] * scale_ref[:, :1]).astype(BF16)
    out_ref[:, width:] = (total[:, width:] * scale_ref[:, 128:129]).astype(BF16)


def weight_kernel(routes_ref, *refs):
    *in_refs, out_ref = refs
    hit, slot = slot_of_token(routes_ref[...])
    tile = jnp.zeros((MAIN, 128), F32)
    for ref in in_refs:
        full = ref.shape[1] - 256
        tile = tile + ref[:, full : full + 128].astype(F32) + ref[:, full + 128 :].astype(F32)
    lane = lax.broadcasted_iota(jnp.int32, tile.shape, 1)
    main = jnp.sum(jnp.where(lane < 3, tile, 0.0), axis=1, keepdims=True)
    tail = jnp.sum(jnp.where((lane >= 3) & (lane < 6), tile, 0.0), axis=1, keepdims=True)
    row = lax.broadcasted_iota(jnp.int32, slot.shape, 0).astype(F32)
    value = jnp.sum(
        jnp.where(slot == row, main, 0.0) + jnp.where((slot == row + MAIN) & (row < TAIL), tail, 0.0),
        axis=0,
        keepdims=True,
    )
    out_ref[...] = jnp.where(hit, value, 0.0)


def final_kernel(back_ref, rows_ref, base_ref, out_ref, done_ref, sems):
    width = base_ref.shape[1]
    part = width // FOLDS
    copies = []
    for fold in range(FOLDS):
        span = slice(fold * part, (fold + 1) * part)
        rows = jnp.concatenate([rows_ref[:, span], rows_ref[:, width:]], axis=0)
        mixed = jnp.dot(back_ref[fold], rows, preferred_element_type=F32)
        done_ref[:, span] = (base_ref[:, span].astype(F32) + mixed).astype(BF16)
        copy = pltpu.make_async_copy(done_ref.at[:, span], out_ref.at[:, span], sems.at[fold])
        copy.start()
        copies.append(copy)
    for copy in copies:
        copy.wait()


def across(value, bits):
    count = lax.axis_size("ep")
    return lax.ppermute(value, "ep", [(i, i ^ bits) for i in range(count)])


def sections_across(value, bits):
    count = lax.axis_size("ep")
    pairs = [(s * count + i, (1 - s) * count + (i ^ bits)) for s in range(2) for i in range(count)]
    return lax.ppermute(value, ("pp", "ep"), pairs)


def single_device(upstream, saved, routes, route_weight, w_gate, w_up, w_down):
    routes_t = routes[0].T
    weight_t = route_weight[0].T
    next_routes = passed_along(routes_t, "pp", 1)
    count, width = saved.shape[1:]
    full = width + width // FOLDS
    units = 2 * w_gate.shape[1]
    slots = SHARDS // 2 * CAP

    own = (w_gate[0], w_up[0], w_down[0])
    other = from_partner(own, "ep", 0)

    input_block, scale = near_call(
        pick_inputs_kernel,
        [pltpu.VMEM((MAIN, full), BF16), pltpu.VMEM((MAIN, 256), F32)],
        routes_t,
        weight_t,
        saved[0],
        name="pick_inputs",
    )
    grad_block, back = near_call(
        pick_grads_kernel,
        [pltpu.VMEM((MAIN, full), BF16), pltpu.VMEM((FOLDS, count, 2 * MAIN), BF16)],
        next_routes,
        upstream[0],
        name="pick_grads",
    )
    input_block, grad_block, other = lax.optimization_barrier((input_block, grad_block, other))
    gate_up = jnp.concatenate([own[0], other[0], own[1], other[1]], axis=0)
    down = jnp.concatenate([own[2], other[2]], axis=0)

    z_inputs = [input_block] + [across(input_block, 4 * k) for k in (1, 2, 3)]
    z_grads = [sections_across(grad_block, 4 * k) for k in (0, 1, 2, 3)]
    y_inputs = across(jnp.stack(z_inputs), 2)
    y_grads_a = across(jnp.stack(z_grads[:2]), 2)
    y_grads_b = across(jnp.stack(z_grads[2:]), 2)

    hidden = near_call(
        forward_kernel,
        pltpu.VMEM((slots, 2 * units), F32),
        *z_inputs,
        y_inputs,
        gate_up,
        scratch_shapes=[pltpu.VMEM((slots, width), BF16)],
        name="expert_forward",
    )
    pair = pltpu.VMEM((2, MAIN, full + 128), BF16)
    near_a, near_b, far_a, far_b = near_call(
        backward_kernel,
        [pair] * 4,
        *z_grads,
        y_grads_a,
        y_grads_b,
        down,
        gate_up,
        hidden,
        scratch_shapes=[pltpu.VMEM((slots, width), BF16)],
        name="expert_backward",
    )
    sum_shape = pltpu.VMEM((MAIN, full + 256), BF16)
    far_b = across(far_b, 2)
    far_a = across(far_a, 2)
    sums_b = near_call(fold_kernel, [sum_shape] * 2, near_b, far_b, name="fold_far")
    sums_a = near_call(fold_kernel, [sum_shape] * 2, near_a, far_a, name="fold_near")
    sums = [*sums_a, *sums_b]
    arrived = [sums[0]] + [across(sums[k], 4 * k) for k in (1, 2, 3)]
    slot_rows = near_call(
        gather_kernel, pltpu.VMEM((MAIN, full), BF16), scale, *arrived, name="sum_z"
    )
    weight_out = near_call(
        weight_kernel,
        jax.ShapeDtypeStruct((TOP, count), F32),
        routes_t,
        *arrived,
        name="weight_out",
    )
    slot_rows = sections_across(slot_rows, 0)
    grad_prev = near_call(
        final_kernel,
        jax.ShapeDtypeStruct((count, width), BF16),
        back,
        slot_rows,
        upstream[0],
        out_specs=pl.BlockSpec(memory_space=pl.ANY),
        scratch_shapes=[pltpu.VMEM((count, width), BF16), pltpu.SemaphoreType.DMA((FOLDS,))],
        name="final_rows",
    )
    return (grad_prev[None], weight_out.T[None])


def solution(mesh):
    single = mesh.shape["ep"] == SHARDS and mesh.shape["pp"] == 2
    spec = P("pp", "ep", None)
    return jax.shard_map(
        single_device if single else general_device,
        mesh=mesh,
        in_specs=(spec,) * 7,
        out_specs=(spec, spec),
        check_vma=False,
    )
```

```python
import functools

import jax
import jax.numpy as jnp
from jax import lax
from jax.experimental import pallas as pl
from jax.experimental.pallas import tpu as pltpu
from jax.sharding import PartitionSpec as P

TOP = 8
SHARDS = 16
CAP = 10
MAIN = 8
TAIL = CAP - MAIN
FOLDS = MAIN // TAIL
F32 = jnp.float32
BF16 = jnp.bfloat16


def from_partner(block, axis, apart):
    count = lax.axis_size(axis)
    route = []
    for low in range(count):
        high = low | 1 << apart
        if high != low and high < count:
            route += [(low, high), (high, low)]
    return lax.ppermute(block, axis, route)


def passed_along(value, axis, by):
    size = lax.axis_size(axis)
    return lax.ppermute(value, axis, [(i, (i + by) % size) for i in range(size)])


def route_match(block_routes, experts_win):
    flat_routes = block_routes.reshape(-1)
    onehot = (flat_routes[:, None] == jnp.arange(experts_win, dtype=jnp.int32)[None, :]).astype(
        jnp.int32
    )
    earlier = jnp.cumsum(onehot, axis=0) - onehot
    ranking = jnp.sum(earlier * onehot, axis=1)
    kept = (flat_routes < experts_win) & (ranking < CAP)
    slot_index = flat_routes * CAP + ranking
    match = (slot_index[:, None] == jnp.arange(experts_win * CAP, dtype=jnp.int32)[None, :]) & kept[
        :, None
    ]
    return match.astype(jnp.float32)


def expert_grad(grad_rows, input_rows, gate_rows, up_rows, down_rows):
    contract = (((1,), (1,)), ((), ()))
    gate = lax.dot_general(input_rows, gate_rows, contract, preferred_element_type=jnp.float32)
    up_proj = lax.dot_general(input_rows, up_rows, contract, preferred_element_type=jnp.float32)
    grad_hidden = lax.dot_general(
        grad_rows, down_rows, contract, preferred_element_type=jnp.float32
    )
    sigmoid = jax.nn.sigmoid(gate)
    swish = gate * sigmoid
    hidden = swish * up_proj
    slot_weight = jnp.sum(grad_hidden * hidden, axis=1)
    grad_up = (grad_hidden * swish).astype(jnp.bfloat16)
    grad_gate = (grad_hidden * up_proj * sigmoid * (1.0 + gate * (1.0 - sigmoid))).astype(
        jnp.bfloat16
    )
    partial_value = jnp.dot(grad_gate, gate_rows, preferred_element_type=jnp.float32)
    partial_value = partial_value + jnp.dot(grad_up, up_rows, preferred_element_type=jnp.float32)
    return (partial_value, slot_weight)


def pair_rows(mine, other, pair_low):
    return jnp.where(
        pair_low, jnp.concatenate([mine, other], axis=0), jnp.concatenate([other, mine], axis=0)
    )


def general_device(upstream, saved, routes, route_weight, w_gate, w_up, w_down):
    shards = SHARDS
    groups = shards // 2
    experts_win = lax.axis_size("ep") // shards
    dev_count = experts_win * shards
    my_index = lax.axis_index("ep")
    half_cap = CAP // 2
    pair_low = my_index % 2 == 0
    other_gate, other_up, other_down = from_partner((w_gate[0], w_up[0], w_down[0]), "ep", 0)
    gate_rows = pair_rows(w_gate[0], other_gate, pair_low)
    up_rows = pair_rows(w_up[0], other_up, pair_low)
    down_rows = pair_rows(w_down[0], other_down, pair_low)
    grad_in = passed_along(upstream, "pp", -1)[0]
    inputs = saved[0]
    token_count, width = inputs.shape
    slot_total = experts_win * CAP
    match = route_match(routes[0], experts_win)
    match_three = match.reshape(token_count, TOP, slot_total)
    tok_match = match_three.sum(axis=1).astype(jnp.bfloat16)
    grad_slots = jnp.einsum(
        "ts,td->sd", tok_match, grad_in, preferred_element_type=jnp.float32
    ).astype(jnp.bfloat16)
    input_slots = jnp.einsum(
        "ts,td->sd", tok_match, inputs, preferred_element_type=jnp.float32
    ).astype(jnp.bfloat16)
    grad_halves = grad_slots.reshape(experts_win, 2, half_cap, width)
    input_halves = input_slots.reshape(experts_win, 2, half_cap, width)

    def copies_of(halves):
        return jnp.broadcast_to(halves[:, None], (experts_win, groups, 2, half_cap, width)).reshape(
            dev_count, half_cap, width
        )

    recv_grad, recv_input = (
        lax.all_to_all(copies_of(grad_halves), "ep", split_axis=0, concat_axis=0, tiled=True),
        lax.all_to_all(copies_of(input_halves), "ep", split_axis=0, concat_axis=0, tiled=True),
    )
    grad_rows = recv_grad.reshape(dev_count * half_cap, width)
    input_rows = recv_input.reshape(dev_count * half_cap, width)
    partial_value, slot_weight = expert_grad(grad_rows, input_rows, gate_rows, up_rows, down_rows)
    back_part, back_weight = (
        lax.all_to_all(
            partial_value.reshape(dev_count, half_cap, width),
            "ep",
            split_axis=0,
            concat_axis=0,
            tiled=True,
        ),
        lax.all_to_all(
            slot_weight.reshape(dev_count, half_cap), "ep", split_axis=0, concat_axis=0, tiled=True
        ),
    )
    slot_grads = (
        back_part.reshape(experts_win, groups, 2, half_cap, width)
        .sum(axis=1)
        .reshape(slot_total, width)
    )
    slot_weights = (
        back_weight.reshape(experts_win, groups, 2, half_cap).sum(axis=1).reshape(slot_total)
    )
    weighted = jnp.sum(match_three * route_weight[0][:, :, None], axis=1)
    mixed = jnp.dot(
        weighted, slot_grads, precision=lax.Precision.HIGHEST, preferred_element_type=jnp.float32
    )
    grad_out = (grad_in.astype(jnp.float32) + mixed).astype(jnp.bfloat16)
    weight_out = jnp.dot(
        match, slot_weights, precision=lax.Precision.HIGHEST, preferred_element_type=jnp.float32
    )
    weight_out = weight_out.reshape(token_count, TOP)
    sent_back = passed_along(grad_out[None], "pp", -1)
    return (sent_back, weight_out[None])


def near_call(kernel, out_shape, *args, **kwargs):
    if "in_specs" not in kwargs:
        args = [pltpu.with_memory_space_constraint(arg, pltpu.VMEM) for arg in args]
    params = pltpu.CompilerParams(vmem_limit_bytes=16 * 1024 * 1024)
    return pl.pallas_call(kernel, out_shape=out_shape, compiler_params=params, **kwargs)(*args)


def as_bf16(mask):
    return mask.astype(F32).astype(BF16)


def slot_of_token(routes_t):
    count = routes_t.shape[1]
    hit = routes_t == 0
    found = jnp.max(hit.astype(F32), axis=0, keepdims=True)
    found = jnp.broadcast_to(found, (MAIN, count))
    before = lax.broadcasted_iota(jnp.int32, (count, count), 0) < lax.broadcasted_iota(
        jnp.int32, (count, count), 1
    )
    rank = jnp.dot(found.astype(BF16), as_bf16(before), preferred_element_type=F32)
    slot = jnp.where((found > 0.5) & (rank < CAP - 0.5), rank, -1.0)
    return hit, slot


def main_pick(slot):
    row = lax.broadcasted_iota(jnp.int32, slot.shape, 0).astype(F32)
    return slot == row


def tail_pick(slot, fold):
    row = lax.broadcasted_iota(jnp.int32, slot.shape, 0)
    want = (row + (MAIN - TAIL * fold)).astype(F32)
    inside = (row >= TAIL * fold) & (row < TAIL * fold + TAIL)
    return (slot == want) & inside


def both_picks(slot, fold):
    picks = [main_pick(slot).astype(F32), tail_pick(slot, fold).astype(F32)]
    return jnp.concatenate(picks, axis=0).astype(BF16)


def pick_into(slot, rows_ref, out_ref, before=lambda fold: None):
    width = rows_ref.shape[1]
    part = width // FOLDS
    tail = jnp.zeros((MAIN, part), F32)
    for fold in range(FOLDS):
        before(fold)
        span = slice(fold * part, (fold + 1) * part)
        got = jnp.dot(both_picks(slot, fold), rows_ref[:, span], preferred_element_type=F32)
        out_ref[:, span] = got[:MAIN].astype(BF16)
        tail = tail + got[MAIN:]
    out_ref[:, width:] = tail.astype(BF16)


def pick_inputs_kernel(routes_in, rows_in, base_in, out_ref, routes_ref, base_ref, rows_ref, sems):
    part = rows_ref.shape[1] // FOLDS
    routes_copy = pltpu.make_async_copy(routes_in, routes_ref, sems.at[FOLDS])
    routes_copy.start()
    copies = []
    for fold in range(FOLDS):
        span = slice(fold * part, (fold + 1) * part)
        copies.append(
            pltpu.make_async_copy(rows_in.at[:, span], rows_ref.at[:, span], sems.at[fold])
        )
        copies[-1].start()
    base_copy = pltpu.make_async_copy(base_in, base_ref, sems.at[FOLDS + 1])
    base_copy.start()
    routes_copy.wait()
    _, slot = slot_of_token(routes_ref[...])
    pick_into(slot, rows_ref, out_ref, lambda fold: copies[fold].wait())
    base_copy.wait()


def pick_grads_kernel(routes_ref, rows_ref, out_ref):
    _, slot = slot_of_token(routes_ref[...])
    pick_into(slot, rows_ref, out_ref)


TN = (((0,), (0,)), ((), ()))
NT = (((1,), (1,)), ((), ()))


def back_kernel(routes_ref, weight_ref, back_ref, scale_ref):
    hit, slot = slot_of_token(routes_ref[...])
    size = 2 * MAIN
    eye = as_bf16(
        lax.broadcasted_iota(jnp.int32, (size, 2 * size), 0)
        == lax.broadcasted_iota(jnp.int32, (size, 2 * size), 1) % size
    )
    for fold in range(FOLDS):
        back_ref[fold] = lax.dot_general(
            both_picks(slot, fold), eye, TN, preferred_element_type=F32
        ).astype(BF16)
    weight_row = jnp.sum(jnp.where(hit, weight_ref[...], 0.0), axis=0, keepdims=True)
    main = jnp.sum(jnp.where(main_pick(slot), weight_row, 0.0), axis=1, keepdims=True)
    tail = jnp.zeros_like(main)
    for fold in range(FOLDS):
        tail = tail + jnp.sum(
            jnp.where(tail_pick(slot, fold), weight_row, 0.0), axis=1, keepdims=True
        )
    scale_ref[:, :128] = jnp.broadcast_to(main, (MAIN, 128))
    scale_ref[:, 128:] = jnp.broadcast_to(tail, (MAIN, 128))


def unfold(blocks, width, rows_ref):
    part = width // FOLDS
    count = len(blocks)
    for k, block in enumerate(blocks):
        rows_ref[MAIN * k : MAIN * (k + 1), :] = block[:, :width]
    tails = jnp.concatenate([block[:, width:] for block in blocks], axis=0)
    row = lax.broadcasted_iota(jnp.int32, (TAIL * count, MAIN * count), 0)
    col = lax.broadcasted_iota(jnp.int32, (TAIL * count, MAIN * count), 1)
    for fold in range(FOLDS):
        place = as_bf16(col == (row // TAIL) * MAIN + TAIL * fold + row % TAIL)
        rows_ref[MAIN * count :, fold * part : (fold + 1) * part] = jnp.dot(
            place, tails, preferred_element_type=F32
        ).astype(BF16)


def forward_kernel(own, z2, y0, y2, low, high, gu_ref, h_ref, rows_ref):
    blocks = [own, low.at[0], z2, high.at[0], y0, low.at[1], y2, high.at[1]]
    unfold(blocks, gu_ref.shape[1], rows_ref)
    h_ref[...] = lax.dot_general(rows_ref[...], gu_ref[...], NT, preferred_element_type=F32)


def three_parts(value):
    high = value.astype(BF16)
    rest = value - high.astype(F32)
    mid = rest.astype(BF16)
    low = (rest - mid.astype(F32)).astype(BF16)
    return high, mid, low


def backward_kernel(*refs):
    g0, g2, z_refs, y_refs, yz_refs, down_ref, gu_ref, h_ref, *outs, rows_ref = refs
    near_a, far_a, near_b, far_b = outs
    width = gu_ref.shape[1]
    half = width // 2
    part = half // FOLDS
    units = down_ref.shape[0]
    slots = rows_ref.shape[0]
    count = slots // CAP
    blocks = [g0, z_refs.at[0], g2, z_refs.at[1]]
    blocks += [y_refs.at[0], yz_refs.at[0], y_refs.at[1], yz_refs.at[1]]
    unfold(blocks, width, rows_ref)
    grad_hidden = lax.dot_general(rows_ref[...], down_ref[...], NT, preferred_element_type=F32)
    gate = h_ref[:, :units]
    up = h_ref[:, units:]
    sigmoid = 1.0 / (1.0 + jnp.exp(-gate))
    swish = gate * sigmoid
    weight = jnp.sum(grad_hidden * (swish * up), axis=1, keepdims=True)
    grad_up = (grad_hidden * swish).astype(BF16)
    grad_gate = (grad_hidden * up * sigmoid * (1.0 + gate * (1.0 - sigmoid))).astype(BF16)
    both = jnp.concatenate([grad_gate, grad_up], axis=1)
    place_a = [(near_a, 0), (near_a, 1), (near_a, 2), (near_a, 3)]
    place_a += [(far_a, 0), (far_a, 1), (far_a, 2), (far_a, 3)]
    place_b = [(near_b, 0), (far_b, 0), (near_b, 1), (far_b, 1)]
    place_b += [(near_b, 2), (far_b, 2), (near_b, 3), (far_b, 3)]
    back = lax.broadcasted_iota(jnp.int32, (MAIN * count, TAIL * count), 0)
    col = lax.broadcasted_iota(jnp.int32, (MAIN * count, TAIL * count), 1)
    for side, places in enumerate((place_a, place_b)):
        tails = jnp.zeros((MAIN * count, part), F32)
        for fold in range(FOLDS):
            start = side * half + fold * part
            value = jnp.dot(both, gu_ref[:, start : start + part], preferred_element_type=F32)
            value = value.astype(BF16)
            for k, (ref, j) in enumerate(places):
                ref[j, :, fold * part : (fold + 1) * part] = value[MAIN * k : MAIN * (k + 1), :]
            place = as_bf16(back == (col // TAIL) * MAIN + TAIL * fold + col % TAIL)
            tails = tails + jnp.dot(place, value[MAIN * count :, :], preferred_element_type=F32)
        tails = tails.astype(BF16)
        for k, (ref, j) in enumerate(places):
            ref[j, :, half : half + part] = tails[MAIN * k : MAIN * (k + 1), :]
    lane = lax.broadcasted_iota(jnp.int32, (slots, 128), 1)
    high, mid, low = (p.astype(F32) for p in three_parts(weight))
    spread = jnp.where(lane == 0, high, jnp.where(lane == 1, mid, jnp.where(lane == 2, low, 0.0)))
    shifted = jnp.where(lane == 3, high, jnp.where(lane == 4, mid, jnp.where(lane == 5, low, 0.0)))
    place = as_bf16(back == (col // TAIL) * MAIN + col % TAIL)
    tile = spread[: MAIN * count, :] + jnp.dot(
        place, shifted[MAIN * count :, :].astype(BF16), preferred_element_type=F32
    )
    tile = tile.astype(BF16)
    for k, (ref, j) in enumerate(place_a):
        ref[j, :, half + part :] = tile[MAIN * k : MAIN * (k + 1), :]


def added(one, two):
    return (one.astype(F32) + two.astype(F32)).astype(BF16)


def fold_a_kernel(near_ref, got_ref, send_ref, keep_ref):
    full = near_ref.shape[2] - 128
    for k in range(near_ref.shape[0]):
        ref = (keep_ref, send_ref)[k % 2]
        ref[k // 2, :, :full] = added(near_ref[k, :, :full], got_ref[k, :, :full])
        ref[k // 2, :, full : full + 128] = near_ref[k, :, full:]
        ref[k // 2, :, full + 128 :] = got_ref[k, :, full:]


def fold_b_kernel(near_ref, got_ref, send_ref, keep_ref):
    for k in range(near_ref.shape[0]):
        ref = (keep_ref, send_ref)[k // 2]
        ref[k % 2] = added(near_ref[k], got_ref[k])


def fold_both_kernel(keep_a, got_a, keep_b, got_b, own_ref, send_ref, own_tile, send_tile):
    full = keep_b.shape[2]
    for k, (ref, tile_ref) in enumerate(((own_ref, own_tile), (send_ref, send_tile))):
        ref[:, :full] = added(keep_a[k, :, :full], got_a[k, :, :full])
        ref[:, full:] = added(keep_b[k], got_b[k])
        tile = jnp.zeros((MAIN, 128), F32)
        for source in (keep_a, got_a):
            for start in (full, full + 128):
                tile = tile + source[k, :, start : start + 128].astype(F32)
        tile_ref[...] = tile


def weight_kernel(routes_ref, own_tile, got_tile, out_ref):
    hit, slot = slot_of_token(routes_ref[...])
    tile = own_tile[...] + got_tile[...]
    lane = lax.broadcasted_iota(jnp.int32, tile.shape, 1)
    main = jnp.sum(jnp.where(lane < 3, tile, 0.0), axis=1, keepdims=True)
    tail = jnp.sum(jnp.where((lane >= 3) & (lane < 6), tile, 0.0), axis=1, keepdims=True)
    row = lax.broadcasted_iota(jnp.int32, slot.shape, 0).astype(F32)
    value = jnp.sum(
        jnp.where(slot == row, main, 0.0) + jnp.where((slot == row + MAIN) & (row < TAIL), tail, 0.0),
        axis=0,
        keepdims=True,
    )
    out_ref[...] = jnp.where(hit, value, 0.0)


def final_kernel(back_ref, scale_ref, one_ref, two_ref, base_ref, out_ref, done_ref, sems):
    width = base_ref.shape[1]
    half = width // 2
    part = half // FOLDS
    copies = []
    for side in range(2):
        first = side * (half + part)
        for fold in range(FOLDS):
            rows = []
            for lane, start in ((0, first + fold * part), (128, first + half)):
                total = one_ref[:, start : start + part].astype(F32)
                total = total + two_ref[:, start : start + part].astype(F32)
                rows.append(total * scale_ref[:, lane : lane + 1])
            rows = jnp.concatenate(rows, axis=0)
            high = rows.astype(BF16)
            low = (rows - high.astype(F32)).astype(BF16)
            rows = jnp.concatenate([high, low], axis=0)
            mixed = jnp.dot(back_ref[fold], rows, preferred_element_type=F32)
            start = side * half + fold * part
            span = slice(start, start + part)
            done_ref[:, span] = (base_ref[:, span].astype(F32) + mixed).astype(BF16)
            if fold % 2:
                span = slice(start - part, start + part)
                copy = pltpu.make_async_copy(
                    done_ref.at[:, span], out_ref.at[:, span], sems.at[len(copies)]
                )
                copy.start()
                copies.append(copy)
    for copy in copies:
        copy.wait()


def across(value, bits):
    count = lax.axis_size("ep")
    return lax.ppermute(value, "ep", [(i, i ^ bits) for i in range(count)])


def sections_across(value, bits):
    count = lax.axis_size("ep")
    pairs = [(s * count + i, (1 - s) * count + (i ^ bits)) for s in range(2) for i in range(count)]
    return lax.ppermute(value, ("pp", "ep"), pairs)


Y1, Z1, Z2 = 2, 4, 8


def single_device(upstream, saved, routes, route_weight, w_gate, w_up, w_down):
    routes_t = routes[0].T
    weight_t = route_weight[0].T
    next_routes = passed_along(routes_t, "pp", 1)
    next_weight = passed_along(weight_t, "pp", 1)
    count, width = saved.shape[1:]
    full = width + width // FOLDS
    half = full // 2
    units = 2 * w_gate.shape[1]
    slots = SHARDS // 2 * CAP
    hbm = pl.BlockSpec(memory_space=pltpu.HBM)

    next_routes, next_weight = lax.optimization_barrier((next_routes, next_weight))
    input_block, near_routes, base = near_call(
        pick_inputs_kernel,
        [
            pltpu.VMEM((MAIN, full), BF16),
            pltpu.VMEM(routes_t.shape, jnp.int32),
            pltpu.VMEM((count, width), BF16),
        ],
        *(pltpu.with_memory_space_constraint(v, pltpu.HBM) for v in (routes_t, saved[0], upstream[0])),
        in_specs=[hbm] * 3,
        scratch_shapes=[pltpu.VMEM((count, width), BF16), pltpu.SemaphoreType.DMA((FOLDS + 2,))],
        name="pick_inputs",
    )
    grad_block = near_call(
        pick_grads_kernel, pltpu.VMEM((MAIN, full), BF16), next_routes, base, name="pick_grads"
    )
    own = (w_gate[0], w_up[0], w_down[0])
    other = from_partner(own, "ep", 0)
    input_block, grad_block, other = lax.optimization_barrier((input_block, grad_block, other))
    gate_up = jnp.concatenate([own[0], other[0], own[1], other[1]], axis=0)
    down = jnp.concatenate([own[2], other[2]], axis=0)
    back, scale = near_call(
        back_kernel,
        [pltpu.VMEM((FOLDS, count, 4 * MAIN), BF16), pltpu.VMEM((MAIN, 256), F32)],
        next_routes,
        next_weight,
        name="back_rows",
    )

    grad_z2 = sections_across(grad_block, Z2)
    grad_z0 = sections_across(grad_block, 0)
    input_z2 = across(input_block, Z2)
    input_y0 = across(input_block, Y1)
    grad_z = jnp.stack([grad_z0, grad_z2])
    grad_z1 = across(grad_z, Z1)
    grad_y = across(grad_z, Y1)
    input_y2 = across(input_z2, Y1)
    input_low = across(jnp.stack([input_block, input_y0]), Z1)
    input_high = across(jnp.stack([input_z2, input_y2]), Z1)
    grad_yz1 = across(grad_z1, Y1)
    input_high, back, scale = lax.optimization_barrier((input_high, back, scale))

    hidden = near_call(
        forward_kernel,
        pltpu.VMEM((slots, 2 * units), F32),
        input_block,
        input_z2,
        input_y0,
        input_y2,
        input_low,
        input_high,
        gate_up,
        scratch_shapes=[pltpu.VMEM((slots, width), BF16)],
        name="expert_forward",
    )
    side_a = pltpu.VMEM((4, MAIN, half + 128), BF16)
    side_b = pltpu.VMEM((4, MAIN, half), BF16)
    near_a, far_a, near_b, far_b = near_call(
        backward_kernel,
        [side_a, side_a, side_b, side_b],
        grad_z0,
        grad_z2,
        grad_z1,
        grad_y,
        grad_yz1,
        down,
        gate_up,
        hidden,
        scratch_shapes=[pltpu.VMEM((slots, width), BF16)],
        name="expert_backward",
    )
    got_a = across(far_a, Y1)
    got_b = across(far_b, Z1)
    send_a, keep_a = near_call(
        fold_a_kernel, [pltpu.VMEM((2, MAIN, half + 256), BF16)] * 2, near_a, got_a, name="fold_a"
    )
    send_b, keep_b = near_call(
        fold_b_kernel, [pltpu.VMEM((2, MAIN, half), BF16)] * 2, near_b, got_b, name="fold_b"
    )
    rows_0, rows_2, tile_0, tile_2 = near_call(
        fold_both_kernel,
        [pltpu.VMEM((MAIN, full), BF16)] * 2 + [pltpu.VMEM((MAIN, 128), F32)] * 2,
        keep_a,
        across(send_a, Z1),
        keep_b,
        across(send_b, Y1),
        name="fold_both",
    )
    got_2 = sections_across(rows_2, Z2)
    got_0 = sections_across(rows_0, 0)
    weight_out = near_call(
        weight_kernel,
        jax.ShapeDtypeStruct((TOP, count), F32),
        near_routes,
        tile_0,
        across(tile_2, Z2),
        name="weight_out",
    )
    grad_prev = near_call(
        final_kernel,
        jax.ShapeDtypeStruct((count, width), BF16),
        back,
        scale,
        got_0,
        got_2,
        base,
        out_specs=hbm,
        scratch_shapes=[pltpu.VMEM((count, width), BF16), pltpu.SemaphoreType.DMA((FOLDS,))],
        name="final_rows",
    )
    return (grad_prev[None], weight_out.T[None])


def solution(mesh):
    single = mesh.shape["ep"] == SHARDS and mesh.shape["pp"] == 2
    spec = P("pp", "ep", None)
    return jax.shard_map(
        single_device if single else general_device,
        mesh=mesh,
        in_specs=(spec,) * 7,
        out_specs=(spec, spec),
        check_vma=False,
    )
```

```python
import functools

import jax
import jax.numpy as jnp
from jax import lax
from jax.experimental import pallas as pl
from jax.experimental.pallas import tpu as pltpu
from jax.sharding import PartitionSpec as P

TOP = 8
SHARDS = 16
CAP = 10
MAIN = 8
TAIL = CAP - MAIN
FOLDS = MAIN // TAIL
F32 = jnp.float32
BF16 = jnp.bfloat16


def from_partner(block, axis, apart):
    count = lax.axis_size(axis)
    route = []
    for low in range(count):
        high = low | 1 << apart
        if high != low and high < count:
            route += [(low, high), (high, low)]
    return lax.ppermute(block, axis, route)


def passed_along(value, axis, by):
    size = lax.axis_size(axis)
    return lax.ppermute(value, axis, [(i, (i + by) % size) for i in range(size)])


def route_match(block_routes, experts_win):
    flat_routes = block_routes.reshape(-1)
    onehot = (flat_routes[:, None] == jnp.arange(experts_win, dtype=jnp.int32)[None, :]).astype(
        jnp.int32
    )
    earlier = jnp.cumsum(onehot, axis=0) - onehot
    ranking = jnp.sum(earlier * onehot, axis=1)
    kept = (flat_routes < experts_win) & (ranking < CAP)
    slot_index = flat_routes * CAP + ranking
    match = (slot_index[:, None] == jnp.arange(experts_win * CAP, dtype=jnp.int32)[None, :]) & kept[
        :, None
    ]
    return match.astype(jnp.float32)


def expert_grad(grad_rows, input_rows, gate_rows, up_rows, down_rows):
    contract = (((1,), (1,)), ((), ()))
    gate = lax.dot_general(input_rows, gate_rows, contract, preferred_element_type=jnp.float32)
    up_proj = lax.dot_general(input_rows, up_rows, contract, preferred_element_type=jnp.float32)
    grad_hidden = lax.dot_general(
        grad_rows, down_rows, contract, preferred_element_type=jnp.float32
    )
    sigmoid = jax.nn.sigmoid(gate)
    swish = gate * sigmoid
    hidden = swish * up_proj
    slot_weight = jnp.sum(grad_hidden * hidden, axis=1)
    grad_up = (grad_hidden * swish).astype(jnp.bfloat16)
    grad_gate = (grad_hidden * up_proj * sigmoid * (1.0 + gate * (1.0 - sigmoid))).astype(
        jnp.bfloat16
    )
    partial_value = jnp.dot(grad_gate, gate_rows, preferred_element_type=jnp.float32)
    partial_value = partial_value + jnp.dot(grad_up, up_rows, preferred_element_type=jnp.float32)
    return (partial_value, slot_weight)


def pair_rows(mine, other, pair_low):
    return jnp.where(
        pair_low, jnp.concatenate([mine, other], axis=0), jnp.concatenate([other, mine], axis=0)
    )


def general_device(upstream, saved, routes, route_weight, w_gate, w_up, w_down):
    shards = SHARDS
    groups = shards // 2
    experts_win = lax.axis_size("ep") // shards
    dev_count = experts_win * shards
    my_index = lax.axis_index("ep")
    half_cap = CAP // 2
    pair_low = my_index % 2 == 0
    other_gate, other_up, other_down = from_partner((w_gate[0], w_up[0], w_down[0]), "ep", 0)
    gate_rows = pair_rows(w_gate[0], other_gate, pair_low)
    up_rows = pair_rows(w_up[0], other_up, pair_low)
    down_rows = pair_rows(w_down[0], other_down, pair_low)
    grad_in = passed_along(upstream, "pp", -1)[0]
    inputs = saved[0]
    token_count, width = inputs.shape
    slot_total = experts_win * CAP
    match = route_match(routes[0], experts_win)
    match_three = match.reshape(token_count, TOP, slot_total)
    tok_match = match_three.sum(axis=1).astype(jnp.bfloat16)
    grad_slots = jnp.einsum(
        "ts,td->sd", tok_match, grad_in, preferred_element_type=jnp.float32
    ).astype(jnp.bfloat16)
    input_slots = jnp.einsum(
        "ts,td->sd", tok_match, inputs, preferred_element_type=jnp.float32
    ).astype(jnp.bfloat16)
    grad_halves = grad_slots.reshape(experts_win, 2, half_cap, width)
    input_halves = input_slots.reshape(experts_win, 2, half_cap, width)

    def copies_of(halves):
        return jnp.broadcast_to(halves[:, None], (experts_win, groups, 2, half_cap, width)).reshape(
            dev_count, half_cap, width
        )

    recv_grad, recv_input = (
        lax.all_to_all(copies_of(grad_halves), "ep", split_axis=0, concat_axis=0, tiled=True),
        lax.all_to_all(copies_of(input_halves), "ep", split_axis=0, concat_axis=0, tiled=True),
    )
    grad_rows = recv_grad.reshape(dev_count * half_cap, width)
    input_rows = recv_input.reshape(dev_count * half_cap, width)
    partial_value, slot_weight = expert_grad(grad_rows, input_rows, gate_rows, up_rows, down_rows)
    back_part, back_weight = (
        lax.all_to_all(
            partial_value.reshape(dev_count, half_cap, width),
            "ep",
            split_axis=0,
            concat_axis=0,
            tiled=True,
        ),
        lax.all_to_all(
            slot_weight.reshape(dev_count, half_cap), "ep", split_axis=0, concat_axis=0, tiled=True
        ),
    )
    slot_grads = (
        back_part.reshape(experts_win, groups, 2, half_cap, width)
        .sum(axis=1)
        .reshape(slot_total, width)
    )
    slot_weights = (
        back_weight.reshape(experts_win, groups, 2, half_cap).sum(axis=1).reshape(slot_total)
    )
    weighted = jnp.sum(match_three * route_weight[0][:, :, None], axis=1)
    mixed = jnp.dot(
        weighted, slot_grads, precision=lax.Precision.HIGHEST, preferred_element_type=jnp.float32
    )
    grad_out = (grad_in.astype(jnp.float32) + mixed).astype(jnp.bfloat16)
    weight_out = jnp.dot(
        match, slot_weights, precision=lax.Precision.HIGHEST, preferred_element_type=jnp.float32
    )
    weight_out = weight_out.reshape(token_count, TOP)
    sent_back = passed_along(grad_out[None], "pp", -1)
    return (sent_back, weight_out[None])


def near_call(kernel, out_shape, *args, **kwargs):
    if "in_specs" not in kwargs:
        args = [pltpu.with_memory_space_constraint(arg, pltpu.VMEM) for arg in args]
    params = pltpu.CompilerParams(vmem_limit_bytes=16 * 1024 * 1024)
    return pl.pallas_call(kernel, out_shape=out_shape, compiler_params=params, **kwargs)(*args)


def as_bf16(mask):
    return mask.astype(F32).astype(BF16)


def slot_of_token(routes_t):
    count = routes_t.shape[1]
    hit = routes_t == 0
    found = jnp.max(hit.astype(F32), axis=0, keepdims=True)
    found = jnp.broadcast_to(found, (MAIN, count))
    before = lax.broadcasted_iota(jnp.int32, (count, count), 0) < lax.broadcasted_iota(
        jnp.int32, (count, count), 1
    )
    rank = jnp.dot(found.astype(BF16), as_bf16(before), preferred_element_type=F32)
    slot = jnp.where((found > 0.5) & (rank < CAP - 0.5), rank, -1.0)
    return hit, slot


def main_pick(slot):
    row = lax.broadcasted_iota(jnp.int32, slot.shape, 0).astype(F32)
    return slot == row


def tail_pick(slot, fold):
    row = lax.broadcasted_iota(jnp.int32, slot.shape, 0)
    want = (row + (MAIN - TAIL * fold)).astype(F32)
    inside = (row >= TAIL * fold) & (row < TAIL * fold + TAIL)
    return (slot == want) & inside


def both_picks(slot, fold):
    picks = [main_pick(slot).astype(F32), tail_pick(slot, fold).astype(F32)]
    return jnp.concatenate(picks, axis=0).astype(BF16)


def pick_into(slot, rows_ref, out_ref, before=lambda fold: None):
    width = rows_ref.shape[1]
    part = width // FOLDS
    tail = jnp.zeros((MAIN, part), F32)
    for fold in range(FOLDS):
        before(fold)
        span = slice(fold * part, (fold + 1) * part)
        got = jnp.dot(both_picks(slot, fold), rows_ref[:, span], preferred_element_type=F32)
        out_ref[:, span] = got[:MAIN].astype(BF16)
        tail = tail + got[MAIN:]
    out_ref[:, width:] = tail.astype(BF16)


def pick_inputs_kernel(routes_in, rows_in, base_in, out_ref, routes_ref, base_ref, rows_ref, sems):
    part = rows_ref.shape[1] // FOLDS
    routes_copy = pltpu.make_async_copy(routes_in, routes_ref, sems.at[FOLDS])
    routes_copy.start()
    copies = []
    for fold in range(FOLDS):
        span = slice(fold * part, (fold + 1) * part)
        copies.append(
            pltpu.make_async_copy(rows_in.at[:, span], rows_ref.at[:, span], sems.at[fold])
        )
        copies[-1].start()
    base_copies = []
    for fold in range(FOLDS):
        span = slice(fold * part, (fold + 1) * part)
        base_copies.append(
            pltpu.make_async_copy(
                base_in.at[:, span], base_ref.at[:, span], sems.at[FOLDS + 1 + fold]
            )
        )
        base_copies[-1].start()
    routes_copy.wait()
    _, slot = slot_of_token(routes_ref[...])
    pick_into(slot, rows_ref, out_ref, lambda fold: copies[fold].wait())
    for copy in base_copies:
        copy.wait()


def pick_grads_kernel(routes_ref, rows_ref, out_ref):
    _, slot = slot_of_token(routes_ref[...])
    pick_into(slot, rows_ref, out_ref)


TN = (((0,), (0,)), ((), ()))
NT = (((1,), (1,)), ((), ()))


def back_kernel(routes_ref, weight_ref, back_ref, scale_ref):
    hit, slot = slot_of_token(routes_ref[...])
    size = 2 * MAIN
    eye = as_bf16(
        lax.broadcasted_iota(jnp.int32, (size, 2 * size), 0)
        == lax.broadcasted_iota(jnp.int32, (size, 2 * size), 1) % size
    )
    for fold in range(FOLDS):
        back_ref[fold] = lax.dot_general(
            both_picks(slot, fold), eye, TN, preferred_element_type=F32
        ).astype(BF16)
    weight_row = jnp.sum(jnp.where(hit, weight_ref[...], 0.0), axis=0, keepdims=True)
    main = jnp.sum(jnp.where(main_pick(slot), weight_row, 0.0), axis=1, keepdims=True)
    tail = jnp.zeros_like(main)
    for fold in range(FOLDS):
        tail = tail + jnp.sum(
            jnp.where(tail_pick(slot, fold), weight_row, 0.0), axis=1, keepdims=True
        )
    scale_ref[:, :128] = jnp.broadcast_to(main, (MAIN, 128))
    scale_ref[:, 128:] = jnp.broadcast_to(tail, (MAIN, 128))


def against(blocks, weights_ref, rows_ref):
    width = weights_ref.shape[1]
    part = width // FOLDS
    count = MAIN * len(blocks)
    for k, block in enumerate(blocks):
        rows_ref[MAIN * k : MAIN * (k + 1), :] = block[:, :width]
        rows_ref[count + MAIN * k : count + MAIN * (k + 1), :part] = block[:, width:]
    tails = rows_ref[count:, :part]
    quarter = lax.broadcasted_iota(jnp.int32, (count, weights_ref.shape[0]), 0) % MAIN // TAIL
    main = tail = None
    for fold in range(FOLDS):
        span = slice(fold * part, (fold + 1) * part)
        rows = jnp.concatenate([rows_ref[:count, span], tails], axis=0)
        got = lax.dot_general(rows, weights_ref[:, span], NT, preferred_element_type=F32)
        here = jnp.where(quarter == fold, got[count:], 0.0)
        main = got[:count] if fold == 0 else main + got[:count]
        tail = here if fold == 0 else tail + here
    tail = tail.reshape(len(blocks), MAIN, -1)
    turn = TAIL
    while turn < MAIN:
        tail = tail + pltpu.roll(tail, turn, 1)
        turn *= 2
    return jnp.concatenate([main, tail.reshape(count, -1)], axis=0)


def forward_kernel(own, z2, y0, y2, low, high, gu_ref, h_ref, rows_ref):
    blocks = [own, low.at[0], z2, high.at[0], y0, low.at[1], y2, high.at[1]]
    h_ref[...] = against(blocks, gu_ref, rows_ref)


def three_parts(value):
    high = value.astype(BF16)
    rest = value - high.astype(F32)
    mid = rest.astype(BF16)
    low = (rest - mid.astype(F32)).astype(BF16)
    return [part.astype(F32) for part in (high, mid, low)]


def backward_kernel(*refs):
    g0, g2, z_refs, y_refs, yz_refs, down_ref, gu_ref, h_ref, *outs, rows_ref = refs
    near_a, far_a, near_b, far_b = outs
    half = gu_ref.shape[1] // 2
    part = half // FOLDS
    units = down_ref.shape[0]
    blocks = [g0, z_refs.at[0], g2, z_refs.at[1]]
    blocks += [y_refs.at[0], yz_refs.at[0], y_refs.at[1], yz_refs.at[1]]
    count = MAIN * len(blocks)
    grad_hidden = against(blocks, down_ref, rows_ref)
    gate = h_ref[:, :units]
    up = h_ref[:, units:]
    sigmoid = 1.0 / (1.0 + jnp.exp(-gate))
    swish = gate * sigmoid
    grad_up = (grad_hidden * swish).astype(BF16)
    grad_gate = (grad_hidden * up * sigmoid * (1.0 + gate * (1.0 - sigmoid))).astype(BF16)
    both = jnp.concatenate([grad_gate, grad_up], axis=1)
    place_a = [(ref, k) for ref in (near_a, far_a) for k in range(4)]
    place_b = [((near_b, far_b)[k % 2], k // 2) for k in range(8)]
    quarter = lax.broadcasted_iota(jnp.int32, (count, part), 0) % MAIN // TAIL
    for side, places in enumerate((place_a, place_b)):
        tails = None
        for fold in range(FOLDS):
            start = side * half + fold * part
            value = jnp.dot(both, gu_ref[:, start : start + part], preferred_element_type=F32)
            here = jnp.where(quarter == fold, value[count:], 0.0)
            tails = here if fold == 0 else tails + here
            value = value[:count].astype(BF16)
            for k, (ref, j) in enumerate(places):
                ref[j, :, fold * part : (fold + 1) * part] = value[MAIN * k : MAIN * (k + 1), :]
        tails = tails.astype(BF16)
        for k, (ref, j) in enumerate(places):
            ref[j, :, half : half + part] = tails[MAIN * k : MAIN * (k + 1), :]
    weight = jnp.sum(grad_hidden * (swish * up), axis=1, keepdims=True)
    lane = lax.broadcasted_iota(jnp.int32, (count, 128), 1)
    first = lax.broadcasted_iota(jnp.int32, (count, 128), 0) % MAIN < TAIL
    tile = jnp.zeros((count, 128), F32)
    for k, piece in enumerate(three_parts(weight)):
        tile = jnp.where(lane == k, piece[:count], tile)
        tile = jnp.where((lane == k + 3) & first, piece[count:], tile)
    tile = tile.astype(BF16)
    for k, (ref, j) in enumerate(place_a):
        ref[j, :, half + part :] = tile[MAIN * k : MAIN * (k + 1), :]


def added(one, two):
    return (one.astype(F32) + two.astype(F32)).astype(BF16)


def fold_a_kernel(near_ref, got_ref, send_ref, keep_ref):
    full = near_ref.shape[2] - 128
    for k in range(near_ref.shape[0]):
        ref = (keep_ref, send_ref)[k % 2]
        ref[k // 2, :, :full] = added(near_ref[k, :, :full], got_ref[k, :, :full])
        ref[k // 2, :, full : full + 128] = near_ref[k, :, full:]
        ref[k // 2, :, full + 128 :] = got_ref[k, :, full:]


def fold_b_kernel(near_ref, got_ref, send_ref, keep_ref):
    for k in range(near_ref.shape[0]):
        ref = (keep_ref, send_ref)[k // 2]
        ref[k % 2] = added(near_ref[k], got_ref[k])


def fold_both_kernel(keep_a, got_a, keep_b, got_b, own_ref, send_ref, own_tile, send_tile):
    full = keep_b.shape[2]
    for k, (ref, tile_ref) in enumerate(((own_ref, own_tile), (send_ref, send_tile))):
        ref[:, :full] = added(keep_a[k, :, :full], got_a[k, :, :full])
        ref[:, full:] = added(keep_b[k], got_b[k])
        tile = jnp.zeros((MAIN, 128), F32)
        for source in (keep_a, got_a):
            for start in (full, full + 128):
                tile = tile + source[k, :, start : start + 128].astype(F32)
        tile_ref[...] = tile


def weight_kernel(routes_ref, own_tile, got_tile, after_ref, out_ref):
    hit, slot = slot_of_token(routes_ref[...])
    tile = own_tile[...] + got_tile[...] + after_ref[...]
    lane = lax.broadcasted_iota(jnp.int32, tile.shape, 1)
    main = jnp.sum(jnp.where(lane < 3, tile, 0.0), axis=1, keepdims=True)
    tail = jnp.sum(jnp.where((lane >= 3) & (lane < 6), tile, 0.0), axis=1, keepdims=True)
    row = lax.broadcasted_iota(jnp.int32, slot.shape, 0).astype(F32)
    value = jnp.sum(
        jnp.where(slot == row, main, 0.0) + jnp.where((slot == row + MAIN) & (row < TAIL), tail, 0.0),
        axis=0,
        keepdims=True,
    )
    out_ref[...] = jnp.where(hit, value, 0.0)


def final_kernel(back_ref, scale_ref, one_ref, two_ref, base_ref, out_ref, end_ref, done_ref, sems):
    end_ref[...] = jnp.zeros_like(end_ref)
    width = base_ref.shape[1]
    half = width // 2
    part = half // FOLDS
    copies = []
    for side in range(2):
        first = side * (half + part)
        for fold in range(FOLDS):
            rows = []
            for lane, start in ((0, first + fold * part), (128, first + half)):
                total = one_ref[:, start : start + part].astype(F32)
                total = total + two_ref[:, start : start + part].astype(F32)
                rows.append(total * scale_ref[:, lane : lane + 1])
            rows = jnp.concatenate(rows, axis=0)
            high = rows.astype(BF16)
            low = (rows - high.astype(F32)).astype(BF16)
            rows = jnp.concatenate([high, low], axis=0)
            mixed = jnp.dot(back_ref[fold], rows, preferred_element_type=F32)
            start = side * half + fold * part
            span = slice(start, start + part)
            done_ref[:, span] = (base_ref[:, span].astype(F32) + mixed).astype(BF16)
            if fold % 2:
                span = slice(start - part, start + part)
                copy = pltpu.make_async_copy(
                    done_ref.at[:, span], out_ref.at[:, span], sems.at[len(copies)]
                )
                copy.start()
                copies.append(copy)
    for copy in copies:
        copy.wait()


def across(value, bits):
    count = lax.axis_size("ep")
    return lax.ppermute(value, "ep", [(i, i ^ bits) for i in range(count)])


def sections_across(value, bits):
    count = lax.axis_size("ep")
    pairs = [(s * count + i, (1 - s) * count + (i ^ bits)) for s in range(2) for i in range(count)]
    return lax.ppermute(value, ("pp", "ep"), pairs)


Y1, Z1, Z2 = 2, 4, 8


def single_device(upstream, saved, routes, route_weight, w_gate, w_up, w_down):
    routes_t = routes[0].T
    weight_t = route_weight[0].T
    next_routes = passed_along(routes_t, "pp", 1)
    count, width = saved.shape[1:]
    full = width + width // FOLDS
    half = full // 2
    units = 2 * w_gate.shape[1]
    slots = SHARDS // 2 * 2 * MAIN
    hbm = pl.BlockSpec(memory_space=pltpu.HBM)
    tile = pltpu.VMEM((MAIN, 128), F32)

    input_block, near_routes, base = near_call(
        pick_inputs_kernel,
        [
            pltpu.VMEM((MAIN, full), BF16),
            pltpu.VMEM(routes_t.shape, jnp.int32),
            pltpu.VMEM((count, width), BF16),
        ],
        *(pltpu.with_memory_space_constraint(v, pltpu.HBM) for v in (routes_t, saved[0], upstream[0])),
        in_specs=[hbm] * 3,
        scratch_shapes=[
            pltpu.VMEM((count, width), BF16),
            pltpu.SemaphoreType.DMA((2 * FOLDS + 1,)),
        ],
        name="pick_inputs",
    )
    grad_block = near_call(
        pick_grads_kernel, pltpu.VMEM((MAIN, full), BF16), next_routes, base, name="pick_grads"
    )

    own = (w_gate[0], w_up[0], w_down[0])
    other = from_partner(own, "ep", 0)
    input_block, grad_block, other = lax.optimization_barrier((input_block, grad_block, other))

    grad_z2 = sections_across(grad_block, Z2)
    grad_z0 = sections_across(grad_block, 0)
    input_z2 = across(input_block, Z2)
    input_y0 = across(input_block, Y1)
    gate_up = jnp.concatenate([own[0], other[0], own[1], other[1]], axis=0)
    down = jnp.concatenate([own[2], other[2]], axis=0)

    grad_z = jnp.stack([grad_z0, grad_z2])
    grad_z1 = across(grad_z, Z1)
    grad_y = across(grad_z, Y1)
    input_y2 = across(input_z2, Y1)
    input_low = across(jnp.stack([input_block, input_y0]), Z1)
    input_high = across(jnp.stack([input_z2, input_y2]), Z1)
    grad_yz1 = across(grad_z1, Y1)

    late_routes, weight_t, _ = lax.optimization_barrier((next_routes, weight_t, grad_z1))
    back, scale = near_call(
        back_kernel,
        [pltpu.VMEM((FOLDS, count, 4 * MAIN), BF16), pltpu.VMEM((MAIN, 256), F32)],
        late_routes,
        passed_along(weight_t, "pp", 1),
        name="back_rows",
    )
    input_high, back, scale = lax.optimization_barrier((input_high, back, scale))
    hidden = near_call(
        forward_kernel,
        pltpu.VMEM((slots, 2 * units), F32),
        input_block,
        input_z2,
        input_y0,
        input_y2,
        input_low,
        input_high,
        gate_up,
        scratch_shapes=[pltpu.VMEM((slots, width), BF16)],
        name="expert_forward",
    )
    side_a = pltpu.VMEM((4, MAIN, half + 128), BF16)
    side_b = pltpu.VMEM((4, MAIN, half), BF16)
    near_a, far_a, near_b, far_b = near_call(
        backward_kernel,
        [side_a, side_a, side_b, side_b],
        grad_z0,
        grad_z2,
        grad_z1,
        grad_y,
        grad_yz1,
        down,
        gate_up,
        hidden,
        scratch_shapes=[pltpu.VMEM((slots, width), BF16)],
        name="expert_backward",
    )
    got_a = across(far_a, Y1)
    got_b = across(far_b, Z1)
    send_a, keep_a = near_call(
        fold_a_kernel, [pltpu.VMEM((2, MAIN, half + 256), BF16)] * 2, near_a, got_a, name="fold_a"
    )
    send_b, keep_b = near_call(
        fold_b_kernel, [pltpu.VMEM((2, MAIN, half), BF16)] * 2, near_b, got_b, name="fold_b"
    )
    rows_0, rows_2, tile_0, tile_2 = near_call(
        fold_both_kernel,
        [pltpu.VMEM((MAIN, full), BF16)] * 2 + [tile] * 2,
        keep_a,
        across(send_a, Z1),
        keep_b,
        across(send_b, Y1),
        name="fold_both",
    )
    got_2 = sections_across(rows_2, Z2)
    got_0 = sections_across(rows_0, 0)
    grad_prev, end = near_call(
        final_kernel,
        [jax.ShapeDtypeStruct((count, width), BF16), tile],
        back,
        scale,
        got_0,
        got_2,
        base,
        out_specs=[hbm, pl.BlockSpec(memory_space=pltpu.VMEM)],
        scratch_shapes=[pltpu.VMEM((count, width), BF16), pltpu.SemaphoreType.DMA((FOLDS,))],
        name="final_rows",
    )
    weight_out = near_call(
        weight_kernel,
        jax.ShapeDtypeStruct((TOP, count), F32),
        near_routes,
        tile_0,
        across(tile_2, Z2),
        end,
        name="weight_out",
    )
    return (grad_prev[None], weight_out.T[None])


def solution(mesh):
    single = mesh.shape["ep"] == SHARDS and mesh.shape["pp"] == 2
    spec = P("pp", "ep", None)
    return jax.shard_map(
        single_device if single else general_device,
        mesh=mesh,
        in_specs=(spec,) * 7,
        out_specs=(spec, spec),
        check_vma=False,
    )
```

```python
import functools

import jax
import jax.numpy as jnp
from jax import lax
from jax.experimental import pallas as pl
from jax.experimental.pallas import tpu as pltpu
from jax.sharding import PartitionSpec as P

TOP = 8
SHARDS = 16
CAP = 10
MAIN = 8
TAIL = CAP - MAIN
FOLDS = MAIN // TAIL
F32 = jnp.float32
BF16 = jnp.bfloat16


def from_partner(block, axis, apart):
    count = lax.axis_size(axis)
    route = []
    for low in range(count):
        high = low | 1 << apart
        if high != low and high < count:
            route += [(low, high), (high, low)]
    return lax.ppermute(block, axis, route)


def passed_along(value, axis, by):
    size = lax.axis_size(axis)
    return lax.ppermute(value, axis, [(i, (i + by) % size) for i in range(size)])


def route_match(block_routes, experts_win):
    flat_routes = block_routes.reshape(-1)
    onehot = (flat_routes[:, None] == jnp.arange(experts_win, dtype=jnp.int32)[None, :]).astype(
        jnp.int32
    )
    earlier = jnp.cumsum(onehot, axis=0) - onehot
    ranking = jnp.sum(earlier * onehot, axis=1)
    kept = (flat_routes < experts_win) & (ranking < CAP)
    slot_index = flat_routes * CAP + ranking
    match = (slot_index[:, None] == jnp.arange(experts_win * CAP, dtype=jnp.int32)[None, :]) & kept[
        :, None
    ]
    return match.astype(jnp.float32)


def expert_grad(grad_rows, input_rows, gate_rows, up_rows, down_rows):
    contract = (((1,), (1,)), ((), ()))
    gate = lax.dot_general(input_rows, gate_rows, contract, preferred_element_type=jnp.float32)
    up_proj = lax.dot_general(input_rows, up_rows, contract, preferred_element_type=jnp.float32)
    grad_hidden = lax.dot_general(
        grad_rows, down_rows, contract, preferred_element_type=jnp.float32
    )
    sigmoid = jax.nn.sigmoid(gate)
    swish = gate * sigmoid
    hidden = swish * up_proj
    slot_weight = jnp.sum(grad_hidden * hidden, axis=1)
    grad_up = (grad_hidden * swish).astype(jnp.bfloat16)
    grad_gate = (grad_hidden * up_proj * sigmoid * (1.0 + gate * (1.0 - sigmoid))).astype(
        jnp.bfloat16
    )
    partial_value = jnp.dot(grad_gate, gate_rows, preferred_element_type=jnp.float32)
    partial_value = partial_value + jnp.dot(grad_up, up_rows, preferred_element_type=jnp.float32)
    return (partial_value, slot_weight)


def pair_rows(mine, other, pair_low):
    return jnp.where(
        pair_low, jnp.concatenate([mine, other], axis=0), jnp.concatenate([other, mine], axis=0)
    )


def general_device(upstream, saved, routes, route_weight, w_gate, w_up, w_down):
    shards = SHARDS
    groups = shards // 2
    experts_win = lax.axis_size("ep") // shards
    dev_count = experts_win * shards
    my_index = lax.axis_index("ep")
    half_cap = CAP // 2
    pair_low = my_index % 2 == 0
    other_gate, other_up, other_down = from_partner((w_gate[0], w_up[0], w_down[0]), "ep", 0)
    gate_rows = pair_rows(w_gate[0], other_gate, pair_low)
    up_rows = pair_rows(w_up[0], other_up, pair_low)
    down_rows = pair_rows(w_down[0], other_down, pair_low)
    grad_in = passed_along(upstream, "pp", -1)[0]
    inputs = saved[0]
    token_count, width = inputs.shape
    slot_total = experts_win * CAP
    match = route_match(routes[0], experts_win)
    match_three = match.reshape(token_count, TOP, slot_total)
    tok_match = match_three.sum(axis=1).astype(jnp.bfloat16)
    grad_slots = jnp.einsum(
        "ts,td->sd", tok_match, grad_in, preferred_element_type=jnp.float32
    ).astype(jnp.bfloat16)
    input_slots = jnp.einsum(
        "ts,td->sd", tok_match, inputs, preferred_element_type=jnp.float32
    ).astype(jnp.bfloat16)
    grad_halves = grad_slots.reshape(experts_win, 2, half_cap, width)
    input_halves = input_slots.reshape(experts_win, 2, half_cap, width)

    def copies_of(halves):
        return jnp.broadcast_to(halves[:, None], (experts_win, groups, 2, half_cap, width)).reshape(
            dev_count, half_cap, width
        )

    recv_grad, recv_input = (
        lax.all_to_all(copies_of(grad_halves), "ep", split_axis=0, concat_axis=0, tiled=True),
        lax.all_to_all(copies_of(input_halves), "ep", split_axis=0, concat_axis=0, tiled=True),
    )
    grad_rows = recv_grad.reshape(dev_count * half_cap, width)
    input_rows = recv_input.reshape(dev_count * half_cap, width)
    partial_value, slot_weight = expert_grad(grad_rows, input_rows, gate_rows, up_rows, down_rows)
    back_part, back_weight = (
        lax.all_to_all(
            partial_value.reshape(dev_count, half_cap, width),
            "ep",
            split_axis=0,
            concat_axis=0,
            tiled=True,
        ),
        lax.all_to_all(
            slot_weight.reshape(dev_count, half_cap), "ep", split_axis=0, concat_axis=0, tiled=True
        ),
    )
    slot_grads = (
        back_part.reshape(experts_win, groups, 2, half_cap, width)
        .sum(axis=1)
        .reshape(slot_total, width)
    )
    slot_weights = (
        back_weight.reshape(experts_win, groups, 2, half_cap).sum(axis=1).reshape(slot_total)
    )
    weighted = jnp.sum(match_three * route_weight[0][:, :, None], axis=1)
    mixed = jnp.dot(
        weighted, slot_grads, precision=lax.Precision.HIGHEST, preferred_element_type=jnp.float32
    )
    grad_out = (grad_in.astype(jnp.float32) + mixed).astype(jnp.bfloat16)
    weight_out = jnp.dot(
        match, slot_weights, precision=lax.Precision.HIGHEST, preferred_element_type=jnp.float32
    )
    weight_out = weight_out.reshape(token_count, TOP)
    sent_back = passed_along(grad_out[None], "pp", -1)
    return (sent_back, weight_out[None])


def near_call(kernel, out_shape, *args, **kwargs):
    if "in_specs" not in kwargs:
        args = [pltpu.with_memory_space_constraint(arg, pltpu.VMEM) for arg in args]
    params = pltpu.CompilerParams(vmem_limit_bytes=16 * 1024 * 1024)
    return pl.pallas_call(kernel, out_shape=out_shape, compiler_params=params, **kwargs)(*args)


def as_bf16(mask):
    return mask.astype(F32).astype(BF16)


def slot_of_token(routes_t):
    count = routes_t.shape[1]
    hit = routes_t == 0
    found = jnp.max(hit.astype(F32), axis=0, keepdims=True)
    found = jnp.broadcast_to(found, (MAIN, count))
    before = lax.broadcasted_iota(jnp.int32, (count, count), 0) < lax.broadcasted_iota(
        jnp.int32, (count, count), 1
    )
    rank = jnp.dot(found.astype(BF16), as_bf16(before), preferred_element_type=F32)
    slot = jnp.where((found > 0.5) & (rank < CAP - 0.5), rank, -1.0)
    return hit, slot


def main_pick(slot):
    row = lax.broadcasted_iota(jnp.int32, slot.shape, 0).astype(F32)
    return slot == row


def tail_pick(slot, fold):
    row = lax.broadcasted_iota(jnp.int32, slot.shape, 0)
    want = (row + (MAIN - TAIL * fold)).astype(F32)
    inside = (row >= TAIL * fold) & (row < TAIL * fold + TAIL)
    return (slot == want) & inside


def both_picks(slot, fold):
    picks = [main_pick(slot).astype(F32), tail_pick(slot, fold).astype(F32)]
    return jnp.concatenate(picks, axis=0).astype(BF16)


def three_parts(value):
    high = value.astype(BF16)
    rest = value - high.astype(F32)
    mid = rest.astype(BF16)
    low = (rest - mid.astype(F32)).astype(BF16)
    return [part.astype(F32) for part in (high, mid, low)]


def pick_into(slot, rows_ref, out_ref, before=lambda fold: None):
    width = rows_ref.shape[1]
    part = width // FOLDS
    tail = jnp.zeros((MAIN, part), F32)
    for fold in range(FOLDS):
        before(fold)
        span = slice(fold * part, (fold + 1) * part)
        got = jnp.dot(both_picks(slot, fold), rows_ref[:, span], preferred_element_type=F32)
        out_ref[:, span] = got[:MAIN].astype(BF16)
        tail = tail + got[MAIN:]
    out_ref[:, width:] = tail.astype(BF16)


def pick_inputs_kernel(
    routes_in, weight_in, rows_in, base_in, out_ref, slot_ref, weight_ref, base_ref, routes_ref, rows_ref, sems
):
    part = rows_ref.shape[1] // FOLDS
    routes_copy = pltpu.make_async_copy(routes_in, routes_ref, sems.at[2 * FOLDS])
    routes_copy.start()
    weight_copy = pltpu.make_async_copy(weight_in, weight_ref, sems.at[2 * FOLDS + 1])
    weight_copy.start()
    copies = []
    for fold in range(FOLDS):
        span = slice(fold * part, (fold + 1) * part)
        copies.append(
            pltpu.make_async_copy(rows_in.at[:, span], rows_ref.at[:, span], sems.at[fold])
        )
        copies[-1].start()
    base_copies = []
    for fold in range(FOLDS):
        span = slice(fold * part, (fold + 1) * part)
        base_copies.append(
            pltpu.make_async_copy(
                base_in.at[:, span], base_ref.at[:, span], sems.at[FOLDS + fold]
            )
        )
        base_copies[-1].start()
    routes_copy.wait()
    hit, slot = slot_of_token(routes_ref[...])
    slot_ref[...] = jnp.where(hit, slot, -1.0)
    pick_into(slot, rows_ref, out_ref, lambda fold: copies[fold].wait())
    weight_copy.wait()
    for copy in base_copies:
        copy.wait()


def pick_grads_kernel(routes_ref, rows_ref, weight_ref, out_ref, with_ref):
    full = out_ref.shape[1]
    _, slot = slot_of_token(routes_ref[...])
    pick_into(slot, rows_ref, out_ref)
    with_ref[:, :full] = out_ref[...]
    for k, piece in enumerate(three_parts(weight_ref[...])):
        with_ref[:, full + 128 * k : full + 128 * (k + 1)] = piece.astype(BF16)


TN = (((0,), (0,)), ((), ()))
NT = (((1,), (1,)), ((), ()))


def back_kernel(routes_ref, with_ref, back_ref, scale_ref):
    hit, slot = slot_of_token(routes_ref[...])
    size = 2 * MAIN
    eye = as_bf16(
        lax.broadcasted_iota(jnp.int32, (size, 2 * size), 0)
        == lax.broadcasted_iota(jnp.int32, (size, 2 * size), 1) % size
    )
    for fold in range(FOLDS):
        back_ref[fold] = lax.dot_general(
            both_picks(slot, fold), eye, TN, preferred_element_type=F32
        ).astype(BF16)
    weight = jnp.zeros(hit.shape, F32)
    for k in range(3, 0, -1):
        start = with_ref.shape[1] - 128 * k
        weight = weight + with_ref[:, start : start + 128].astype(F32)
    weight_row = jnp.sum(jnp.where(hit, weight, 0.0), axis=0, keepdims=True)
    main = jnp.sum(jnp.where(main_pick(slot), weight_row, 0.0), axis=1, keepdims=True)
    tail = jnp.zeros_like(main)
    for fold in range(FOLDS):
        tail = tail + jnp.sum(
            jnp.where(tail_pick(slot, fold), weight_row, 0.0), axis=1, keepdims=True
        )
    scale_ref[:, :128] = jnp.broadcast_to(main, (MAIN, 128))
    scale_ref[:, 128:] = jnp.broadcast_to(tail, (MAIN, 128))


def against(blocks, weights_ref, rows_ref):
    width = weights_ref.shape[1]
    part = width // FOLDS
    count = MAIN * len(blocks)
    for k, block in enumerate(blocks):
        rows_ref[MAIN * k : MAIN * (k + 1), :] = block[:, :width]
        rows_ref[count + MAIN * k : count + MAIN * (k + 1), :part] = block[:, width : width + part]
    tails = rows_ref[count:, :part]
    quarter = lax.broadcasted_iota(jnp.int32, (count, weights_ref.shape[0]), 0) % MAIN // TAIL
    main = tail = None
    for fold in range(FOLDS):
        span = slice(fold * part, (fold + 1) * part)
        rows = jnp.concatenate([rows_ref[:count, span], tails], axis=0)
        got = lax.dot_general(rows, weights_ref[:, span], NT, preferred_element_type=F32)
        here = jnp.where(quarter == fold, got[count:], 0.0)
        main = got[:count] if fold == 0 else main + got[:count]
        tail = here if fold == 0 else tail + here
    tail = tail.reshape(len(blocks), MAIN, -1)
    turn = TAIL
    while turn < MAIN:
        tail = tail + pltpu.roll(tail, turn, 1)
        turn *= 2
    return jnp.concatenate([main, tail.reshape(count, -1)], axis=0)


def forward_kernel(own, z2, y0, y2, low, high, gu_ref, h_ref, rows_ref):
    blocks = [own, low.at[0], z2, high.at[0], y0, low.at[1], y2, high.at[1]]
    h_ref[...] = against(blocks, gu_ref, rows_ref)


def backward_kernel(*refs):
    g0, g2, z_refs, y_refs, yz_refs, down_ref, gu_ref, h_ref, *outs, rows_ref = refs
    near_a, far_a, near_b, far_b = outs
    half = gu_ref.shape[1] // 2
    part = half // FOLDS
    units = down_ref.shape[0]
    blocks = [g0, z_refs.at[0], g2, z_refs.at[1]]
    blocks += [y_refs.at[0], yz_refs.at[0], y_refs.at[1], yz_refs.at[1]]
    count = MAIN * len(blocks)
    grad_hidden = against(blocks, down_ref, rows_ref)
    gate = h_ref[:, :units]
    up = h_ref[:, units:]
    sigmoid = 1.0 / (1.0 + jnp.exp(-gate))
    swish = gate * sigmoid
    grad_up = (grad_hidden * swish).astype(BF16)
    grad_gate = (grad_hidden * up * sigmoid * (1.0 + gate * (1.0 - sigmoid))).astype(BF16)
    both = jnp.concatenate([grad_gate, grad_up], axis=1)
    place_a = [(ref, k) for ref in (near_a, far_a) for k in range(4)]
    place_b = [((near_b, far_b)[k % 2], k // 2) for k in range(8)]
    quarter = lax.broadcasted_iota(jnp.int32, (count, part), 0) % MAIN // TAIL
    for side, places in enumerate((place_a, place_b)):
        tails = None
        for fold in range(FOLDS):
            start = side * half + fold * part
            value = jnp.dot(both, gu_ref[:, start : start + part], preferred_element_type=F32)
            here = jnp.where(quarter == fold, value[count:], 0.0)
            tails = here if fold == 0 else tails + here
            value = value[:count].astype(BF16)
            for k, (ref, j) in enumerate(places):
                ref[j, :, fold * part : (fold + 1) * part] = value[MAIN * k : MAIN * (k + 1), :]
        tails = tails.astype(BF16)
        for k, (ref, j) in enumerate(places):
            ref[j, :, half : half + part] = tails[MAIN * k : MAIN * (k + 1), :]
    weight = jnp.sum(grad_hidden * (swish * up), axis=1, keepdims=True)
    lane = lax.broadcasted_iota(jnp.int32, (count, 128), 1)
    first = lax.broadcasted_iota(jnp.int32, (count, 128), 0) % MAIN < TAIL
    tile = jnp.zeros((count, 128), F32)
    for k, piece in enumerate(three_parts(weight)):
        tile = jnp.where(lane == k, piece[:count], tile)
        tile = jnp.where((lane == k + 3) & first, piece[count:], tile)
    tile = tile.astype(BF16)
    for k, (ref, j) in enumerate(place_a):
        ref[j, :, half + part :] = tile[MAIN * k : MAIN * (k + 1), :]


def added(one, two):
    return (one.astype(F32) + two.astype(F32)).astype(BF16)


def fold_a_kernel(near_ref, got_ref, send_ref, keep_ref):
    full = near_ref.shape[2] - 128
    for k in range(near_ref.shape[0]):
        ref = (keep_ref, send_ref)[k % 2]
        ref[k // 2, :, :full] = added(near_ref[k, :, :full], got_ref[k, :, :full])
        ref[k // 2, :, full : full + 128] = near_ref[k, :, full:]
        ref[k // 2, :, full + 128 :] = got_ref[k, :, full:]


def fold_b_kernel(near_ref, got_ref, send_ref, keep_ref):
    for k in range(near_ref.shape[0]):
        ref = (keep_ref, send_ref)[k // 2]
        ref[k % 2] = added(near_ref[k], got_ref[k])


def fold_both_kernel(keep_a, got_a, keep_b, got_b, own_ref, send_ref, own_tile, send_tile):
    full = keep_b.shape[2]
    for k, (ref, tile_ref) in enumerate(((own_ref, own_tile), (send_ref, send_tile))):
        ref[:, :full] = added(keep_a[k, :, :full], got_a[k, :, :full])
        ref[:, full:] = added(keep_b[k], got_b[k])
        tile = jnp.zeros((MAIN, 128), F32)
        for source in (keep_a, got_a):
            for start in (full, full + 128):
                tile = tile + source[k, :, start : start + 128].astype(F32)
        tile_ref[...] = tile


def weight_kernel(slot_ref, own_tile, got_tile, after_ref, out_ref):
    tile = own_tile[...] + got_tile[...] + after_ref[...]
    lane = lax.broadcasted_iota(jnp.int32, tile.shape, 1)
    main = jnp.sum(jnp.where(lane < 3, tile, 0.0), axis=1, keepdims=True)
    tail = jnp.sum(jnp.where((lane >= 3) & (lane < 6), tile, 0.0), axis=1, keepdims=True)
    table = slot_ref[...]
    slot = jnp.broadcast_to(jnp.max(table, axis=0, keepdims=True), table.shape)
    row = lax.broadcasted_iota(jnp.int32, slot.shape, 0).astype(F32)
    value = jnp.sum(
        jnp.where(slot == row, main, 0.0) + jnp.where((slot == row + MAIN) & (row < TAIL), tail, 0.0),
        axis=0,
        keepdims=True,
    )
    out_ref[...] = jnp.where(table >= 0.0, value, 0.0)


def final_kernel(back_ref, scale_ref, one_ref, two_ref, base_ref, out_ref, end_ref, done_ref, sems):
    end_ref[...] = jnp.zeros_like(end_ref)
    width = base_ref.shape[1]
    half = width // 2
    part = half // FOLDS
    copies = []
    for side in range(2):
        first = side * (half + part)
        for fold in range(FOLDS):
            rows = []
            for lane, start in ((0, first + fold * part), (128, first + half)):
                total = one_ref[:, start : start + part].astype(F32)
                total = total + two_ref[:, start : start + part].astype(F32)
                rows.append(total * scale_ref[:, lane : lane + 1])
            rows = jnp.concatenate(rows, axis=0)
            high = rows.astype(BF16)
            low = (rows - high.astype(F32)).astype(BF16)
            rows = jnp.concatenate([high, low], axis=0)
            mixed = jnp.dot(back_ref[fold], rows, preferred_element_type=F32)
            start = side * half + fold * part
            span = slice(start, start + part)
            done_ref[:, span] = (base_ref[:, span].astype(F32) + mixed).astype(BF16)
            if fold % 2:
                span = slice(start - part, start + part)
                copy = pltpu.make_async_copy(
                    done_ref.at[:, span], out_ref.at[:, span], sems.at[len(copies)]
                )
                copy.start()
                copies.append(copy)
    for copy in copies:
        copy.wait()


def across(value, bits):
    count = lax.axis_size("ep")
    return lax.ppermute(value, "ep", [(i, i ^ bits) for i in range(count)])


def sections_across(value, bits):
    count = lax.axis_size("ep")
    pairs = [(s * count + i, (1 - s) * count + (i ^ bits)) for s in range(2) for i in range(count)]
    return lax.ppermute(value, ("pp", "ep"), pairs)


Y1, Z1, Z2 = 2, 4, 8


def single_device(upstream, saved, routes, route_weight, w_gate, w_up, w_down):
    routes_t = routes[0].T
    weight_t = route_weight[0].T
    next_routes = passed_along(routes_t, "pp", 1)
    count, width = saved.shape[1:]
    full = width + width // FOLDS
    half = full // 2
    units = 2 * w_gate.shape[1]
    slots = SHARDS // 2 * 2 * MAIN
    hbm = pl.BlockSpec(memory_space=pltpu.HBM)
    tile = pltpu.VMEM((MAIN, 128), F32)

    input_block, slot_table, near_weight, base = near_call(
        pick_inputs_kernel,
        [
            pltpu.VMEM((MAIN, full), BF16),
            pltpu.VMEM(routes_t.shape, F32),
            pltpu.VMEM(weight_t.shape, F32),
            pltpu.VMEM((count, width), BF16),
        ],
        *(
            pltpu.with_memory_space_constraint(v, pltpu.HBM)
            for v in (routes_t, weight_t, saved[0], upstream[0])
        ),
        in_specs=[hbm] * 4,
        scratch_shapes=[
            pltpu.VMEM(routes_t.shape, jnp.int32),
            pltpu.VMEM((count, width), BF16),
            pltpu.SemaphoreType.DMA((2 * FOLDS + 2,)),
        ],
        name="pick_inputs",
    )
    grad_block, grad_with = near_call(
        pick_grads_kernel,
        [pltpu.VMEM((MAIN, full), BF16), pltpu.VMEM((MAIN, full + 384), BF16)],
        next_routes,
        base,
        near_weight,
        name="pick_grads",
    )

    grad_z2 = sections_across(grad_block, Z2)
    grad_z0 = sections_across(grad_with, 0)
    input_z2 = across(input_block, Z2)
    input_y0 = across(input_block, Y1)
    own = jnp.stack([w_gate[0], w_up[0], w_down[0]])
    own, _ = lax.optimization_barrier((own, input_z2))
    other = across(own, 1)
    gate_up = jnp.concatenate([own[0], other[0], own[1], other[1]], axis=0)
    down = jnp.concatenate([own[2], other[2]], axis=0)

    grad_z = jnp.stack([grad_z0[:, :full], grad_z2])
    grad_z1 = across(grad_z, Z1)
    grad_y = across(grad_z, Y1)
    input_y2 = across(input_z2, Y1)
    input_low = across(jnp.stack([input_block, input_y0]), Z1)
    input_high = across(jnp.stack([input_z2, input_y2]), Z1)
    grad_yz1 = across(grad_z1, Y1)

    late_routes, late_with, _ = lax.optimization_barrier((next_routes, grad_z0, grad_z1))
    back, scale = near_call(
        back_kernel,
        [pltpu.VMEM((FOLDS, count, 4 * MAIN), BF16), pltpu.VMEM((MAIN, 256), F32)],
        late_routes,
        late_with,
        name="back_rows",
    )
    input_high, back, scale = lax.optimization_barrier((input_high, back, scale))
    hidden = near_call(
        forward_kernel,
        pltpu.VMEM((slots, 2 * units), F32),
        input_block,
        input_z2,
        input_y0,
        input_y2,
        input_low,
        input_high,
        gate_up,
        scratch_shapes=[pltpu.VMEM((slots, width), BF16)],
        name="expert_forward",
    )
    side_a = pltpu.VMEM((4, MAIN, half + 128), BF16)
    side_b = pltpu.VMEM((4, MAIN, half), BF16)
    near_a, far_a, near_b, far_b = near_call(
        backward_kernel,
        [side_a, side_a, side_b, side_b],
        grad_z0,
        grad_z2,
        grad_z1,
        grad_y,
        grad_yz1,
        down,
        gate_up,
        hidden,
        scratch_shapes=[pltpu.VMEM((slots, width), BF16)],
        name="expert_backward",
    )
    got_a = across(far_a, Y1)
    got_b = across(far_b, Z1)
    send_a, keep_a = near_call(
        fold_a_kernel, [pltpu.VMEM((2, MAIN, half + 256), BF16)] * 2, near_a, got_a, name="fold_a"
    )
    send_b, keep_b = near_call(
        fold_b_kernel, [pltpu.VMEM((2, MAIN, half), BF16)] * 2, near_b, got_b, name="fold_b"
    )
    rows_0, rows_2, tile_0, tile_2 = near_call(
        fold_both_kernel,
        [pltpu.VMEM((MAIN, full), BF16)] * 2 + [tile] * 2,
        keep_a,
        across(send_a, Z1),
        keep_b,
        across(send_b, Y1),
        name="fold_both",
    )
    got_2 = sections_across(rows_2, Z2)
    got_0 = sections_across(rows_0, 0)
    grad_prev, end = near_call(
        final_kernel,
        [jax.ShapeDtypeStruct((count, width), BF16), tile],
        back,
        scale,
        got_0,
        got_2,
        base,
        out_specs=[hbm, pl.BlockSpec(memory_space=pltpu.VMEM)],
        scratch_shapes=[pltpu.VMEM((count, width), BF16), pltpu.SemaphoreType.DMA((FOLDS,))],
        name="final_rows",
    )
    weight_out = near_call(
        weight_kernel,
        jax.ShapeDtypeStruct((TOP, count), F32),
        slot_table,
        tile_0,
        across(tile_2, Z2),
        end,
        name="weight_out",
    )
    return (grad_prev[None], weight_out.T[None])


def solution(mesh):
    single = mesh.shape["ep"] == SHARDS and mesh.shape["pp"] == 2
    spec = P("pp", "ep", None)
    return jax.shard_map(
        single_device if single else general_device,
        mesh=mesh,
        in_specs=(spec,) * 7,
        out_specs=(spec, spec),
        check_vma=False,
    )
```

```python
import functools

import jax
import jax.numpy as jnp
from jax import lax
from jax.experimental import pallas as pl
from jax.experimental.pallas import tpu as pltpu
from jax.sharding import PartitionSpec as P

TOP = 8
SHARDS = 16
CAP = 10
MAIN = 8
TAIL = CAP - MAIN
FOLDS = MAIN // TAIL
F32 = jnp.float32
BF16 = jnp.bfloat16


def from_partner(block, axis, apart):
    count = lax.axis_size(axis)
    route = []
    for low in range(count):
        high = low | 1 << apart
        if high != low and high < count:
            route += [(low, high), (high, low)]
    return lax.ppermute(block, axis, route)


def passed_along(value, axis, by):
    size = lax.axis_size(axis)
    return lax.ppermute(value, axis, [(i, (i + by) % size) for i in range(size)])


def route_match(block_routes, experts_win):
    flat_routes = block_routes.reshape(-1)
    onehot = (flat_routes[:, None] == jnp.arange(experts_win, dtype=jnp.int32)[None, :]).astype(
        jnp.int32
    )
    earlier = jnp.cumsum(onehot, axis=0) - onehot
    ranking = jnp.sum(earlier * onehot, axis=1)
    kept = (flat_routes < experts_win) & (ranking < CAP)
    slot_index = flat_routes * CAP + ranking
    match = (slot_index[:, None] == jnp.arange(experts_win * CAP, dtype=jnp.int32)[None, :]) & kept[
        :, None
    ]
    return match.astype(jnp.float32)


def expert_grad(grad_rows, input_rows, gate_rows, up_rows, down_rows):
    contract = (((1,), (1,)), ((), ()))
    gate = lax.dot_general(input_rows, gate_rows, contract, preferred_element_type=jnp.float32)
    up_proj = lax.dot_general(input_rows, up_rows, contract, preferred_element_type=jnp.float32)
    grad_hidden = lax.dot_general(
        grad_rows, down_rows, contract, preferred_element_type=jnp.float32
    )
    sigmoid = jax.nn.sigmoid(gate)
    swish = gate * sigmoid
    hidden = swish * up_proj
    slot_weight = jnp.sum(grad_hidden * hidden, axis=1)
    grad_up = (grad_hidden * swish).astype(jnp.bfloat16)
    grad_gate = (grad_hidden * up_proj * sigmoid * (1.0 + gate * (1.0 - sigmoid))).astype(
        jnp.bfloat16
    )
    partial_value = jnp.dot(grad_gate, gate_rows, preferred_element_type=jnp.float32)
    partial_value = partial_value + jnp.dot(grad_up, up_rows, preferred_element_type=jnp.float32)
    return (partial_value, slot_weight)


def pair_rows(mine, other, pair_low):
    return jnp.where(
        pair_low, jnp.concatenate([mine, other], axis=0), jnp.concatenate([other, mine], axis=0)
    )


def general_device(upstream, saved, routes, route_weight, w_gate, w_up, w_down):
    shards = SHARDS
    groups = shards // 2
    experts_win = lax.axis_size("ep") // shards
    dev_count = experts_win * shards
    my_index = lax.axis_index("ep")
    half_cap = CAP // 2
    pair_low = my_index % 2 == 0
    other_gate, other_up, other_down = from_partner((w_gate[0], w_up[0], w_down[0]), "ep", 0)
    gate_rows = pair_rows(w_gate[0], other_gate, pair_low)
    up_rows = pair_rows(w_up[0], other_up, pair_low)
    down_rows = pair_rows(w_down[0], other_down, pair_low)
    grad_in = passed_along(upstream, "pp", -1)[0]
    inputs = saved[0]
    token_count, width = inputs.shape
    slot_total = experts_win * CAP
    match = route_match(routes[0], experts_win)
    match_three = match.reshape(token_count, TOP, slot_total)
    tok_match = match_three.sum(axis=1).astype(jnp.bfloat16)
    grad_slots = jnp.einsum(
        "ts,td->sd", tok_match, grad_in, preferred_element_type=jnp.float32
    ).astype(jnp.bfloat16)
    input_slots = jnp.einsum(
        "ts,td->sd", tok_match, inputs, preferred_element_type=jnp.float32
    ).astype(jnp.bfloat16)
    grad_halves = grad_slots.reshape(experts_win, 2, half_cap, width)
    input_halves = input_slots.reshape(experts_win, 2, half_cap, width)

    def copies_of(halves):
        return jnp.broadcast_to(halves[:, None], (experts_win, groups, 2, half_cap, width)).reshape(
            dev_count, half_cap, width
        )

    recv_grad, recv_input = (
        lax.all_to_all(copies_of(grad_halves), "ep", split_axis=0, concat_axis=0, tiled=True),
        lax.all_to_all(copies_of(input_halves), "ep", split_axis=0, concat_axis=0, tiled=True),
    )
    grad_rows = recv_grad.reshape(dev_count * half_cap, width)
    input_rows = recv_input.reshape(dev_count * half_cap, width)
    partial_value, slot_weight = expert_grad(grad_rows, input_rows, gate_rows, up_rows, down_rows)
    back_part, back_weight = (
        lax.all_to_all(
            partial_value.reshape(dev_count, half_cap, width),
            "ep",
            split_axis=0,
            concat_axis=0,
            tiled=True,
        ),
        lax.all_to_all(
            slot_weight.reshape(dev_count, half_cap), "ep", split_axis=0, concat_axis=0, tiled=True
        ),
    )
    slot_grads = (
        back_part.reshape(experts_win, groups, 2, half_cap, width)
        .sum(axis=1)
        .reshape(slot_total, width)
    )
    slot_weights = (
        back_weight.reshape(experts_win, groups, 2, half_cap).sum(axis=1).reshape(slot_total)
    )
    weighted = jnp.sum(match_three * route_weight[0][:, :, None], axis=1)
    mixed = jnp.dot(
        weighted, slot_grads, precision=lax.Precision.HIGHEST, preferred_element_type=jnp.float32
    )
    grad_out = (grad_in.astype(jnp.float32) + mixed).astype(jnp.bfloat16)
    weight_out = jnp.dot(
        match, slot_weights, precision=lax.Precision.HIGHEST, preferred_element_type=jnp.float32
    )
    weight_out = weight_out.reshape(token_count, TOP)
    sent_back = passed_along(grad_out[None], "pp", -1)
    return (sent_back, weight_out[None])


def near_call(kernel, out_shape, *args, **kwargs):
    if "in_specs" not in kwargs:
        args = [pltpu.with_memory_space_constraint(arg, pltpu.VMEM) for arg in args]
    params = pltpu.CompilerParams(vmem_limit_bytes=16 * 1024 * 1024)
    return pl.pallas_call(kernel, out_shape=out_shape, compiler_params=params, **kwargs)(*args)


def as_bf16(mask):
    return mask.astype(F32).astype(BF16)


def slot_of_token(routes_t):
    count = routes_t.shape[1]
    hit = routes_t == 0
    found = jnp.max(hit.astype(F32), axis=0, keepdims=True)
    found = jnp.broadcast_to(found, (MAIN, count))
    before = lax.broadcasted_iota(jnp.int32, (count, count), 0) < lax.broadcasted_iota(
        jnp.int32, (count, count), 1
    )
    rank = jnp.dot(found.astype(BF16), as_bf16(before), preferred_element_type=F32)
    slot = jnp.where((found > 0.5) & (rank < CAP - 0.5), rank, -1.0)
    return hit, slot


def main_pick(slot):
    row = lax.broadcasted_iota(jnp.int32, slot.shape, 0).astype(F32)
    return slot == row


def tail_pick(slot, fold):
    row = lax.broadcasted_iota(jnp.int32, slot.shape, 0)
    want = (row + (MAIN - TAIL * fold)).astype(F32)
    inside = (row >= TAIL * fold) & (row < TAIL * fold + TAIL)
    return (slot == want) & inside


def both_picks(slot, fold):
    picks = [main_pick(slot).astype(F32), tail_pick(slot, fold).astype(F32)]
    return jnp.concatenate(picks, axis=0).astype(BF16)


def three_parts(value):
    high = value.astype(BF16)
    rest = value - high.astype(F32)
    mid = rest.astype(BF16)
    low = (rest - mid.astype(F32)).astype(BF16)
    return [part.astype(F32) for part in (high, mid, low)]


def pick_into(slot, rows_ref, out_ref, before=lambda fold: None):
    width = rows_ref.shape[1]
    part = width // FOLDS
    tail = jnp.zeros((MAIN, part), F32)
    for fold in range(FOLDS):
        before(fold)
        span = slice(fold * part, (fold + 1) * part)
        got = jnp.dot(both_picks(slot, fold), rows_ref[:, span], preferred_element_type=F32)
        out_ref[:, span] = got[:MAIN].astype(BF16)
        tail = tail + got[MAIN:]
    out_ref[:, width:] = tail.astype(BF16)


def pick_inputs_kernel(
    routes_in, weight_in, rows_in, base_in, out_ref, slot_ref, weight_ref, base_ref, routes_ref, rows_ref, sems
):
    part = rows_ref.shape[1] // FOLDS
    routes_copy = pltpu.make_async_copy(routes_in, routes_ref, sems.at[2 * FOLDS])
    routes_copy.start()
    weight_copy = pltpu.make_async_copy(weight_in, weight_ref, sems.at[2 * FOLDS + 1])
    weight_copy.start()
    copies = []
    for fold in range(FOLDS):
        span = slice(fold * part, (fold + 1) * part)
        copies.append(
            pltpu.make_async_copy(rows_in.at[:, span], rows_ref.at[:, span], sems.at[fold])
        )
        copies[-1].start()
    base_copies = []
    for fold in range(FOLDS):
        span = slice(fold * part, (fold + 1) * part)
        base_copies.append(
            pltpu.make_async_copy(
                base_in.at[:, span], base_ref.at[:, span], sems.at[FOLDS + fold]
            )
        )
        base_copies[-1].start()
    routes_copy.wait()
    hit, slot = slot_of_token(routes_ref[...])
    slot_ref[...] = jnp.where(hit, slot, -1.0)
    pick_into(slot, rows_ref, out_ref, lambda fold: copies[fold].wait())
    weight_copy.wait()
    for copy in base_copies:
        copy.wait()


def pick_grads_kernel(routes_ref, rows_ref, weight_ref, out_ref, with_ref):
    full = out_ref.shape[1]
    _, slot = slot_of_token(routes_ref[...])
    pick_into(slot, rows_ref, out_ref)
    with_ref[:, :full] = out_ref[...]
    for k, piece in enumerate(three_parts(weight_ref[...])):
        with_ref[:, full + 128 * k : full + 128 * (k + 1)] = piece.astype(BF16)


TN = (((0,), (0,)), ((), ()))
NT = (((1,), (1,)), ((), ()))


def back_kernel(routes_ref, with_ref, back_ref, scale_ref):
    hit, slot = slot_of_token(routes_ref[...])
    size = 2 * MAIN
    eye = as_bf16(
        lax.broadcasted_iota(jnp.int32, (size, 2 * size), 0)
        == lax.broadcasted_iota(jnp.int32, (size, 2 * size), 1) % size
    )
    for fold in range(FOLDS):
        back_ref[fold] = lax.dot_general(
            both_picks(slot, fold), eye, TN, preferred_element_type=F32
        ).astype(BF16)
    weight = jnp.zeros(hit.shape, F32)
    for k in range(3, 0, -1):
        start = with_ref.shape[1] - 128 * k
        weight = weight + with_ref[:, start : start + 128].astype(F32)
    weight_row = jnp.sum(jnp.where(hit, weight, 0.0), axis=0, keepdims=True)
    main = jnp.sum(jnp.where(main_pick(slot), weight_row, 0.0), axis=1, keepdims=True)
    tail = jnp.zeros_like(main)
    for fold in range(FOLDS):
        tail = tail + jnp.sum(
            jnp.where(tail_pick(slot, fold), weight_row, 0.0), axis=1, keepdims=True
        )
    scale_ref[:, :128] = jnp.broadcast_to(main, (MAIN, 128))
    scale_ref[:, 128:] = jnp.broadcast_to(tail, (MAIN, 128))


def against(blocks, weights_ref, rows_ref):
    width = weights_ref.shape[1]
    part = width // FOLDS
    count = MAIN * len(blocks)
    for k, block in enumerate(blocks):
        rows_ref[MAIN * k : MAIN * (k + 1), :] = block[:, :width]
        rows_ref[count + MAIN * k : count + MAIN * (k + 1), :part] = block[:, width : width + part]
    tails = rows_ref[count:, :part]
    quarter = lax.broadcasted_iota(jnp.int32, (count, weights_ref.shape[0]), 0) % MAIN // TAIL
    main = tail = None
    for fold in range(FOLDS):
        span = slice(fold * part, (fold + 1) * part)
        rows = jnp.concatenate([rows_ref[:count, span], tails], axis=0)
        got = lax.dot_general(rows, weights_ref[:, span], NT, preferred_element_type=F32)
        here = jnp.where(quarter == fold, got[count:], 0.0)
        main = got[:count] if fold == 0 else main + got[:count]
        tail = here if fold == 0 else tail + here
    tail = tail.reshape(len(blocks), MAIN, -1)
    turn = TAIL
    while turn < MAIN:
        tail = tail + pltpu.roll(tail, turn, 1)
        turn *= 2
    return jnp.concatenate([main, tail.reshape(count, -1)], axis=0)


def forward_kernel(own, z2, y_refs, low, high, gu_ref, h_ref, rows_ref):
    blocks = [own, low.at[0], z2, low.at[1], y_refs.at[0], high.at[0], y_refs.at[1], high.at[1]]
    h_ref[...] = against(blocks, gu_ref, rows_ref)


def backward_kernel(*refs):
    g0, g2, z_refs, y_refs, yz_refs, down_ref, gu_ref, h_ref, *outs, rows_ref = refs
    near_a, far_a, near_b, far_b = outs
    half = gu_ref.shape[1] // 2
    part = half // FOLDS
    units = down_ref.shape[0]
    blocks = [g0, z_refs.at[0], g2, z_refs.at[1]]
    blocks += [y_refs.at[0], yz_refs.at[0], y_refs.at[1], yz_refs.at[1]]
    count = MAIN * len(blocks)
    grad_hidden = against(blocks, down_ref, rows_ref)
    gate = h_ref[:, :units]
    up = h_ref[:, units:]
    sigmoid = 1.0 / (1.0 + jnp.exp(-gate))
    swish = gate * sigmoid
    grad_up = (grad_hidden * swish).astype(BF16)
    grad_gate = (grad_hidden * up * sigmoid * (1.0 + gate * (1.0 - sigmoid))).astype(BF16)
    both = jnp.concatenate([grad_gate, grad_up], axis=1)
    place_a = [(ref, k) for ref in (near_a, far_a) for k in range(4)]
    place_b = [((near_b, far_b)[k % 2], k // 2) for k in range(8)]
    quarter = lax.broadcasted_iota(jnp.int32, (count, part), 0) % MAIN // TAIL
    for side, places in enumerate((place_a, place_b)):
        tails = None
        for fold in range(FOLDS):
            start = side * half + fold * part
            value = jnp.dot(both, gu_ref[:, start : start + part], preferred_element_type=F32)
            here = jnp.where(quarter == fold, value[count:], 0.0)
            tails = here if fold == 0 else tails + here
            value = value[:count].astype(BF16)
            for k, (ref, j) in enumerate(places):
                ref[j, :, fold * part : (fold + 1) * part] = value[MAIN * k : MAIN * (k + 1), :]
        tails = tails.astype(BF16)
        for k, (ref, j) in enumerate(places):
            ref[j, :, half : half + part] = tails[MAIN * k : MAIN * (k + 1), :]
    weight = jnp.sum(grad_hidden * (swish * up), axis=1, keepdims=True)
    lane = lax.broadcasted_iota(jnp.int32, (count, 128), 1)
    first = lax.broadcasted_iota(jnp.int32, (count, 128), 0) % MAIN < TAIL
    tile = jnp.zeros((count, 128), F32)
    for k, piece in enumerate(three_parts(weight)):
        tile = jnp.where(lane == k, piece[:count], tile)
        tile = jnp.where((lane == k + 3) & first, piece[count:], tile)
    tile = tile.astype(BF16)
    for k, (ref, j) in enumerate(place_a):
        ref[j, :, half + part :] = tile[MAIN * k : MAIN * (k + 1), :]


def added(one, two):
    return (one.astype(F32) + two.astype(F32)).astype(BF16)


def fold_a_kernel(near_ref, got_ref, send_ref, keep_ref):
    full = near_ref.shape[2] - 128
    for k in range(near_ref.shape[0]):
        ref = (keep_ref, send_ref)[k % 2]
        ref[k // 2, :, :full] = added(near_ref[k, :, :full], got_ref[k, :, :full])
        ref[k // 2, :, full : full + 128] = near_ref[k, :, full:]
        ref[k // 2, :, full + 128 :] = got_ref[k, :, full:]


def fold_b_kernel(near_ref, got_ref, send_ref, keep_ref):
    for k in range(near_ref.shape[0]):
        ref = (keep_ref, send_ref)[k // 2]
        ref[k % 2] = added(near_ref[k], got_ref[k])


def fold_both_kernel(keep_a, got_a, keep_b, got_b, own_ref, send_ref, own_tile, send_tile):
    full = keep_b.shape[2]
    for k, (ref, tile_ref) in enumerate(((own_ref, own_tile), (send_ref, send_tile))):
        ref[:, :full] = added(keep_a[k, :, :full], got_a[k, :, :full])
        ref[:, full:] = added(keep_b[k], got_b[k])
        tile = jnp.zeros((MAIN, 128), F32)
        for source in (keep_a, got_a):
            for start in (full, full + 128):
                tile = tile + source[k, :, start : start + 128].astype(F32)
        tile_ref[...] = tile


def weight_kernel(slot_ref, own_tile, got_tile, after_ref, out_ref):
    tile = own_tile[...] + got_tile[...] + after_ref[...]
    lane = lax.broadcasted_iota(jnp.int32, tile.shape, 1)
    main = jnp.sum(jnp.where(lane < 3, tile, 0.0), axis=1, keepdims=True)
    tail = jnp.sum(jnp.where((lane >= 3) & (lane < 6), tile, 0.0), axis=1, keepdims=True)
    table = slot_ref[...]
    slot = jnp.broadcast_to(jnp.max(table, axis=0, keepdims=True), table.shape)
    row = lax.broadcasted_iota(jnp.int32, slot.shape, 0).astype(F32)
    value = jnp.sum(
        jnp.where(slot == row, main, 0.0) + jnp.where((slot == row + MAIN) & (row < TAIL), tail, 0.0),
        axis=0,
        keepdims=True,
    )
    out_ref[...] = jnp.where(table >= 0.0, value, 0.0)


def final_kernel(back_ref, scale_ref, one_ref, two_ref, base_ref, out_ref, end_ref, done_ref, sems):
    end_ref[...] = jnp.zeros_like(end_ref)
    width = base_ref.shape[1]
    half = width // 2
    part = half // FOLDS
    copies = []
    for side in range(2):
        first = side * (half + part)
        for fold in range(FOLDS):
            rows = []
            for lane, start in ((0, first + fold * part), (128, first + half)):
                total = one_ref[:, start : start + part].astype(F32)
                total = total + two_ref[:, start : start + part].astype(F32)
                rows.append(total * scale_ref[:, lane : lane + 1])
            rows = jnp.concatenate(rows, axis=0)
            high = rows.astype(BF16)
            low = (rows - high.astype(F32)).astype(BF16)
            rows = jnp.concatenate([high, low], axis=0)
            mixed = jnp.dot(back_ref[fold], rows, preferred_element_type=F32)
            start = side * half + fold * part
            span = slice(start, start + part)
            done_ref[:, span] = (base_ref[:, span].astype(F32) + mixed).astype(BF16)
            if fold % 2:
                span = slice(start - part, start + part)
                copy = pltpu.make_async_copy(
                    done_ref.at[:, span], out_ref.at[:, span], sems.at[len(copies)]
                )
                copy.start()
                copies.append(copy)
    for copy in copies:
        copy.wait()


def across(value, bits):
    count = lax.axis_size("ep")
    return lax.ppermute(value, "ep", [(i, i ^ bits) for i in range(count)])


def sections_across(value, bits):
    count = lax.axis_size("ep")
    pairs = [(s * count + i, (1 - s) * count + (i ^ bits)) for s in range(2) for i in range(count)]
    return lax.ppermute(value, ("pp", "ep"), pairs)


Y1, Z1, Z2 = 2, 4, 8


def single_device(upstream, saved, routes, route_weight, w_gate, w_up, w_down):
    routes_t = routes[0].T
    weight_t = route_weight[0].T
    next_routes = passed_along(routes_t, "pp", 1)
    count, width = saved.shape[1:]
    full = width + width // FOLDS
    half = full // 2
    units = 2 * w_gate.shape[1]
    slots = SHARDS // 2 * 2 * MAIN
    hbm = pl.BlockSpec(memory_space=pltpu.HBM)
    tile = pltpu.VMEM((MAIN, 128), F32)

    input_block, slot_table, near_weight, base = near_call(
        pick_inputs_kernel,
        [
            pltpu.VMEM((MAIN, full), BF16),
            pltpu.VMEM(routes_t.shape, F32),
            pltpu.VMEM(weight_t.shape, F32),
            pltpu.VMEM((count, width), BF16),
        ],
        *(
            pltpu.with_memory_space_constraint(v, pltpu.HBM)
            for v in (routes_t, weight_t, saved[0], upstream[0])
        ),
        in_specs=[hbm] * 4,
        scratch_shapes=[
            pltpu.VMEM(routes_t.shape, jnp.int32),
            pltpu.VMEM((count, width), BF16),
            pltpu.SemaphoreType.DMA((2 * FOLDS + 2,)),
        ],
        name="pick_inputs",
    )
    grad_block, grad_with = near_call(
        pick_grads_kernel,
        [pltpu.VMEM((MAIN, full), BF16), pltpu.VMEM((MAIN, full + 384), BF16)],
        next_routes,
        base,
        near_weight,
        name="pick_grads",
    )

    grad_z2 = sections_across(grad_block, Z2)
    grad_z0 = sections_across(grad_with, 0)
    input_z2 = across(input_block, Z2)
    own = jnp.stack([w_gate[0], w_up[0], w_down[0]])
    own, _ = lax.optimization_barrier((own, input_z2))
    other = across(own, 1)
    gate_up = jnp.concatenate([own[0], other[0], own[1], other[1]], axis=0)
    down = jnp.concatenate([own[2], other[2]], axis=0)

    grad_z = jnp.stack([grad_z0[:, :full], grad_z2])
    grad_z1 = across(grad_z, Z1)
    grad_y = across(grad_z, Y1)
    input_z = jnp.stack([input_block, input_z2])
    input_y = across(input_z, Y1)
    input_low = across(input_z, Z1)
    input_high = across(input_y, Z1)
    grad_yz1 = across(grad_z1, Y1)

    late_routes, late_with, _ = lax.optimization_barrier((next_routes, grad_z0, grad_z1))
    back, scale = near_call(
        back_kernel,
        [pltpu.VMEM((FOLDS, count, 4 * MAIN), BF16), pltpu.VMEM((MAIN, 256), F32)],
        late_routes,
        late_with,
        name="back_rows",
    )
    input_high, back, scale = lax.optimization_barrier((input_high, back, scale))
    hidden = near_call(
        forward_kernel,
        pltpu.VMEM((slots, 2 * units), F32),
        input_block,
        input_z2,
        input_y,
        input_low,
        input_high,
        gate_up,
        scratch_shapes=[pltpu.VMEM((slots, width), BF16)],
        name="expert_forward",
    )
    side_a = pltpu.VMEM((4, MAIN, half + 128), BF16)
    side_b = pltpu.VMEM((4, MAIN, half), BF16)
    near_a, far_a, near_b, far_b = near_call(
        backward_kernel,
        [side_a, side_a, side_b, side_b],
        grad_z0,
        grad_z2,
        grad_z1,
        grad_y,
        grad_yz1,
        down,
        gate_up,
        hidden,
        scratch_shapes=[pltpu.VMEM((slots, width), BF16)],
        name="expert_backward",
    )
    got_a = across(far_a, Y1)
    got_b = across(far_b, Z1)
    send_a, keep_a = near_call(
        fold_a_kernel, [pltpu.VMEM((2, MAIN, half + 256), BF16)] * 2, near_a, got_a, name="fold_a"
    )
    send_b, keep_b = near_call(
        fold_b_kernel, [pltpu.VMEM((2, MAIN, half), BF16)] * 2, near_b, got_b, name="fold_b"
    )
    rows_0, rows_2, tile_0, tile_2 = near_call(
        fold_both_kernel,
        [pltpu.VMEM((MAIN, full), BF16)] * 2 + [tile] * 2,
        keep_a,
        across(send_a, Z1),
        keep_b,
        across(send_b, Y1),
        name="fold_both",
    )
    got_2 = sections_across(rows_2, Z2)
    got_0 = sections_across(rows_0, 0)
    grad_prev, end = near_call(
        final_kernel,
        [jax.ShapeDtypeStruct((count, width), BF16), tile],
        back,
        scale,
        got_0,
        got_2,
        base,
        out_specs=[hbm, pl.BlockSpec(memory_space=pltpu.VMEM)],
        scratch_shapes=[pltpu.VMEM((count, width), BF16), pltpu.SemaphoreType.DMA((FOLDS,))],
        name="final_rows",
    )
    weight_out = near_call(
        weight_kernel,
        jax.ShapeDtypeStruct((TOP, count), F32),
        slot_table,
        tile_0,
        across(tile_2, Z2),
        end,
        name="weight_out",
    )
    return (grad_prev[None], weight_out.T[None])


def solution(mesh):
    single = mesh.shape["ep"] == SHARDS and mesh.shape["pp"] == 2
    spec = P("pp", "ep", None)
    return jax.shard_map(
        single_device if single else general_device,
        mesh=mesh,
        in_specs=(spec,) * 7,
        out_specs=(spec, spec),
        check_vma=False,
    )
```

```python
import functools

import jax
import jax.numpy as jnp
from jax import lax
from jax.experimental import pallas as pl
from jax.experimental.pallas import tpu as pltpu
from jax.sharding import PartitionSpec as P

TOP = 8
SHARDS = 16
CAP = 10
MAIN = 8
TAIL = CAP - MAIN
FOLDS = MAIN // TAIL
F32 = jnp.float32
BF16 = jnp.bfloat16


def from_partner(block, axis, apart):
    count = lax.axis_size(axis)
    route = []
    for low in range(count):
        high = low | 1 << apart
        if high != low and high < count:
            route += [(low, high), (high, low)]
    return lax.ppermute(block, axis, route)


def passed_along(value, axis, by):
    size = lax.axis_size(axis)
    return lax.ppermute(value, axis, [(i, (i + by) % size) for i in range(size)])


def route_match(block_routes, experts_win):
    flat_routes = block_routes.reshape(-1)
    onehot = (flat_routes[:, None] == jnp.arange(experts_win, dtype=jnp.int32)[None, :]).astype(
        jnp.int32
    )
    earlier = jnp.cumsum(onehot, axis=0) - onehot
    ranking = jnp.sum(earlier * onehot, axis=1)
    kept = (flat_routes < experts_win) & (ranking < CAP)
    slot_index = flat_routes * CAP + ranking
    match = (slot_index[:, None] == jnp.arange(experts_win * CAP, dtype=jnp.int32)[None, :]) & kept[
        :, None
    ]
    return match.astype(jnp.float32)


def expert_grad(grad_rows, input_rows, gate_rows, up_rows, down_rows):
    contract = (((1,), (1,)), ((), ()))
    gate = lax.dot_general(input_rows, gate_rows, contract, preferred_element_type=jnp.float32)
    up_proj = lax.dot_general(input_rows, up_rows, contract, preferred_element_type=jnp.float32)
    grad_hidden = lax.dot_general(
        grad_rows, down_rows, contract, preferred_element_type=jnp.float32
    )
    sigmoid = jax.nn.sigmoid(gate)
    swish = gate * sigmoid
    hidden = swish * up_proj
    slot_weight = jnp.sum(grad_hidden * hidden, axis=1)
    grad_up = (grad_hidden * swish).astype(jnp.bfloat16)
    grad_gate = (grad_hidden * up_proj * sigmoid * (1.0 + gate * (1.0 - sigmoid))).astype(
        jnp.bfloat16
    )
    partial_value = jnp.dot(grad_gate, gate_rows, preferred_element_type=jnp.float32)
    partial_value = partial_value + jnp.dot(grad_up, up_rows, preferred_element_type=jnp.float32)
    return (partial_value, slot_weight)


def pair_rows(mine, other, pair_low):
    return jnp.where(
        pair_low, jnp.concatenate([mine, other], axis=0), jnp.concatenate([other, mine], axis=0)
    )


def general_device(upstream, saved, routes, route_weight, w_gate, w_up, w_down):
    shards = SHARDS
    groups = shards // 2
    experts_win = lax.axis_size("ep") // shards
    dev_count = experts_win * shards
    my_index = lax.axis_index("ep")
    half_cap = CAP // 2
    pair_low = my_index % 2 == 0
    other_gate, other_up, other_down = from_partner((w_gate[0], w_up[0], w_down[0]), "ep", 0)
    gate_rows = pair_rows(w_gate[0], other_gate, pair_low)
    up_rows = pair_rows(w_up[0], other_up, pair_low)
    down_rows = pair_rows(w_down[0], other_down, pair_low)
    grad_in = passed_along(upstream, "pp", -1)[0]
    inputs = saved[0]
    token_count, width = inputs.shape
    slot_total = experts_win * CAP
    match = route_match(routes[0], experts_win)
    match_three = match.reshape(token_count, TOP, slot_total)
    tok_match = match_three.sum(axis=1).astype(jnp.bfloat16)
    grad_slots = jnp.einsum(
        "ts,td->sd", tok_match, grad_in, preferred_element_type=jnp.float32
    ).astype(jnp.bfloat16)
    input_slots = jnp.einsum(
        "ts,td->sd", tok_match, inputs, preferred_element_type=jnp.float32
    ).astype(jnp.bfloat16)
    grad_halves = grad_slots.reshape(experts_win, 2, half_cap, width)
    input_halves = input_slots.reshape(experts_win, 2, half_cap, width)

    def copies_of(halves):
        return jnp.broadcast_to(halves[:, None], (experts_win, groups, 2, half_cap, width)).reshape(
            dev_count, half_cap, width
        )

    recv_grad, recv_input = (
        lax.all_to_all(copies_of(grad_halves), "ep", split_axis=0, concat_axis=0, tiled=True),
        lax.all_to_all(copies_of(input_halves), "ep", split_axis=0, concat_axis=0, tiled=True),
    )
    grad_rows = recv_grad.reshape(dev_count * half_cap, width)
    input_rows = recv_input.reshape(dev_count * half_cap, width)
    partial_value, slot_weight = expert_grad(grad_rows, input_rows, gate_rows, up_rows, down_rows)
    back_part, back_weight = (
        lax.all_to_all(
            partial_value.reshape(dev_count, half_cap, width),
            "ep",
            split_axis=0,
            concat_axis=0,
            tiled=True,
        ),
        lax.all_to_all(
            slot_weight.reshape(dev_count, half_cap), "ep", split_axis=0, concat_axis=0, tiled=True
        ),
    )
    slot_grads = (
        back_part.reshape(experts_win, groups, 2, half_cap, width)
        .sum(axis=1)
        .reshape(slot_total, width)
    )
    slot_weights = (
        back_weight.reshape(experts_win, groups, 2, half_cap).sum(axis=1).reshape(slot_total)
    )
    weighted = jnp.sum(match_three * route_weight[0][:, :, None], axis=1)
    mixed = jnp.dot(
        weighted, slot_grads, precision=lax.Precision.HIGHEST, preferred_element_type=jnp.float32
    )
    grad_out = (grad_in.astype(jnp.float32) + mixed).astype(jnp.bfloat16)
    weight_out = jnp.dot(
        match, slot_weights, precision=lax.Precision.HIGHEST, preferred_element_type=jnp.float32
    )
    weight_out = weight_out.reshape(token_count, TOP)
    sent_back = passed_along(grad_out[None], "pp", -1)
    return (sent_back, weight_out[None])


def near_call(kernel, out_shape, *args, **kwargs):
    if "in_specs" not in kwargs:
        args = [pltpu.with_memory_space_constraint(arg, pltpu.VMEM) for arg in args]
    params = pltpu.CompilerParams(vmem_limit_bytes=16 * 1024 * 1024)
    return pl.pallas_call(kernel, out_shape=out_shape, compiler_params=params, **kwargs)(*args)


def as_bf16(mask):
    return mask.astype(F32).astype(BF16)


def slot_of_token(routes_t):
    count = routes_t.shape[1]
    hit = routes_t == 0
    found = jnp.max(hit.astype(F32), axis=0, keepdims=True)
    found = jnp.broadcast_to(found, (MAIN, count))
    before = lax.broadcasted_iota(jnp.int32, (count, count), 0) < lax.broadcasted_iota(
        jnp.int32, (count, count), 1
    )
    rank = jnp.dot(found.astype(BF16), as_bf16(before), preferred_element_type=F32)
    slot = jnp.where((found > 0.5) & (rank < CAP - 0.5), rank, -1.0)
    return hit, slot


def main_pick(slot):
    row = lax.broadcasted_iota(jnp.int32, slot.shape, 0).astype(F32)
    return slot == row


def tail_pick(slot, fold):
    row = lax.broadcasted_iota(jnp.int32, slot.shape, 0)
    want = (row + (MAIN - TAIL * fold)).astype(F32)
    inside = (row >= TAIL * fold) & (row < TAIL * fold + TAIL)
    return (slot == want) & inside


def both_picks(slot, fold):
    picks = [main_pick(slot).astype(F32), tail_pick(slot, fold).astype(F32)]
    return jnp.concatenate(picks, axis=0).astype(BF16)


def three_parts(value):
    high = value.astype(BF16)
    rest = value - high.astype(F32)
    mid = rest.astype(BF16)
    low = (rest - mid.astype(F32)).astype(BF16)
    return [part.astype(F32) for part in (high, mid, low)]


def pick_into(slot, rows_ref, out_ref, before=lambda fold: None):
    width = rows_ref.shape[1]
    part = width // FOLDS
    tail = jnp.zeros((MAIN, part), F32)
    for fold in range(FOLDS):
        before(fold)
        span = slice(fold * part, (fold + 1) * part)
        got = jnp.dot(both_picks(slot, fold), rows_ref[:, span], preferred_element_type=F32)
        out_ref[:, span] = got[:MAIN].astype(BF16)
        tail = tail + got[MAIN:]
    out_ref[:, width:] = tail.astype(BF16)


def pick_inputs_kernel(
    routes_in, weight_in, rows_in, base_in, out_ref, slot_ref, weight_ref, base_ref, routes_ref, rows_ref, sems
):
    part = rows_ref.shape[1] // FOLDS
    routes_copy = pltpu.make_async_copy(routes_in, routes_ref, sems.at[2 * FOLDS])
    routes_copy.start()
    weight_copy = pltpu.make_async_copy(weight_in, weight_ref, sems.at[2 * FOLDS + 1])
    weight_copy.start()
    copies = []
    for fold in range(FOLDS):
        span = slice(fold * part, (fold + 1) * part)
        copies.append(
            pltpu.make_async_copy(rows_in.at[:, span], rows_ref.at[:, span], sems.at[fold])
        )
        copies[-1].start()
    base_copies = []
    for fold in range(FOLDS):
        span = slice(fold * part, (fold + 1) * part)
        base_copies.append(
            pltpu.make_async_copy(
                base_in.at[:, span], base_ref.at[:, span], sems.at[FOLDS + fold]
            )
        )
        base_copies[-1].start()
    routes_copy.wait()
    hit, slot = slot_of_token(routes_ref[...])
    slot_ref[...] = jnp.where(hit, slot, -1.0)
    pick_into(slot, rows_ref, out_ref, lambda fold: copies[fold].wait())
    weight_copy.wait()
    for copy in base_copies:
        copy.wait()


def pick_grads_kernel(routes_ref, rows_ref, weight_ref, out_ref, with_ref):
    full = out_ref.shape[1]
    _, slot = slot_of_token(routes_ref[...])
    pick_into(slot, rows_ref, out_ref)
    with_ref[:, :full] = out_ref[...]
    for k, piece in enumerate(three_parts(weight_ref[...])):
        with_ref[:, full + 128 * k : full + 128 * (k + 1)] = piece.astype(BF16)


TN = (((0,), (0,)), ((), ()))
NT = (((1,), (1,)), ((), ()))


def back_kernel(routes_ref, with_ref, back_ref, scale_ref):
    hit, slot = slot_of_token(routes_ref[...])
    size = 2 * MAIN
    eye = as_bf16(
        lax.broadcasted_iota(jnp.int32, (size, 2 * size), 0)
        == lax.broadcasted_iota(jnp.int32, (size, 2 * size), 1) % size
    )
    for fold in range(FOLDS):
        back_ref[fold] = lax.dot_general(
            both_picks(slot, fold), eye, TN, preferred_element_type=F32
        ).astype(BF16)
    weight = jnp.zeros(hit.shape, F32)
    for k in range(3, 0, -1):
        start = with_ref.shape[1] - 128 * k
        weight = weight + with_ref[:, start : start + 128].astype(F32)
    weight_row = jnp.sum(jnp.where(hit, weight, 0.0), axis=0, keepdims=True)
    main = jnp.sum(jnp.where(main_pick(slot), weight_row, 0.0), axis=1, keepdims=True)
    tail = jnp.zeros_like(main)
    for fold in range(FOLDS):
        tail = tail + jnp.sum(
            jnp.where(tail_pick(slot, fold), weight_row, 0.0), axis=1, keepdims=True
        )
    scale_ref[:, :128] = jnp.broadcast_to(main, (MAIN, 128))
    scale_ref[:, 128:] = jnp.broadcast_to(tail, (MAIN, 128))


def against(blocks, weights_ref, rows_ref):
    width = weights_ref.shape[1]
    part = width // FOLDS
    count = MAIN * len(blocks)
    for k, block in enumerate(blocks):
        rows_ref[MAIN * k : MAIN * (k + 1), :] = block[:, :width]
        rows_ref[count + MAIN * k : count + MAIN * (k + 1), :part] = block[:, width : width + part]
    tails = rows_ref[count:, :part]
    quarter = lax.broadcasted_iota(jnp.int32, (count, weights_ref.shape[0]), 0) % MAIN // TAIL
    main = tail = None
    for fold in range(FOLDS):
        span = slice(fold * part, (fold + 1) * part)
        rows = jnp.concatenate([rows_ref[:count, span], tails], axis=0)
        got = lax.dot_general(rows, weights_ref[:, span], NT, preferred_element_type=F32)
        here = jnp.where(quarter == fold, got[count:], 0.0)
        main = got[:count] if fold == 0 else main + got[:count]
        tail = here if fold == 0 else tail + here
    tail = tail.reshape(len(blocks), MAIN, -1)
    turn = TAIL
    while turn < MAIN:
        tail = tail + pltpu.roll(tail, turn, 1)
        turn *= 2
    return jnp.concatenate([main, tail.reshape(count, -1)], axis=0)


def forward_kernel(own, z2, y_refs, low, high, gu_ref, h_ref, rows_ref):
    blocks = [own, low.at[0], z2, low.at[1], y_refs.at[0], high.at[0], y_refs.at[1], high.at[1]]
    h_ref[...] = against(blocks, gu_ref, rows_ref)


def spread(both, gu_ref, start, places):
    half = gu_ref.shape[1] // 2
    part = half // FOLDS
    count = MAIN * len(places)
    quarter = lax.broadcasted_iota(jnp.int32, (count, part), 0) % MAIN // TAIL
    tails = None
    for fold in range(FOLDS):
        span = slice(start + fold * part, start + (fold + 1) * part)
        value = jnp.dot(both, gu_ref[:, span], preferred_element_type=F32)
        here = jnp.where(quarter == fold, value[count:], 0.0)
        tails = here if fold == 0 else tails + here
        value = value[:count].astype(BF16)
        for k, (ref, j) in enumerate(places):
            ref[j, :, fold * part : (fold + 1) * part] = value[MAIN * k : MAIN * (k + 1), :]
    tails = tails.astype(BF16)
    for k, (ref, j) in enumerate(places):
        ref[j, :, half : half + part] = tails[MAIN * k : MAIN * (k + 1), :]


def backward_a_kernel(*refs):
    g0, g2, z_refs, y_refs, yz_refs, down_ref, gu_ref, h_ref, near, far, both_ref, rows_ref = refs
    units = down_ref.shape[0]
    blocks = [g0, z_refs.at[0], g2, z_refs.at[1]]
    blocks += [y_refs.at[0], yz_refs.at[0], y_refs.at[1], yz_refs.at[1]]
    count = MAIN * len(blocks)
    grad_hidden = against(blocks, down_ref, rows_ref)
    gate = h_ref[:, :units]
    up = h_ref[:, units:]
    sigmoid = 1.0 / (1.0 + jnp.exp(-gate))
    swish = gate * sigmoid
    grad_up = (grad_hidden * swish).astype(BF16)
    grad_gate = (grad_hidden * up * sigmoid * (1.0 + gate * (1.0 - sigmoid))).astype(BF16)
    both = jnp.concatenate([grad_gate, grad_up], axis=1)
    both_ref[...] = both
    places = [(ref, k) for ref in (near, far) for k in range(4)]
    spread(both, gu_ref, 0, places)
    weight = jnp.sum(grad_hidden * (swish * up), axis=1, keepdims=True)
    lane = lax.broadcasted_iota(jnp.int32, (count, 128), 1)
    first = lax.broadcasted_iota(jnp.int32, (count, 128), 0) % MAIN < TAIL
    tile = jnp.zeros((count, 128), F32)
    for k, piece in enumerate(three_parts(weight)):
        tile = jnp.where(lane == k, piece[:count], tile)
        tile = jnp.where((lane == k + 3) & first, piece[count:], tile)
    tile = tile.astype(BF16)
    full = near.shape[2] - 128
    for k, (ref, j) in enumerate(places):
        ref[j, :, full:] = tile[MAIN * k : MAIN * (k + 1), :]


def backward_b_kernel(both_ref, gu_ref, near, far):
    places = [((near, far)[k % 2], k // 2) for k in range(8)]
    spread(both_ref[...], gu_ref, gu_ref.shape[1] // 2, places)


def added(one, two):
    return (one.astype(F32) + two.astype(F32)).astype(BF16)


def fold_a_kernel(near_ref, got_ref, send_ref, keep_ref):
    full = near_ref.shape[2] - 128
    for k in range(near_ref.shape[0]):
        ref = (keep_ref, send_ref)[k % 2]
        ref[k // 2, :, :full] = added(near_ref[k, :, :full], got_ref[k, :, :full])
        ref[k // 2, :, full : full + 128] = near_ref[k, :, full:]
        ref[k // 2, :, full + 128 :] = got_ref[k, :, full:]


def fold_b_kernel(near_ref, got_ref, send_ref, keep_ref):
    for k in range(near_ref.shape[0]):
        ref = (keep_ref, send_ref)[k // 2]
        ref[k % 2] = added(near_ref[k], got_ref[k])


def fold_both_kernel(keep_a, got_a, keep_b, got_b, own_ref, send_ref, own_tile, send_tile):
    full = keep_b.shape[2]
    for k, (ref, tile_ref) in enumerate(((own_ref, own_tile), (send_ref, send_tile))):
        ref[:, :full] = added(keep_a[k, :, :full], got_a[k, :, :full])
        ref[:, full:] = added(keep_b[k], got_b[k])
        tile = jnp.zeros((MAIN, 128), F32)
        for source in (keep_a, got_a):
            for start in (full, full + 128):
                tile = tile + source[k, :, start : start + 128].astype(F32)
        tile_ref[...] = tile


def weight_kernel(slot_ref, own_tile, got_tile, after_ref, out_ref):
    tile = own_tile[...] + got_tile[...] + after_ref[...]
    lane = lax.broadcasted_iota(jnp.int32, tile.shape, 1)
    main = jnp.sum(jnp.where(lane < 3, tile, 0.0), axis=1, keepdims=True)
    tail = jnp.sum(jnp.where((lane >= 3) & (lane < 6), tile, 0.0), axis=1, keepdims=True)
    table = slot_ref[...]
    slot = jnp.broadcast_to(jnp.max(table, axis=0, keepdims=True), table.shape)
    row = lax.broadcasted_iota(jnp.int32, slot.shape, 0).astype(F32)
    value = jnp.sum(
        jnp.where(slot == row, main, 0.0) + jnp.where((slot == row + MAIN) & (row < TAIL), tail, 0.0),
        axis=0,
        keepdims=True,
    )
    out_ref[...] = jnp.where(table >= 0.0, value, 0.0)


def final_kernel(back_ref, scale_ref, one_ref, two_ref, base_ref, out_ref, end_ref, done_ref, sems):
    end_ref[...] = jnp.zeros_like(end_ref)
    width = base_ref.shape[1]
    half = width // 2
    part = half // FOLDS
    copies = []
    for side in range(2):
        first = side * (half + part)
        for fold in range(FOLDS):
            rows = []
            for lane, start in ((0, first + fold * part), (128, first + half)):
                total = one_ref[:, start : start + part].astype(F32)
                total = total + two_ref[:, start : start + part].astype(F32)
                rows.append(total * scale_ref[:, lane : lane + 1])
            rows = jnp.concatenate(rows, axis=0)
            high = rows.astype(BF16)
            low = (rows - high.astype(F32)).astype(BF16)
            rows = jnp.concatenate([high, low], axis=0)
            mixed = jnp.dot(back_ref[fold], rows, preferred_element_type=F32)
            start = side * half + fold * part
            span = slice(start, start + part)
            done_ref[:, span] = (base_ref[:, span].astype(F32) + mixed).astype(BF16)
            if fold % 2:
                span = slice(start - part, start + part)
                copy = pltpu.make_async_copy(
                    done_ref.at[:, span], out_ref.at[:, span], sems.at[len(copies)]
                )
                copy.start()
                copies.append(copy)
    for copy in copies:
        copy.wait()


def across(value, bits):
    count = lax.axis_size("ep")
    return lax.ppermute(value, "ep", [(i, i ^ bits) for i in range(count)])


def sections_across(value, bits):
    count = lax.axis_size("ep")
    pairs = [(s * count + i, (1 - s) * count + (i ^ bits)) for s in range(2) for i in range(count)]
    return lax.ppermute(value, ("pp", "ep"), pairs)


Y1, Z1, Z2 = 2, 4, 8


def single_device(upstream, saved, routes, route_weight, w_gate, w_up, w_down):
    routes_t = routes[0].T
    weight_t = route_weight[0].T
    next_routes = passed_along(routes_t, "pp", 1)
    count, width = saved.shape[1:]
    full = width + width // FOLDS
    half = full // 2
    units = 2 * w_gate.shape[1]
    slots = SHARDS // 2 * 2 * MAIN
    hbm = pl.BlockSpec(memory_space=pltpu.HBM)
    tile = pltpu.VMEM((MAIN, 128), F32)

    input_block, slot_table, near_weight, base = near_call(
        pick_inputs_kernel,
        [
            pltpu.VMEM((MAIN, full), BF16),
            pltpu.VMEM(routes_t.shape, F32),
            pltpu.VMEM(weight_t.shape, F32),
            pltpu.VMEM((count, width), BF16),
        ],
        *(
            pltpu.with_memory_space_constraint(v, pltpu.HBM)
            for v in (routes_t, weight_t, saved[0], upstream[0])
        ),
        in_specs=[hbm] * 4,
        scratch_shapes=[
            pltpu.VMEM(routes_t.shape, jnp.int32),
            pltpu.VMEM((count, width), BF16),
            pltpu.SemaphoreType.DMA((2 * FOLDS + 2,)),
        ],
        name="pick_inputs",
    )
    grad_block, grad_with = near_call(
        pick_grads_kernel,
        [pltpu.VMEM((MAIN, full), BF16), pltpu.VMEM((MAIN, full + 384), BF16)],
        next_routes,
        base,
        near_weight,
        name="pick_grads",
    )

    grad_z2 = sections_across(grad_block, Z2)
    grad_z0 = sections_across(grad_with, 0)
    input_z2 = across(input_block, Z2)
    own = jnp.stack([w_gate[0], w_up[0], w_down[0]])
    own, _ = lax.optimization_barrier((own, input_z2))
    other = across(own, 1)
    gate_up = jnp.concatenate([own[0], other[0], own[1], other[1]], axis=0)
    down = jnp.concatenate([own[2], other[2]], axis=0)

    grad_z = jnp.stack([grad_z0[:, :full], grad_z2])
    grad_z1 = across(grad_z, Z1)
    grad_y = across(grad_z, Y1)
    input_z = jnp.stack([input_block, input_z2])
    input_y = across(input_z, Y1)
    input_low = across(input_z, Z1)
    input_high = across(input_y, Z1)
    grad_z1, grad_y = lax.optimization_barrier((grad_z1, grad_y))
    grad_yz1 = across(grad_z1, Y1)

    late_routes, late_with, _ = lax.optimization_barrier((next_routes, grad_z0, grad_z1))
    back, scale = near_call(
        back_kernel,
        [pltpu.VMEM((FOLDS, count, 4 * MAIN), BF16), pltpu.VMEM((MAIN, 256), F32)],
        late_routes,
        late_with,
        name="back_rows",
    )
    input_high, back, scale = lax.optimization_barrier((input_high, back, scale))
    hidden = near_call(
        forward_kernel,
        pltpu.VMEM((slots, 2 * units), F32),
        input_block,
        input_z2,
        input_y,
        input_low,
        input_high,
        gate_up,
        scratch_shapes=[pltpu.VMEM((slots, width), BF16)],
        name="expert_forward",
    )
    side_a = pltpu.VMEM((4, MAIN, half + 128), BF16)
    side_b = pltpu.VMEM((4, MAIN, half), BF16)
    near_a, far_a, both = near_call(
        backward_a_kernel,
        [side_a, side_a, pltpu.VMEM((slots, 2 * units), BF16)],
        grad_z0,
        grad_z2,
        grad_z1,
        grad_y,
        grad_yz1,
        down,
        gate_up,
        hidden,
        scratch_shapes=[pltpu.VMEM((slots, width), BF16)],
        name="backward_a",
    )
    got_a = across(far_a, Y1)
    near_b, far_b = near_call(
        backward_b_kernel, [side_b, side_b], both, gate_up, name="backward_b"
    )
    got_b = across(far_b, Z1)
    send_a, keep_a = near_call(
        fold_a_kernel, [pltpu.VMEM((2, MAIN, half + 256), BF16)] * 2, near_a, got_a, name="fold_a"
    )
    send_b, keep_b = near_call(
        fold_b_kernel, [pltpu.VMEM((2, MAIN, half), BF16)] * 2, near_b, got_b, name="fold_b"
    )
    rows_0, rows_2, tile_0, tile_2 = near_call(
        fold_both_kernel,
        [pltpu.VMEM((MAIN, full), BF16)] * 2 + [tile] * 2,
        keep_a,
        across(send_a, Z1),
        keep_b,
        across(send_b, Y1),
        name="fold_both",
    )
    got_2 = sections_across(rows_2, Z2)
    got_0 = sections_across(rows_0, 0)
    grad_prev, end = near_call(
        final_kernel,
        [jax.ShapeDtypeStruct((count, width), BF16), tile],
        back,
        scale,
        got_2,
        got_0,
        base,
        out_specs=[hbm, pl.BlockSpec(memory_space=pltpu.VMEM)],
        scratch_shapes=[pltpu.VMEM((count, width), BF16), pltpu.SemaphoreType.DMA((FOLDS,))],
        name="final_rows",
    )
    weight_out = near_call(
        weight_kernel,
        jax.ShapeDtypeStruct((TOP, count), F32),
        slot_table,
        tile_0,
        across(tile_2, Z2),
        end,
        name="weight_out",
    )
    return (grad_prev[None], weight_out.T[None])


def solution(mesh):
    single = mesh.shape["ep"] == SHARDS and mesh.shape["pp"] == 2
    spec = P("pp", "ep", None)
    return jax.shard_map(
        single_device if single else general_device,
        mesh=mesh,
        in_specs=(spec,) * 7,
        out_specs=(spec, spec),
        check_vma=False,
    )
```

```python
import functools

import jax
import jax.numpy as jnp
from jax import lax
from jax.experimental import pallas as pl
from jax.experimental.pallas import tpu as pltpu
from jax.sharding import PartitionSpec as P

TOP = 8
SHARDS = 16
CAP = 10
MAIN = 8
TAIL = CAP - MAIN
FOLDS = MAIN // TAIL
F32 = jnp.float32
BF16 = jnp.bfloat16


def from_partner(block, axis, apart):
    count = lax.axis_size(axis)
    route = []
    for low in range(count):
        high = low | 1 << apart
        if high != low and high < count:
            route += [(low, high), (high, low)]
    return lax.ppermute(block, axis, route)


def passed_along(value, axis, by):
    size = lax.axis_size(axis)
    return lax.ppermute(value, axis, [(i, (i + by) % size) for i in range(size)])


def route_match(block_routes, experts_win):
    flat_routes = block_routes.reshape(-1)
    onehot = (flat_routes[:, None] == jnp.arange(experts_win, dtype=jnp.int32)[None, :]).astype(
        jnp.int32
    )
    earlier = jnp.cumsum(onehot, axis=0) - onehot
    ranking = jnp.sum(earlier * onehot, axis=1)
    kept = (flat_routes < experts_win) & (ranking < CAP)
    slot_index = flat_routes * CAP + ranking
    match = (slot_index[:, None] == jnp.arange(experts_win * CAP, dtype=jnp.int32)[None, :]) & kept[
        :, None
    ]
    return match.astype(jnp.float32)


def expert_grad(grad_rows, input_rows, gate_rows, up_rows, down_rows):
    contract = (((1,), (1,)), ((), ()))
    gate = lax.dot_general(input_rows, gate_rows, contract, preferred_element_type=jnp.float32)
    up_proj = lax.dot_general(input_rows, up_rows, contract, preferred_element_type=jnp.float32)
    grad_hidden = lax.dot_general(
        grad_rows, down_rows, contract, preferred_element_type=jnp.float32
    )
    sigmoid = jax.nn.sigmoid(gate)
    swish = gate * sigmoid
    hidden = swish * up_proj
    slot_weight = jnp.sum(grad_hidden * hidden, axis=1)
    grad_up = (grad_hidden * swish).astype(jnp.bfloat16)
    grad_gate = (grad_hidden * up_proj * sigmoid * (1.0 + gate * (1.0 - sigmoid))).astype(
        jnp.bfloat16
    )
    partial_value = jnp.dot(grad_gate, gate_rows, preferred_element_type=jnp.float32)
    partial_value = partial_value + jnp.dot(grad_up, up_rows, preferred_element_type=jnp.float32)
    return (partial_value, slot_weight)


def pair_rows(mine, other, pair_low):
    return jnp.where(
        pair_low, jnp.concatenate([mine, other], axis=0), jnp.concatenate([other, mine], axis=0)
    )


def general_device(upstream, saved, routes, route_weight, w_gate, w_up, w_down):
    shards = SHARDS
    groups = shards // 2
    experts_win = lax.axis_size("ep") // shards
    dev_count = experts_win * shards
    my_index = lax.axis_index("ep")
    half_cap = CAP // 2
    pair_low = my_index % 2 == 0
    other_gate, other_up, other_down = from_partner((w_gate[0], w_up[0], w_down[0]), "ep", 0)
    gate_rows = pair_rows(w_gate[0], other_gate, pair_low)
    up_rows = pair_rows(w_up[0], other_up, pair_low)
    down_rows = pair_rows(w_down[0], other_down, pair_low)
    grad_in = passed_along(upstream, "pp", -1)[0]
    inputs = saved[0]
    token_count, width = inputs.shape
    slot_total = experts_win * CAP
    match = route_match(routes[0], experts_win)
    match_three = match.reshape(token_count, TOP, slot_total)
    tok_match = match_three.sum(axis=1).astype(jnp.bfloat16)
    grad_slots = jnp.einsum(
        "ts,td->sd", tok_match, grad_in, preferred_element_type=jnp.float32
    ).astype(jnp.bfloat16)
    input_slots = jnp.einsum(
        "ts,td->sd", tok_match, inputs, preferred_element_type=jnp.float32
    ).astype(jnp.bfloat16)
    grad_halves = grad_slots.reshape(experts_win, 2, half_cap, width)
    input_halves = input_slots.reshape(experts_win, 2, half_cap, width)

    def copies_of(halves):
        return jnp.broadcast_to(halves[:, None], (experts_win, groups, 2, half_cap, width)).reshape(
            dev_count, half_cap, width
        )

    recv_grad, recv_input = (
        lax.all_to_all(copies_of(grad_halves), "ep", split_axis=0, concat_axis=0, tiled=True),
        lax.all_to_all(copies_of(input_halves), "ep", split_axis=0, concat_axis=0, tiled=True),
    )
    grad_rows = recv_grad.reshape(dev_count * half_cap, width)
    input_rows = recv_input.reshape(dev_count * half_cap, width)
    partial_value, slot_weight = expert_grad(grad_rows, input_rows, gate_rows, up_rows, down_rows)
    back_part, back_weight = (
        lax.all_to_all(
            partial_value.reshape(dev_count, half_cap, width),
            "ep",
            split_axis=0,
            concat_axis=0,
            tiled=True,
        ),
        lax.all_to_all(
            slot_weight.reshape(dev_count, half_cap), "ep", split_axis=0, concat_axis=0, tiled=True
        ),
    )
    slot_grads = (
        back_part.reshape(experts_win, groups, 2, half_cap, width)
        .sum(axis=1)
        .reshape(slot_total, width)
    )
    slot_weights = (
        back_weight.reshape(experts_win, groups, 2, half_cap).sum(axis=1).reshape(slot_total)
    )
    weighted = jnp.sum(match_three * route_weight[0][:, :, None], axis=1)
    mixed = jnp.dot(
        weighted, slot_grads, precision=lax.Precision.HIGHEST, preferred_element_type=jnp.float32
    )
    grad_out = (grad_in.astype(jnp.float32) + mixed).astype(jnp.bfloat16)
    weight_out = jnp.dot(
        match, slot_weights, precision=lax.Precision.HIGHEST, preferred_element_type=jnp.float32
    )
    weight_out = weight_out.reshape(token_count, TOP)
    sent_back = passed_along(grad_out[None], "pp", -1)
    return (sent_back, weight_out[None])


def near_call(kernel, out_shape, *args, **kwargs):
    if "in_specs" not in kwargs:
        args = [pltpu.with_memory_space_constraint(arg, pltpu.VMEM) for arg in args]
    params = pltpu.CompilerParams(vmem_limit_bytes=16 * 1024 * 1024)
    return pl.pallas_call(kernel, out_shape=out_shape, compiler_params=params, **kwargs)(*args)


def as_bf16(mask):
    return mask.astype(F32).astype(BF16)


def slot_of_token(routes_t):
    count = routes_t.shape[1]
    hit = routes_t == 0
    found = jnp.max(hit.astype(F32), axis=0, keepdims=True)
    found = jnp.broadcast_to(found, (MAIN, count))
    before = lax.broadcasted_iota(jnp.int32, (count, count), 0) < lax.broadcasted_iota(
        jnp.int32, (count, count), 1
    )
    rank = jnp.dot(found.astype(BF16), as_bf16(before), preferred_element_type=F32)
    slot = jnp.where((found > 0.5) & (rank < CAP - 0.5), rank, -1.0)
    return hit, slot


def main_pick(slot):
    row = lax.broadcasted_iota(jnp.int32, slot.shape, 0).astype(F32)
    return slot == row


def tail_pick(slot, fold):
    row = lax.broadcasted_iota(jnp.int32, slot.shape, 0)
    want = (row + (MAIN - TAIL * fold)).astype(F32)
    inside = (row >= TAIL * fold) & (row < TAIL * fold + TAIL)
    return (slot == want) & inside


def both_picks(slot, fold):
    picks = [main_pick(slot).astype(F32), tail_pick(slot, fold).astype(F32)]
    return jnp.concatenate(picks, axis=0).astype(BF16)


def three_parts(value):
    high = value.astype(BF16)
    rest = value - high.astype(F32)
    mid = rest.astype(BF16)
    low = (rest - mid.astype(F32)).astype(BF16)
    return [part.astype(F32) for part in (high, mid, low)]


def pick_into(slot, rows_ref, out_ref, before=lambda fold: None):
    width = rows_ref.shape[1]
    part = width // FOLDS
    tail = jnp.zeros((MAIN, part), F32)
    for fold in range(FOLDS):
        before(fold)
        span = slice(fold * part, (fold + 1) * part)
        got = jnp.dot(both_picks(slot, fold), rows_ref[:, span], preferred_element_type=F32)
        out_ref[:, span] = got[:MAIN].astype(BF16)
        tail = tail + got[MAIN:]
    out_ref[:, width:] = tail.astype(BF16)


def pick_inputs_kernel(
    routes_in, weight_in, rows_in, base_in, out_ref, slot_ref, weight_ref, base_ref, routes_ref, rows_ref, sems
):
    part = rows_ref.shape[1] // FOLDS
    routes_copy = pltpu.make_async_copy(routes_in, routes_ref, sems.at[2 * FOLDS])
    routes_copy.start()
    weight_copy = pltpu.make_async_copy(weight_in, weight_ref, sems.at[2 * FOLDS + 1])
    weight_copy.start()
    copies = []
    for fold in range(FOLDS):
        span = slice(fold * part, (fold + 1) * part)
        copies.append(
            pltpu.make_async_copy(rows_in.at[:, span], rows_ref.at[:, span], sems.at[fold])
        )
        copies[-1].start()
    base_copies = []
    for fold in range(FOLDS):
        span = slice(fold * part, (fold + 1) * part)
        base_copies.append(
            pltpu.make_async_copy(
                base_in.at[:, span], base_ref.at[:, span], sems.at[FOLDS + fold]
            )
        )
        base_copies[-1].start()
    routes_copy.wait()
    hit, slot = slot_of_token(routes_ref[...])
    slot_ref[...] = jnp.where(hit, slot, -1.0)
    pick_into(slot, rows_ref, out_ref, lambda fold: copies[fold].wait())
    weight_copy.wait()
    for copy in base_copies:
        copy.wait()


def pick_grads_kernel(routes_ref, rows_ref, weight_ref, out_ref, with_ref):
    full = out_ref.shape[1]
    _, slot = slot_of_token(routes_ref[...])
    pick_into(slot, rows_ref, out_ref)
    with_ref[:, :full] = out_ref[...]
    for k, piece in enumerate(three_parts(weight_ref[...])):
        with_ref[:, full + 128 * k : full + 128 * (k + 1)] = piece.astype(BF16)


TN = (((0,), (0,)), ((), ()))
NT = (((1,), (1,)), ((), ()))


def back_kernel(routes_ref, with_ref, back_ref, scale_ref):
    hit, slot = slot_of_token(routes_ref[...])
    size = 2 * MAIN
    eye = as_bf16(
        lax.broadcasted_iota(jnp.int32, (size, 2 * size), 0)
        == lax.broadcasted_iota(jnp.int32, (size, 2 * size), 1) % size
    )
    for fold in range(FOLDS):
        back_ref[fold] = lax.dot_general(
            both_picks(slot, fold), eye, TN, preferred_element_type=F32
        ).astype(BF16)
    weight = jnp.zeros(hit.shape, F32)
    for k in range(3, 0, -1):
        start = with_ref.shape[1] - 128 * k
        weight = weight + with_ref[:, start : start + 128].astype(F32)
    weight_row = jnp.sum(jnp.where(hit, weight, 0.0), axis=0, keepdims=True)
    main = jnp.sum(jnp.where(main_pick(slot), weight_row, 0.0), axis=1, keepdims=True)
    tail = jnp.zeros_like(main)
    for fold in range(FOLDS):
        tail = tail + jnp.sum(
            jnp.where(tail_pick(slot, fold), weight_row, 0.0), axis=1, keepdims=True
        )
    scale_ref[:, :128] = jnp.broadcast_to(main, (MAIN, 128))
    scale_ref[:, 128:] = jnp.broadcast_to(tail, (MAIN, 128))


def against(blocks, weights_ref, rows_ref):
    width = weights_ref.shape[1]
    part = width // FOLDS
    count = MAIN * len(blocks)
    for k, block in enumerate(blocks):
        rows_ref[MAIN * k : MAIN * (k + 1), :] = block[:, :width]
        rows_ref[count + MAIN * k : count + MAIN * (k + 1), :part] = block[:, width : width + part]
    tails = rows_ref[count:, :part]
    quarter = lax.broadcasted_iota(jnp.int32, (count, weights_ref.shape[0]), 0) % MAIN // TAIL
    main = tail = None
    for fold in range(FOLDS):
        span = slice(fold * part, (fold + 1) * part)
        rows = jnp.concatenate([rows_ref[:count, span], tails], axis=0)
        got = lax.dot_general(rows, weights_ref[:, span], NT, preferred_element_type=F32)
        here = jnp.where(quarter == fold, got[count:], 0.0)
        main = got[:count] if fold == 0 else main + got[:count]
        tail = here if fold == 0 else tail + here
    tail = tail.reshape(len(blocks), MAIN, -1)
    turn = TAIL
    while turn < MAIN:
        tail = tail + pltpu.roll(tail, turn, 1)
        turn *= 2
    return jnp.concatenate([main, tail.reshape(count, -1)], axis=0)


def early_kernel(own, z2, y_refs, gu_ref, h_ref, rows_ref):
    h_ref[...] = against([own, z2, y_refs.at[0], y_refs.at[1]], gu_ref, rows_ref)


def late_kernel(early_ref, low, high, gu_ref, h_ref, rows_ref):
    late = against([low.at[0], low.at[1], high.at[0], high.at[1]], gu_ref, rows_ref)
    for k in range(2 * FOLDS * 2):
        source = early_ref if k % 2 == 0 else late
        h_ref[MAIN * k : MAIN * (k + 1), :] = source[MAIN * (k // 2) : MAIN * (k // 2 + 1), :]


def spread(both, gu_ref, start, places):
    half = gu_ref.shape[1] // 2
    part = half // FOLDS
    count = MAIN * len(places)
    quarter = lax.broadcasted_iota(jnp.int32, (count, part), 0) % MAIN // TAIL
    tails = None
    for fold in range(FOLDS):
        span = slice(start + fold * part, start + (fold + 1) * part)
        value = jnp.dot(both, gu_ref[:, span], preferred_element_type=F32)
        here = jnp.where(quarter == fold, value[count:], 0.0)
        tails = here if fold == 0 else tails + here
        value = value[:count].astype(BF16)
        for k, (ref, j) in enumerate(places):
            ref[j, :, fold * part : (fold + 1) * part] = value[MAIN * k : MAIN * (k + 1), :]
    tails = tails.astype(BF16)
    for k, (ref, j) in enumerate(places):
        ref[j, :, half : half + part] = tails[MAIN * k : MAIN * (k + 1), :]


def grad_hidden_kernel(g0, g2, z_refs, y_refs, yz_refs, down_ref, grad_ref, rows_ref):
    blocks = [g0, z_refs.at[0], g2, z_refs.at[1]]
    blocks += [y_refs.at[0], yz_refs.at[0], y_refs.at[1], yz_refs.at[1]]
    grad_ref[...] = against(blocks, down_ref, rows_ref)


def backward_a_kernel(*refs):
    grad_ref, gu_ref, h_ref, near, far, both_ref = refs
    count = grad_ref.shape[0] // 2
    units = grad_ref.shape[1]
    grad_hidden = grad_ref[...]
    gate = h_ref[:, :units]
    up = h_ref[:, units:]
    sigmoid = 1.0 / (1.0 + jnp.exp(-gate))
    swish = gate * sigmoid
    grad_up = (grad_hidden * swish).astype(BF16)
    grad_gate = (grad_hidden * up * sigmoid * (1.0 + gate * (1.0 - sigmoid))).astype(BF16)
    both = jnp.concatenate([grad_gate, grad_up], axis=1)
    both_ref[...] = both
    places = [(ref, k) for ref in (near, far) for k in range(4)]
    spread(both, gu_ref, 0, places)
    weight = jnp.sum(grad_hidden * (swish * up), axis=1, keepdims=True)
    lane = lax.broadcasted_iota(jnp.int32, (count, 128), 1)
    first = lax.broadcasted_iota(jnp.int32, (count, 128), 0) % MAIN < TAIL
    tile = jnp.zeros((count, 128), F32)
    for k, piece in enumerate(three_parts(weight)):
        tile = jnp.where(lane == k, piece[:count], tile)
        tile = jnp.where((lane == k + 3) & first, piece[count:], tile)
    tile = tile.astype(BF16)
    full = near.shape[2] - 128
    for k, (ref, j) in enumerate(places):
        ref[j, :, full:] = tile[MAIN * k : MAIN * (k + 1), :]


def backward_b_kernel(both_ref, gu_ref, near, far):
    places = [((near, far)[k % 2], k // 2) for k in range(8)]
    spread(both_ref[...], gu_ref, gu_ref.shape[1] // 2, places)


def added(one, two):
    return (one.astype(F32) + two.astype(F32)).astype(BF16)


def fold_a_kernel(near_ref, got_ref, send_ref, keep_ref):
    full = near_ref.shape[2] - 128
    for k in range(near_ref.shape[0]):
        ref = (keep_ref, send_ref)[k % 2]
        ref[k // 2, :, :full] = added(near_ref[k, :, :full], got_ref[k, :, :full])
        ref[k // 2, :, full : full + 128] = near_ref[k, :, full:]
        ref[k // 2, :, full + 128 :] = got_ref[k, :, full:]


def fold_b_kernel(near_ref, got_ref, send_ref, keep_ref):
    for k in range(near_ref.shape[0]):
        ref = (keep_ref, send_ref)[k // 2]
        ref[k % 2] = added(near_ref[k], got_ref[k])


def fold_both_kernel(keep_a, got_a, keep_b, got_b, own_ref, send_ref, own_tile, send_tile):
    full = keep_b.shape[2]
    for k, (ref, tile_ref) in enumerate(((own_ref, own_tile), (send_ref, send_tile))):
        ref[:, :full] = added(keep_a[k, :, :full], got_a[k, :, :full])
        ref[:, full:] = added(keep_b[k], got_b[k])
        tile = jnp.zeros((MAIN, 128), F32)
        for source in (keep_a, got_a):
            for start in (full, full + 128):
                tile = tile + source[k, :, start : start + 128].astype(F32)
        tile_ref[...] = tile


def weight_kernel(slot_ref, own_tile, got_tile, after_ref, out_ref):
    tile = own_tile[...] + got_tile[...] + after_ref[...]
    lane = lax.broadcasted_iota(jnp.int32, tile.shape, 1)
    main = jnp.sum(jnp.where(lane < 3, tile, 0.0), axis=1, keepdims=True)
    tail = jnp.sum(jnp.where((lane >= 3) & (lane < 6), tile, 0.0), axis=1, keepdims=True)
    table = slot_ref[...]
    slot = jnp.broadcast_to(jnp.max(table, axis=0, keepdims=True), table.shape)
    row = lax.broadcasted_iota(jnp.int32, slot.shape, 0).astype(F32)
    value = jnp.sum(
        jnp.where(slot == row, main, 0.0) + jnp.where((slot == row + MAIN) & (row < TAIL), tail, 0.0),
        axis=0,
        keepdims=True,
    )
    out_ref[...] = jnp.where(table >= 0.0, value, 0.0)


def final_kernel(back_ref, scale_ref, one_ref, two_ref, base_ref, out_ref, end_ref, done_ref, sems):
    end_ref[...] = jnp.zeros_like(end_ref)
    width = base_ref.shape[1]
    half = width // 2
    part = half // FOLDS
    copies = []
    for side in range(2):
        first = side * (half + part)
        for fold in range(FOLDS):
            rows = []
            for lane, start in ((0, first + fold * part), (128, first + half)):
                total = one_ref[:, start : start + part].astype(F32)
                total = total + two_ref[:, start : start + part].astype(F32)
                rows.append(total * scale_ref[:, lane : lane + 1])
            rows = jnp.concatenate(rows, axis=0)
            high = rows.astype(BF16)
            low = (rows - high.astype(F32)).astype(BF16)
            rows = jnp.concatenate([high, low], axis=0)
            mixed = jnp.dot(back_ref[fold], rows, preferred_element_type=F32)
            start = side * half + fold * part
            span = slice(start, start + part)
            done_ref[:, span] = (base_ref[:, span].astype(F32) + mixed).astype(BF16)
            if fold % 2:
                span = slice(start - part, start + part)
                copy = pltpu.make_async_copy(
                    done_ref.at[:, span], out_ref.at[:, span], sems.at[len(copies)]
                )
                copy.start()
                copies.append(copy)
    for copy in copies:
        copy.wait()


def across(value, bits):
    count = lax.axis_size("ep")
    return lax.ppermute(value, "ep", [(i, i ^ bits) for i in range(count)])


def sections_across(value, bits):
    count = lax.axis_size("ep")
    pairs = [(s * count + i, (1 - s) * count + (i ^ bits)) for s in range(2) for i in range(count)]
    return lax.ppermute(value, ("pp", "ep"), pairs)


Y1, Z1, Z2 = 2, 4, 8


def single_device(upstream, saved, routes, route_weight, w_gate, w_up, w_down):
    routes_t = routes[0].T
    weight_t = route_weight[0].T
    next_routes = passed_along(routes_t, "pp", 1)
    count, width = saved.shape[1:]
    full = width + width // FOLDS
    half = full // 2
    units = 2 * w_gate.shape[1]
    slots = SHARDS // 2 * 2 * MAIN
    hbm = pl.BlockSpec(memory_space=pltpu.HBM)
    tile = pltpu.VMEM((MAIN, 128), F32)

    input_block, slot_table, near_weight, base = near_call(
        pick_inputs_kernel,
        [
            pltpu.VMEM((MAIN, full), BF16),
            pltpu.VMEM(routes_t.shape, F32),
            pltpu.VMEM(weight_t.shape, F32),
            pltpu.VMEM((count, width), BF16),
        ],
        *(
            pltpu.with_memory_space_constraint(v, pltpu.HBM)
            for v in (routes_t, weight_t, saved[0], upstream[0])
        ),
        in_specs=[hbm] * 4,
        scratch_shapes=[
            pltpu.VMEM(routes_t.shape, jnp.int32),
            pltpu.VMEM((count, width), BF16),
            pltpu.SemaphoreType.DMA((2 * FOLDS + 2,)),
        ],
        name="pick_inputs",
    )
    grad_block, grad_with = near_call(
        pick_grads_kernel,
        [pltpu.VMEM((MAIN, full), BF16), pltpu.VMEM((MAIN, full + 384), BF16)],
        next_routes,
        base,
        near_weight,
        name="pick_grads",
    )

    grad_z2 = sections_across(grad_block, Z2)
    grad_z0 = sections_across(grad_with, 0)
    input_z2 = across(input_block, Z2)
    own = jnp.stack([w_gate[0], w_up[0], w_down[0]])
    own, _ = lax.optimization_barrier((own, input_z2))
    other = across(own, 1)
    gate_up = jnp.concatenate([own[0], other[0], own[1], other[1]], axis=0)
    down = jnp.concatenate([own[2], other[2]], axis=0)

    grad_z = jnp.stack([grad_z0[:, :full], grad_z2])
    grad_z1 = across(grad_z, Z1)
    grad_y = across(grad_z, Y1)
    input_z = jnp.stack([input_block, input_z2])
    input_y = across(input_z, Y1)
    input_low = across(input_z, Z1)
    input_high = across(input_y, Z1)
    grad_z1, grad_y = lax.optimization_barrier((grad_z1, grad_y))
    grad_yz1 = across(grad_z1, Y1)

    late_routes, late_with, _ = lax.optimization_barrier((next_routes, grad_z0, grad_z1))
    back, scale = near_call(
        back_kernel,
        [pltpu.VMEM((FOLDS, count, 4 * MAIN), BF16), pltpu.VMEM((MAIN, 256), F32)],
        late_routes,
        late_with,
        name="back_rows",
    )
    input_high, back, scale = lax.optimization_barrier((input_high, back, scale))
    grad_hidden = near_call(
        grad_hidden_kernel,
        pltpu.VMEM((slots, units), F32),
        grad_z0,
        grad_z2,
        grad_z1,
        grad_y,
        grad_yz1,
        down,
        scratch_shapes=[pltpu.VMEM((slots, width), BF16)],
        name="grad_hidden",
    )
    early = near_call(
        early_kernel,
        pltpu.VMEM((slots // 2, 2 * units), F32),
        input_block,
        input_z2,
        input_y,
        gate_up,
        scratch_shapes=[pltpu.VMEM((slots // 2, width), BF16)],
        name="forward_early",
    )
    hidden = near_call(
        late_kernel,
        pltpu.VMEM((slots, 2 * units), F32),
        early,
        input_low,
        input_high,
        gate_up,
        scratch_shapes=[pltpu.VMEM((slots // 2, width), BF16)],
        name="forward_late",
    )
    side_a = pltpu.VMEM((4, MAIN, half + 128), BF16)
    side_b = pltpu.VMEM((4, MAIN, half), BF16)
    near_a, far_a, both = near_call(
        backward_a_kernel,
        [side_a, side_a, pltpu.VMEM((slots, 2 * units), BF16)],
        grad_hidden,
        gate_up,
        hidden,
        name="backward_a",
    )
    got_a = across(far_a, Y1)
    near_b, far_b = near_call(
        backward_b_kernel, [side_b, side_b], both, gate_up, name="backward_b"
    )
    got_b = across(far_b, Z1)
    send_a, keep_a = near_call(
        fold_a_kernel, [pltpu.VMEM((2, MAIN, half + 256), BF16)] * 2, near_a, got_a, name="fold_a"
    )
    send_b, keep_b = near_call(
        fold_b_kernel, [pltpu.VMEM((2, MAIN, half), BF16)] * 2, near_b, got_b, name="fold_b"
    )
    rows_0, rows_2, tile_0, tile_2 = near_call(
        fold_both_kernel,
        [pltpu.VMEM((MAIN, full), BF16)] * 2 + [tile] * 2,
        keep_a,
        across(send_a, Z1),
        keep_b,
        across(send_b, Y1),
        name="fold_both",
    )
    got_2 = sections_across(rows_2, Z2)
    got_0 = sections_across(rows_0, 0)
    grad_prev, end = near_call(
        final_kernel,
        [jax.ShapeDtypeStruct((count, width), BF16), tile],
        back,
        scale,
        got_2,
        got_0,
        base,
        out_specs=[hbm, pl.BlockSpec(memory_space=pltpu.VMEM)],
        scratch_shapes=[pltpu.VMEM((count, width), BF16), pltpu.SemaphoreType.DMA((FOLDS,))],
        name="final_rows",
    )
    weight_out = near_call(
        weight_kernel,
        jax.ShapeDtypeStruct((TOP, count), F32),
        slot_table,
        tile_0,
        across(tile_2, Z2),
        end,
        name="weight_out",
    )
    return (grad_prev[None], weight_out.T[None])


def solution(mesh):
    single = mesh.shape["ep"] == SHARDS and mesh.shape["pp"] == 2
    spec = P("pp", "ep", None)
    return jax.shard_map(
        single_device if single else general_device,
        mesh=mesh,
        in_specs=(spec,) * 7,
        out_specs=(spec, spec),
        check_vma=False,
    )
```

```python
import functools

import jax
import jax.numpy as jnp
from jax import lax
from jax.experimental import pallas as pl
from jax.experimental.pallas import tpu as pltpu
from jax.sharding import PartitionSpec as P

TOP = 8
SHARDS = 16
CAP = 10
MAIN = 8
TAIL = CAP - MAIN
FOLDS = MAIN // TAIL
F32 = jnp.float32
BF16 = jnp.bfloat16


def from_partner(block, axis, apart):
    count = lax.axis_size(axis)
    route = []
    for low in range(count):
        high = low | 1 << apart
        if high != low and high < count:
            route += [(low, high), (high, low)]
    return lax.ppermute(block, axis, route)


def passed_along(value, axis, by):
    size = lax.axis_size(axis)
    return lax.ppermute(value, axis, [(i, (i + by) % size) for i in range(size)])


def route_match(block_routes, experts_win):
    flat_routes = block_routes.reshape(-1)
    onehot = (flat_routes[:, None] == jnp.arange(experts_win, dtype=jnp.int32)[None, :]).astype(
        jnp.int32
    )
    earlier = jnp.cumsum(onehot, axis=0) - onehot
    ranking = jnp.sum(earlier * onehot, axis=1)
    kept = (flat_routes < experts_win) & (ranking < CAP)
    slot_index = flat_routes * CAP + ranking
    match = (slot_index[:, None] == jnp.arange(experts_win * CAP, dtype=jnp.int32)[None, :]) & kept[
        :, None
    ]
    return match.astype(jnp.float32)


def expert_grad(grad_rows, input_rows, gate_rows, up_rows, down_rows):
    contract = (((1,), (1,)), ((), ()))
    gate = lax.dot_general(input_rows, gate_rows, contract, preferred_element_type=jnp.float32)
    up_proj = lax.dot_general(input_rows, up_rows, contract, preferred_element_type=jnp.float32)
    grad_hidden = lax.dot_general(
        grad_rows, down_rows, contract, preferred_element_type=jnp.float32
    )
    sigmoid = jax.nn.sigmoid(gate)
    swish = gate * sigmoid
    hidden = swish * up_proj
    slot_weight = jnp.sum(grad_hidden * hidden, axis=1)
    grad_up = (grad_hidden * swish).astype(jnp.bfloat16)
    grad_gate = (grad_hidden * up_proj * sigmoid * (1.0 + gate * (1.0 - sigmoid))).astype(
        jnp.bfloat16
    )
    partial_value = jnp.dot(grad_gate, gate_rows, preferred_element_type=jnp.float32)
    partial_value = partial_value + jnp.dot(grad_up, up_rows, preferred_element_type=jnp.float32)
    return (partial_value, slot_weight)


def pair_rows(mine, other, pair_low):
    return jnp.where(
        pair_low, jnp.concatenate([mine, other], axis=0), jnp.concatenate([other, mine], axis=0)
    )


def general_device(upstream, saved, routes, route_weight, w_gate, w_up, w_down):
    shards = SHARDS
    groups = shards // 2
    experts_win = lax.axis_size("ep") // shards
    dev_count = experts_win * shards
    my_index = lax.axis_index("ep")
    half_cap = CAP // 2
    pair_low = my_index % 2 == 0
    other_gate, other_up, other_down = from_partner((w_gate[0], w_up[0], w_down[0]), "ep", 0)
    gate_rows = pair_rows(w_gate[0], other_gate, pair_low)
    up_rows = pair_rows(w_up[0], other_up, pair_low)
    down_rows = pair_rows(w_down[0], other_down, pair_low)
    grad_in = passed_along(upstream, "pp", -1)[0]
    inputs = saved[0]
    token_count, width = inputs.shape
    slot_total = experts_win * CAP
    match = route_match(routes[0], experts_win)
    match_three = match.reshape(token_count, TOP, slot_total)
    tok_match = match_three.sum(axis=1).astype(jnp.bfloat16)
    grad_slots = jnp.einsum(
        "ts,td->sd", tok_match, grad_in, preferred_element_type=jnp.float32
    ).astype(jnp.bfloat16)
    input_slots = jnp.einsum(
        "ts,td->sd", tok_match, inputs, preferred_element_type=jnp.float32
    ).astype(jnp.bfloat16)
    grad_halves = grad_slots.reshape(experts_win, 2, half_cap, width)
    input_halves = input_slots.reshape(experts_win, 2, half_cap, width)

    def copies_of(halves):
        return jnp.broadcast_to(halves[:, None], (experts_win, groups, 2, half_cap, width)).reshape(
            dev_count, half_cap, width
        )

    recv_grad, recv_input = (
        lax.all_to_all(copies_of(grad_halves), "ep", split_axis=0, concat_axis=0, tiled=True),
        lax.all_to_all(copies_of(input_halves), "ep", split_axis=0, concat_axis=0, tiled=True),
    )
    grad_rows = recv_grad.reshape(dev_count * half_cap, width)
    input_rows = recv_input.reshape(dev_count * half_cap, width)
    partial_value, slot_weight = expert_grad(grad_rows, input_rows, gate_rows, up_rows, down_rows)
    back_part, back_weight = (
        lax.all_to_all(
            partial_value.reshape(dev_count, half_cap, width),
            "ep",
            split_axis=0,
            concat_axis=0,
            tiled=True,
        ),
        lax.all_to_all(
            slot_weight.reshape(dev_count, half_cap), "ep", split_axis=0, concat_axis=0, tiled=True
        ),
    )
    slot_grads = (
        back_part.reshape(experts_win, groups, 2, half_cap, width)
        .sum(axis=1)
        .reshape(slot_total, width)
    )
    slot_weights = (
        back_weight.reshape(experts_win, groups, 2, half_cap).sum(axis=1).reshape(slot_total)
    )
    weighted = jnp.sum(match_three * route_weight[0][:, :, None], axis=1)
    mixed = jnp.dot(
        weighted, slot_grads, precision=lax.Precision.HIGHEST, preferred_element_type=jnp.float32
    )
    grad_out = (grad_in.astype(jnp.float32) + mixed).astype(jnp.bfloat16)
    weight_out = jnp.dot(
        match, slot_weights, precision=lax.Precision.HIGHEST, preferred_element_type=jnp.float32
    )
    weight_out = weight_out.reshape(token_count, TOP)
    sent_back = passed_along(grad_out[None], "pp", -1)
    return (sent_back, weight_out[None])


def near_call(kernel, out_shape, *args, **kwargs):
    if "in_specs" not in kwargs:
        args = [pltpu.with_memory_space_constraint(arg, pltpu.VMEM) for arg in args]
    params = pltpu.CompilerParams(vmem_limit_bytes=16 * 1024 * 1024)
    return pl.pallas_call(kernel, out_shape=out_shape, compiler_params=params, **kwargs)(*args)


def as_bf16(mask):
    return mask.astype(F32).astype(BF16)


def slot_of_token(routes_t):
    count = routes_t.shape[1]
    hit = routes_t == 0
    found = jnp.max(hit.astype(F32), axis=0, keepdims=True)
    found = jnp.broadcast_to(found, (MAIN, count))
    before = lax.broadcasted_iota(jnp.int32, (count, count), 0) < lax.broadcasted_iota(
        jnp.int32, (count, count), 1
    )
    rank = jnp.dot(found.astype(BF16), as_bf16(before), preferred_element_type=F32)
    slot = jnp.where((found > 0.5) & (rank < CAP - 0.5), rank, -1.0)
    return hit, slot


def main_pick(slot):
    row = lax.broadcasted_iota(jnp.int32, slot.shape, 0).astype(F32)
    return slot == row


def tail_pick(slot, fold):
    row = lax.broadcasted_iota(jnp.int32, slot.shape, 0)
    want = (row + (MAIN - TAIL * fold)).astype(F32)
    inside = (row >= TAIL * fold) & (row < TAIL * fold + TAIL)
    return (slot == want) & inside


def both_picks(slot, fold):
    picks = [main_pick(slot).astype(F32), tail_pick(slot, fold).astype(F32)]
    return jnp.concatenate(picks, axis=0).astype(BF16)


def three_parts(value):
    high = value.astype(BF16)
    rest = value - high.astype(F32)
    mid = rest.astype(BF16)
    low = (rest - mid.astype(F32)).astype(BF16)
    return [part.astype(F32) for part in (high, mid, low)]


def pick_into(slot, rows_ref, out_ref, before=lambda fold: None):
    width = rows_ref.shape[1]
    part = width // FOLDS
    tail = jnp.zeros((MAIN, part), F32)
    for fold in range(FOLDS):
        before(fold)
        span = slice(fold * part, (fold + 1) * part)
        got = jnp.dot(both_picks(slot, fold), rows_ref[:, span], preferred_element_type=F32)
        out_ref[:, span] = got[:MAIN].astype(BF16)
        tail = tail + got[MAIN:]
    out_ref[:, width:] = tail.astype(BF16)


def pick_inputs_kernel(
    routes_in, weight_in, rows_in, base_in, out_ref, slot_ref, weight_ref, base_ref, routes_ref, rows_ref, sems
):
    part = rows_ref.shape[1] // FOLDS
    routes_copy = pltpu.make_async_copy(routes_in, routes_ref, sems.at[2 * FOLDS])
    routes_copy.start()
    weight_copy = pltpu.make_async_copy(weight_in, weight_ref, sems.at[2 * FOLDS + 1])
    weight_copy.start()
    copies = []
    for fold in range(FOLDS):
        span = slice(fold * part, (fold + 1) * part)
        copies.append(
            pltpu.make_async_copy(rows_in.at[:, span], rows_ref.at[:, span], sems.at[fold])
        )
        copies[-1].start()
    base_copies = []
    for fold in range(FOLDS):
        span = slice(fold * part, (fold + 1) * part)
        base_copies.append(
            pltpu.make_async_copy(
                base_in.at[:, span], base_ref.at[:, span], sems.at[FOLDS + fold]
            )
        )
        base_copies[-1].start()
    routes_copy.wait()
    hit, slot = slot_of_token(routes_ref[...])
    slot_ref[...] = jnp.where(hit, slot, -1.0)
    pick_into(slot, rows_ref, out_ref, lambda fold: copies[fold].wait())
    weight_copy.wait()
    for copy in base_copies:
        copy.wait()


def pick_grads_kernel(routes_ref, rows_ref, weight_ref, out_ref, with_ref):
    full = out_ref.shape[1]
    _, slot = slot_of_token(routes_ref[...])
    pick_into(slot, rows_ref, out_ref)
    with_ref[:, :full] = out_ref[...]
    for k, piece in enumerate(three_parts(weight_ref[...])):
        with_ref[:, full + 128 * k : full + 128 * (k + 1)] = piece.astype(BF16)


TN = (((0,), (0,)), ((), ()))
NT = (((1,), (1,)), ((), ()))


def back_kernel(routes_ref, with_ref, back_ref, scale_ref):
    hit, slot = slot_of_token(routes_ref[...])
    size = 2 * MAIN
    eye = as_bf16(
        lax.broadcasted_iota(jnp.int32, (size, 2 * size), 0)
        == lax.broadcasted_iota(jnp.int32, (size, 2 * size), 1) % size
    )
    for fold in range(FOLDS):
        back_ref[fold] = lax.dot_general(
            both_picks(slot, fold), eye, TN, preferred_element_type=F32
        ).astype(BF16)
    weight = jnp.zeros(hit.shape, F32)
    for k in range(3, 0, -1):
        start = with_ref.shape[1] - 128 * k
        weight = weight + with_ref[:, start : start + 128].astype(F32)
    weight_row = jnp.sum(jnp.where(hit, weight, 0.0), axis=0, keepdims=True)
    main = jnp.sum(jnp.where(main_pick(slot), weight_row, 0.0), axis=1, keepdims=True)
    tail = jnp.zeros_like(main)
    for fold in range(FOLDS):
        tail = tail + jnp.sum(
            jnp.where(tail_pick(slot, fold), weight_row, 0.0), axis=1, keepdims=True
        )
    scale_ref[:, :128] = jnp.broadcast_to(main, (MAIN, 128))
    scale_ref[:, 128:] = jnp.broadcast_to(tail, (MAIN, 128))


def against(blocks, weights_ref, rows_ref):
    width = weights_ref.shape[1]
    part = width // FOLDS
    count = MAIN * len(blocks)
    for k, block in enumerate(blocks):
        rows_ref[MAIN * k : MAIN * (k + 1), :] = block[:, :width]
        rows_ref[count + MAIN * k : count + MAIN * (k + 1), :part] = block[:, width : width + part]
    tails = rows_ref[count:, :part]
    quarter = lax.broadcasted_iota(jnp.int32, (count, weights_ref.shape[0]), 0) % MAIN // TAIL
    main = tail = None
    for fold in range(FOLDS):
        span = slice(fold * part, (fold + 1) * part)
        rows = jnp.concatenate([rows_ref[:count, span], tails], axis=0)
        got = lax.dot_general(rows, weights_ref[:, span], NT, preferred_element_type=F32)
        here = jnp.where(quarter == fold, got[count:], 0.0)
        main = got[:count] if fold == 0 else main + got[:count]
        tail = here if fold == 0 else tail + here
    tail = tail.reshape(len(blocks), MAIN, -1)
    turn = TAIL
    while turn < MAIN:
        tail = tail + pltpu.roll(tail, turn, 1)
        turn *= 2
    return jnp.concatenate([main, tail.reshape(count, -1)], axis=0)


def early_kernel(own, z2, y_refs, gu_ref, h_ref, rows_ref):
    h_ref[...] = against([own, z2, y_refs.at[0], y_refs.at[1]], gu_ref, rows_ref)


def late_kernel(early_ref, low, high, gu_ref, h_ref, rows_ref):
    late = against([low.at[0], low.at[1], high.at[0], high.at[1]], gu_ref, rows_ref)
    for k in range(2 * FOLDS * 2):
        source = early_ref if k % 2 == 0 else late
        h_ref[MAIN * k : MAIN * (k + 1), :] = source[MAIN * (k // 2) : MAIN * (k // 2 + 1), :]


def spread(both, gu_ref, start, places):
    half = gu_ref.shape[1] // 2
    part = half // FOLDS
    count = MAIN * len(places)
    quarter = lax.broadcasted_iota(jnp.int32, (count, part), 0) % MAIN // TAIL
    tails = None
    for fold in range(FOLDS):
        span = slice(start + fold * part, start + (fold + 1) * part)
        value = jnp.dot(both, gu_ref[:, span], preferred_element_type=F32)
        here = jnp.where(quarter == fold, value[count:], 0.0)
        tails = here if fold == 0 else tails + here
        for k, (ref, j) in enumerate(places):
            rows = value[MAIN * k : MAIN * (k + 1), :].astype(ref.dtype)
            ref[j, :, fold * part : (fold + 1) * part] = rows
    for k, (ref, j) in enumerate(places):
        ref[j, :, half : half + part] = tails[MAIN * k : MAIN * (k + 1), :].astype(ref.dtype)


def grad_hidden_kernel(g0, g2, z_refs, y_refs, yz_refs, down_ref, grad_ref, rows_ref):
    blocks = [g0, z_refs.at[1], g2, z_refs.at[0]]
    blocks += [y_refs.at[1], yz_refs.at[1], y_refs.at[0], yz_refs.at[0]]
    grad_ref[...] = against(blocks, down_ref, rows_ref)


def backward_a_kernel(*refs):
    grad_ref, gu_ref, h_ref, near, far, both_ref = refs
    count = grad_ref.shape[0] // 2
    units = grad_ref.shape[1]
    grad_hidden = grad_ref[...]
    gate = h_ref[:, :units]
    up = h_ref[:, units:]
    sigmoid = 1.0 / (1.0 + jnp.exp(-gate))
    swish = gate * sigmoid
    grad_up = (grad_hidden * swish).astype(BF16)
    grad_gate = (grad_hidden * up * sigmoid * (1.0 + gate * (1.0 - sigmoid))).astype(BF16)
    both = jnp.concatenate([grad_gate, grad_up], axis=1)
    both_ref[...] = both
    places = [(ref, k) for ref in (near, far) for k in range(4)]
    spread(both, gu_ref, 0, places)
    weight = jnp.sum(grad_hidden * (swish * up), axis=1, keepdims=True)
    lane = lax.broadcasted_iota(jnp.int32, (count, 128), 1)
    first = lax.broadcasted_iota(jnp.int32, (count, 128), 0) % MAIN < TAIL
    tile = jnp.zeros((count, 128), F32)
    for k, piece in enumerate(three_parts(weight)):
        tile = jnp.where(lane == k, piece[:count], tile)
        tile = jnp.where((lane == k + 3) & first, piece[count:], tile)
    full = near.shape[2] - 128
    for k, (ref, j) in enumerate(places):
        ref[j, :, full:] = tile[MAIN * k : MAIN * (k + 1), :].astype(ref.dtype)


def backward_b_kernel(both_ref, gu_ref, near, far):
    places = [((near, far)[k % 2], k // 2) for k in range(8)]
    spread(both_ref[...], gu_ref, gu_ref.shape[1] // 2, places)


def added(one, two, dtype):
    return (one.astype(F32) + two.astype(F32)).astype(dtype)


def fold_a_kernel(near_ref, got_ref, send_ref, keep_ref):
    full = near_ref.shape[2] - 128
    for k in range(near_ref.shape[0]):
        ref = (keep_ref, send_ref)[k % 2]
        ref[k // 2, :, :full] = added(near_ref[k, :, :full], got_ref[k, :, :full], ref.dtype)
        ref[k // 2, :, full : full + 128] = near_ref[k, :, full:].astype(ref.dtype)
        ref[k // 2, :, full + 128 :] = got_ref[k, :, full:].astype(ref.dtype)


def fold_b_kernel(near_ref, got_ref, send_ref, keep_ref):
    for k in range(near_ref.shape[0]):
        ref = (keep_ref, send_ref)[k // 2]
        ref[k % 2] = added(near_ref[k], got_ref[k], ref.dtype)


def fold_both_kernel(keep_a, got_a, keep_b, got_b, own_ref, send_ref, own_tile, send_tile):
    full = keep_b.shape[2]
    for k, (ref, tile_ref) in enumerate(((own_ref, own_tile), (send_ref, send_tile))):
        ref[:, :full] = added(keep_a[k, :, :full], got_a[k, :, :full], BF16)
        ref[:, full:] = added(keep_b[k], got_b[k], BF16)
        tile = jnp.zeros((MAIN, 128), F32)
        for source in (keep_a, got_a):
            for start in (full, full + 128):
                tile = tile + source[k, :, start : start + 128].astype(F32)
        tile_ref[...] = tile


def weight_kernel(slot_ref, own_tile, got_tile, after_ref, out_ref):
    tile = own_tile[...] + got_tile[...] + after_ref[...]
    lane = lax.broadcasted_iota(jnp.int32, tile.shape, 1)
    main = jnp.sum(jnp.where(lane < 3, tile, 0.0), axis=1, keepdims=True)
    tail = jnp.sum(jnp.where((lane >= 3) & (lane < 6), tile, 0.0), axis=1, keepdims=True)
    table = slot_ref[...]
    slot = jnp.broadcast_to(jnp.max(table, axis=0, keepdims=True), table.shape)
    row = lax.broadcasted_iota(jnp.int32, slot.shape, 0).astype(F32)
    value = jnp.sum(
        jnp.where(slot == row, main, 0.0) + jnp.where((slot == row + MAIN) & (row < TAIL), tail, 0.0),
        axis=0,
        keepdims=True,
    )
    out_ref[...] = jnp.where(table >= 0.0, value, 0.0)


def final_kernel(back_ref, scale_ref, one_ref, two_ref, base_ref, out_ref, end_ref, done_ref, sems):
    end_ref[...] = jnp.zeros_like(end_ref)
    width = base_ref.shape[1]
    half = width // 2
    part = half // FOLDS
    copies = []
    for side in range(2):
        first = side * (half + part)
        for fold in range(FOLDS):
            rows = []
            for lane, start in ((0, first + fold * part), (128, first + half)):
                total = one_ref[:, start : start + part].astype(F32)
                total = total + two_ref[:, start : start + part].astype(F32)
                rows.append(total * scale_ref[:, lane : lane + 1])
            rows = jnp.concatenate(rows, axis=0)
            high = rows.astype(BF16)
            low = (rows - high.astype(F32)).astype(BF16)
            rows = jnp.concatenate([high, low], axis=0)
            mixed = jnp.dot(back_ref[fold], rows, preferred_element_type=F32)
            start = side * half + fold * part
            span = slice(start, start + part)
            done_ref[:, span] = (base_ref[:, span].astype(F32) + mixed).astype(BF16)
            if fold % 2:
                span = slice(start - part, start + part)
                copy = pltpu.make_async_copy(
                    done_ref.at[:, span], out_ref.at[:, span], sems.at[len(copies)]
                )
                copy.start()
                copies.append(copy)
    for copy in copies:
        copy.wait()


def across(value, bits):
    count = lax.axis_size("ep")
    return lax.ppermute(value, "ep", [(i, i ^ bits) for i in range(count)])


def sections_across(value, bits):
    count = lax.axis_size("ep")
    pairs = [(s * count + i, (1 - s) * count + (i ^ bits)) for s in range(2) for i in range(count)]
    return lax.ppermute(value, ("pp", "ep"), pairs)


Y1, Z1, Z2 = 2, 4, 8


def single_device(upstream, saved, routes, route_weight, w_gate, w_up, w_down):
    routes_t = routes[0].T
    weight_t = route_weight[0].T
    next_routes = passed_along(routes_t, "pp", 1)
    count, width = saved.shape[1:]
    full = width + width // FOLDS
    half = full // 2
    units = 2 * w_gate.shape[1]
    slots = SHARDS // 2 * 2 * MAIN
    hbm = pl.BlockSpec(memory_space=pltpu.HBM)
    tile = pltpu.VMEM((MAIN, 128), F32)

    input_block, slot_table, near_weight, base = near_call(
        pick_inputs_kernel,
        [
            pltpu.VMEM((MAIN, full), BF16),
            pltpu.VMEM(routes_t.shape, F32),
            pltpu.VMEM(weight_t.shape, F32),
            pltpu.VMEM((count, width), BF16),
        ],
        *(
            pltpu.with_memory_space_constraint(v, pltpu.HBM)
            for v in (routes_t, weight_t, saved[0], upstream[0])
        ),
        in_specs=[hbm] * 4,
        scratch_shapes=[
            pltpu.VMEM(routes_t.shape, jnp.int32),
            pltpu.VMEM((count, width), BF16),
            pltpu.SemaphoreType.DMA((2 * FOLDS + 2,)),
        ],
        name="pick_inputs",
    )
    grad_block, grad_with = near_call(
        pick_grads_kernel,
        [pltpu.VMEM((MAIN, full), BF16), pltpu.VMEM((MAIN, full + 384), BF16)],
        next_routes,
        base,
        near_weight,
        name="pick_grads",
    )

    grad_z2 = sections_across(grad_block, Z2)
    grad_z0 = sections_across(grad_with, 0)
    input_z2 = across(input_block, Z2)
    own = jnp.stack([w_gate[0], w_up[0], w_down[0]])
    own, _ = lax.optimization_barrier((own, input_z2))
    other = across(own, 1)
    gate_up = jnp.concatenate([own[0], other[0], own[1], other[1]], axis=0)
    down = jnp.concatenate([own[2], other[2]], axis=0)

    grad_z = jnp.stack([grad_z2, grad_z0[:, :full]])
    grad_z1 = across(grad_z, Z1)
    grad_y = across(grad_z, Y1)
    input_z = jnp.stack([input_block, input_z2])
    input_y = across(input_z, Y1)
    input_low = across(input_z, Z1)
    input_high = across(input_y, Z1)
    grad_z1, grad_y = lax.optimization_barrier((grad_z1, grad_y))
    grad_yz1 = across(grad_z1, Y1)

    late_routes, late_with, _ = lax.optimization_barrier((next_routes, grad_z0, grad_z1))
    back, scale = near_call(
        back_kernel,
        [pltpu.VMEM((FOLDS, count, 4 * MAIN), BF16), pltpu.VMEM((MAIN, 256), F32)],
        late_routes,
        late_with,
        name="back_rows",
    )
    input_high, back, scale = lax.optimization_barrier((input_high, back, scale))
    grad_hidden = near_call(
        grad_hidden_kernel,
        pltpu.VMEM((slots, units), F32),
        grad_z0,
        grad_z2,
        grad_z1,
        grad_y,
        grad_yz1,
        down,
        scratch_shapes=[pltpu.VMEM((slots, width), BF16)],
        name="grad_hidden",
    )
    early = near_call(
        early_kernel,
        pltpu.VMEM((slots // 2, 2 * units), F32),
        input_block,
        input_z2,
        input_y,
        gate_up,
        scratch_shapes=[pltpu.VMEM((slots // 2, width), BF16)],
        name="forward_early",
    )
    hidden = near_call(
        late_kernel,
        pltpu.VMEM((slots, 2 * units), F32),
        early,
        input_low,
        input_high,
        gate_up,
        scratch_shapes=[pltpu.VMEM((slots // 2, width), BF16)],
        name="forward_late",
    )
    side_a = (4, MAIN, half + 128)
    side_b = (4, MAIN, half)
    near_a, far_a, both = near_call(
        backward_a_kernel,
        [pltpu.VMEM(side_a, F32), pltpu.VMEM(side_a, BF16), pltpu.VMEM((slots, 2 * units), BF16)],
        grad_hidden,
        gate_up,
        hidden,
        name="backward_a",
    )
    got_a = across(far_a, Y1)
    near_b, far_b = near_call(
        backward_b_kernel, [pltpu.VMEM(side_b, F32), pltpu.VMEM(side_b, BF16)], both, gate_up, name="backward_b"
    )
    got_b = across(far_b, Z1)
    send_a, keep_a = near_call(
        fold_a_kernel, [pltpu.VMEM((2, MAIN, half + 256), t) for t in (BF16, F32)], near_a, got_a, name="fold_a"
    )
    send_b, keep_b = near_call(
        fold_b_kernel, [pltpu.VMEM((2, MAIN, half), t) for t in (BF16, F32)], near_b, got_b, name="fold_b"
    )
    rows_0, rows_2, tile_0, tile_2 = near_call(
        fold_both_kernel,
        [pltpu.VMEM((MAIN, full), BF16)] * 2 + [tile] * 2,
        keep_a,
        across(send_a, Z1),
        keep_b,
        across(send_b, Y1),
        name="fold_both",
    )
    got_2 = sections_across(rows_2, Z2)
    got_0 = sections_across(rows_0, 0)
    grad_prev, end = near_call(
        final_kernel,
        [jax.ShapeDtypeStruct((count, width), BF16), tile],
        back,
        scale,
        got_2,
        got_0,
        base,
        out_specs=[hbm, pl.BlockSpec(memory_space=pltpu.VMEM)],
        scratch_shapes=[pltpu.VMEM((count, width), BF16), pltpu.SemaphoreType.DMA((FOLDS,))],
        name="final_rows",
    )
    weight_out = near_call(
        weight_kernel,
        jax.ShapeDtypeStruct((TOP, count), F32),
        slot_table,
        tile_0,
        across(tile_2, Z2),
        end,
        name="weight_out",
    )
    return (grad_prev[None], weight_out.T[None])


def solution(mesh):
    single = mesh.shape["ep"] == SHARDS and mesh.shape["pp"] == 2
    spec = P("pp", "ep", None)
    return jax.shard_map(
        single_device if single else general_device,
        mesh=mesh,
        in_specs=(spec,) * 7,
        out_specs=(spec, spec),
        check_vma=False,
    )
```
